512 devices in a mesh: gx: 32 (over z, x_lo, core), gy: 16 (over y, x_hi).
Axes of the slice: x: 4 (x_hi: 2, x_lo: 2; x = x_hi * 2 + x_lo), y: 8, z: 8, core: 2. Of those that a mesh axis runs over, the one named last changes fastest.
Arguments:
- velocity: float32 [4, 2, 2048, 2048], P(None, None, 'gx', 'gy'), may hold values from -6 to 6
- marker_cell: int32 [3, 32, 16, 2048], P(None, 'gx', 'gy'), may hold values from 0 to 2047, as said below
- marker_frac: float32 [2, 32, 16, 2048], P(None, 'gx', 'gy'), may hold values from 0 to 1
- marker_force: float32 [2, 32, 16, 2048], P(None, 'gx', 'gy'), may hold values from -6 to 6
- fish_owner: int32 [768], replicated, may hold values from 0 to 511, as said below
Outputs:
- velocity_next: float32 [4, 2, 2048, 2048], P(None, None, 'gx', 'gy')
- marker_velocity: float32 [2, 32, 16, 2048], P(None, 'gx', 'gy')
The draws below stay inside these ranges and needn't reach their ends.
Inputs may be any that keep to these rules, and one draw needn't show every extreme that they name: `fish_owner`: device number i * 16 + j is the one at index i of gx and j of gy. No device holds more than 2 fish, and some device holds exactly 2. `marker_cell`: components are x cell, y cell and level. For the device at index i of gx and j of gy, every slot's x cell lies cyclically modulo 2048 from i * 64 - 15 to (i + 1) * 64 + 13 and its y cell from j * 128 - 15 to (j + 1) * 128 + 13; on every device both ends are reached. A device holding k fish has their markers in slots 0 to k * 1024 - 1; its other slots are unused.
All inputs are finite; a program needn't handle non-finite values.
Results may differ from the reference program's by a relative error of at most 0.0025.
Values may be sent and summed in bfloat16 or wider, within the bound.
A program may use at most 64 MiB of HBM per device.

```python
import jax
import jax.numpy as jnp
from jax import lax

CX = 64
CY = 128
LEV = 4
MARGIN = 16
FISH_MARK = 1024
FISH = 768
MARK_DEV = 2048
NX = 2048
NY = 2048
N_GX = 32
N_GY = 16


def draw_marker_cell(key, part):
    key_x, key_y, key_level = jax.random.split(key, 3)
    shape = (N_GX, N_GY, MARK_DEV)
    grid_row = lax.broadcasted_iota(jnp.int32, shape, 0)
    grid_col = lax.broadcasted_iota(jnp.int32, shape, 1)
    slot_index = lax.broadcasted_iota(jnp.int32, shape, 2)
    offset_x = jax.random.randint(key_x, shape, 1 - MARGIN, CX + MARGIN - 2)
    offset_x = jnp.where(slot_index == 0, 1 - MARGIN, jnp.where(slot_index == 1, CX + MARGIN - 3, offset_x))
    offset_y = jax.random.randint(key_y, shape, 1 - MARGIN, CY + MARGIN - 2)
    offset_y = jnp.where(slot_index == 1, 1 - MARGIN, jnp.where(slot_index == 0, CY + MARGIN - 3, offset_y))
    cell_x = jnp.mod(grid_row * CX + offset_x, NX)
    cell_y = jnp.mod(grid_col * CY + offset_y, NY)
    level = jax.random.randint(key_level, shape, 0, LEV)
    return jnp.stack([cell_x, cell_y, level], axis=0).astype(jnp.int32)


def draw_fish_owner(key, part):
    devices = N_GX * N_GY
    order = jax.random.permutation(key, devices)
    paired = max(FISH // 4, FISH - devices)
    fish_index = jnp.arange(FISH, dtype=jnp.int32)
    position = jnp.where(fish_index < 2 * paired, fish_index // 2, fish_index - paired)
    return order[position].astype(jnp.int32)


def level_of(rng, extent, shards, low, largest):
    gain, own = 1.0, jax.random.fold_in(rng, 6)
    for axis_at, parts in shards:
        steps = jnp.exp(jax.random.uniform(jax.random.fold_in(own, axis_at), (parts,), jnp.float32, low / len(shards), largest / len(shards)))
        gain = gain * jnp.repeat(steps, extent[axis_at] // parts).reshape([-1 if axis == axis_at else 1 for axis in range(len(extent))])
    return gain


def noise(key, dims, deviation, reach, cuts=(), held_as=jnp.bfloat16):
    factor_of = level_of(key, dims, cuts, -0.22, 0.18) if cuts else 1.0
    drawn = jax.random.normal(key, dims, jnp.float32) * deviation * factor_of
    return jnp.minimum(jnp.maximum(drawn, -reach), reach).astype(held_as)


def setup_inputs(seed: int = 0) -> dict:
    streams_of = jax.random.split(jax.random.key(seed), 6)
    return {
        "velocity": noise(streams_of[0], (LEV, 2, NX, NY), 1.0, 6.0, ((2, 32), (3, 16)), jnp.float32),
        "marker_cell": draw_marker_cell(jax.random.fold_in(streams_of[5], 71), 0),
        "marker_frac": jnp.clip(1.0 * jax.random.uniform(streams_of[2], (2, N_GX, N_GY, MARK_DEV), jnp.float32) ** level_of(streams_of[2], (2, N_GX, N_GY, MARK_DEV), ((1, 32), (2, 16)), -0.2, 0.2), 0.0, 1.0),
        "marker_force": noise(streams_of[3], (2, N_GX, N_GY, MARK_DEV), 1.0, 6.0, ((1, 32), (2, 16)), jnp.float32),
        "fish_owner": draw_fish_owner(jax.random.fold_in(streams_of[5], 71), 0),
    }


COURANT = 0.25
VISCOUS = 1.5


def kernel_weight(offset):
    return jnp.where(jnp.abs(offset) < 2.0, 0.25 * (1.0 + jnp.cos(0.5 * jnp.pi * offset)), 0.0)


def advect(padded):
    center = padded[:, :, 1:-1, 1:-1]
    speed_x = COURANT * center[:, 0:1]
    speed_y = COURANT * center[:, 1:2]
    back_x = center - padded[:, :, :-2, 1:-1]
    fore_x = padded[:, :, 2:, 1:-1] - center
    back_y = center - padded[:, :, 1:-1, :-2]
    fore_y = padded[:, :, 1:-1, 2:] - center
    change = jnp.maximum(speed_x, 0.0) * back_x + jnp.minimum(speed_x, 0.0) * fore_x
    change = change + jnp.maximum(speed_y, 0.0) * back_y + jnp.minimum(speed_y, 0.0) * fore_y
    return center - change


def smooth(source, padded):
    center = padded[:, :, 1:-1, 1:-1]
    above = jnp.concatenate([center[1:], center[-1:]], axis=0)
    below = jnp.concatenate([center[:1], center[:-1]], axis=0)
    summed = padded[:, :, 2:, 1:-1] + padded[:, :, :-2, 1:-1]
    summed = summed + padded[:, :, 1:-1, 2:] + padded[:, :, 1:-1, :-2]
    summed = summed + above + below
    return (source + VISCOUS * summed) / (1.0 + 6.0 * VISCOUS)


def wrap_pad(field):
    return jnp.pad(field, ((0, 0), (0, 0), (1, 1), (1, 1)), mode="wrap")


def reference(velocity, marker_cell, marker_frac, marker_force, fish_owner):
    levels, comps, extent_x, extent_y = velocity.shape
    devices = N_GX * N_GY
    slots = marker_cell.shape[3]
    owned = jnp.sum((fish_owner[:, None] == jnp.arange(devices, dtype=jnp.int32)[None, :]).astype(jnp.int32), axis=0)
    alive_count = (FISH_MARK * owned).reshape(N_GX, N_GY)
    alive_mask = (jnp.arange(slots, dtype=jnp.int32)[None, None, :] < alive_count[:, :, None]).astype(jnp.float32).reshape(-1)
    cell_x = marker_cell[0].reshape(-1)
    cell_y = marker_cell[1].reshape(-1)
    level = marker_cell[2].reshape(-1)
    frac_x = marker_frac[0].reshape(-1)
    frac_y = marker_frac[1].reshape(-1)
    force = marker_force.reshape(2, -1) * alive_mask[None, :]
    shifts = jnp.arange(-1, 3, dtype=jnp.int32)
    shift_float = shifts.astype(jnp.float32)
    weight_x = kernel_weight(shift_float[None, :] - frac_x[:, None])
    weight_y = kernel_weight(shift_float[None, :] - frac_y[:, None])
    weight_y = lax.optimization_barrier(weight_y.astype(jnp.bfloat16)).astype(jnp.float32)
    left = lax.optimization_barrier((force[:, :, None] * weight_x[None]).astype(jnp.bfloat16)).astype(jnp.float32)
    terms = left[:, :, :, None] * weight_y[None, :, None, :]
    index_x = jnp.mod(cell_x[:, None] + shifts[None, :], extent_x).astype(jnp.int32)
    index_y = jnp.mod(cell_y[:, None] + shifts[None, :], extent_y).astype(jnp.int32)
    component = jnp.arange(2, dtype=jnp.int32)
    forcing = jnp.zeros((levels, comps, extent_x, extent_y), jnp.float32)
    forcing = forcing.at[level[None, :, None, None], component[:, None, None, None], index_x[None, :, :, None], index_y[None, :, None, :]].add(terms)
    moved = velocity + forcing
    carried = advect(wrap_pad(moved))
    smoothed = carried
    for sweep_index in range(2):
        smoothed = smooth(carried, wrap_pad(smoothed))
    rounded = lax.optimization_barrier(smoothed.astype(jnp.bfloat16)).astype(jnp.float32)
    by_component = jnp.transpose(rounded, (1, 0, 2, 3))
    picked = by_component[:, level[:, None, None], index_x[:, :, None], index_y[:, None, :]]
    inner = jnp.sum(picked * weight_y[None, :, None, :], axis=3)
    sampled = jnp.sum(inner * weight_x[None], axis=2) * alive_mask[None, :]
    return smoothed, sampled.reshape(comps, N_GX, N_GY, slots)
```

```python
import functools
import math

import jax
import jax.numpy as jnp
from jax import lax
from jax.experimental import pallas as pl
from jax.experimental.pallas import tpu as pltpu
from jax.sharding import PartitionSpec as P

MARGIN = 16
FISH_MARK = 1024
COURANT = 0.25
VISCOUS = 1.5
LANES = 128
BF = jnp.bfloat16
F32 = jnp.float32

SIDES = [(1, 0), (-1, 0), (0, 1), (0, -1), (1, 1), (-1, 1), (1, -1), (-1, -1)]


def half_angle(t):
    z = t * (0.5 * math.pi)
    q = z * z
    s = 1.0 / math.factorial(13)
    for n in (11, 9, 7, 5, 3, 1):
        s = s * q + (-1.0) ** ((n - 1) // 2) / math.factorial(n)
    c = 1.0 / math.factorial(12)
    for n in (10, 8, 6, 4, 2, 0):
        c = c * q + (-1.0) ** (n // 2) / math.factorial(n)
    return s * z, c


def weights(t):
    s, c = half_angle(t)
    return (0.25 * (1.0 - s), 0.25 * (1.0 + c), 0.25 * (1.0 + s), 0.25 * (1.0 - c))


def chain(d, values, zero):
    out = jnp.where(d == 2.0, values[3], zero)
    out = jnp.where(d == 1.0, values[2], out)
    out = jnp.where(d == 0.0, values[1], out)
    return jnp.where(d == -1.0, values[0], out)


def kernel(
    nx, ny,
    vel, cell, frac, force, owner,
    out_v, out_m,
    q32, left, wx_hot, wy_hot, mv, pk16, pk3, rx, ry16, ry3, rc16, rc3,
    mt, ca, w1, stage, ta, tb, pks, rbs,
    send1, recv1, send2, recv2, out_sem,
):
    ix = lax.axis_index("gx")
    iy = lax.axis_index("gy")

    def at(dx, dy):
        return {"gx": lax.rem(ix + dx + nx, nx), "gy": lax.rem(iy + dy + ny, ny)}

    barrier = pltpu.get_barrier_semaphore()
    for dx, dy in SIDES:
        pl.semaphore_signal(
            barrier, inc=1, device_id=at(dx, dy), device_id_type=pl.DeviceIdType.MESH
        )

    mine = jnp.where(owner[...] == ix * ny + iy, 1.0, 0.0)
    count = jnp.sum(jnp.sum(mine, axis=1, keepdims=True), axis=0, keepdims=True)
    slot = lax.broadcasted_iota(jnp.int32, (16, LANES), 0) * LANES + lax.broadcasted_iota(
        jnp.int32, (16, LANES), 1
    )
    alive = jnp.where(slot.astype(F32) < FISH_MARK * count, 1.0, 0.0)
    rel_x = lax.rem(cell[0] - ix * 64 + (MARGIN + nx * 64), nx * 64)
    rel_y = lax.rem(cell[1] - iy * 128 + (MARGIN + ny * 128), ny * 128) - MARGIN
    q32[0] = rel_x.astype(F32)
    q32[1] = rel_y.astype(F32)
    wx = weights(frac[0])
    wy = weights(frac[1])
    for k in range(4):
        q32[2 + k] = wx[k]
        q32[6 + k] = wy[k]
        for c in range(2):
            q32[10 + 4 * c + k] = force[c] * alive * wx[k]
        q32[18 + k] = jnp.where(cell[2] == k, 1.0, 0.0)
    q32[22] = alive

    rows16 = lax.broadcasted_iota(jnp.int32, (16, LANES), 0).astype(F32)
    zero16 = jnp.zeros((16, LANES), BF)

    def operands(r, _):
        lanes = pl.ds(pl.multiple_of(r * LANES, LANES), LANES)

        def row(n):
            return jnp.broadcast_to(q32[n, pl.ds(r, 1), :], (16, LANES))

        dx0 = rows16 - row(0)
        lw = [[row(10 + 4 * c + k).astype(BF) for k in range(4)] for c in range(2)]
        for b in range(6):
            d = (dx0 + 16.0 * b).astype(BF)
            for c in range(2):
                left[pl.ds(96 * c + 16 * b, 16), lanes] = chain(d, lw[c], zero16)
        dy0 = rows16 - row(1)
        yw = [row(6 + k).astype(BF) for k in range(4)]
        lv = [row(18 + k).astype(BF) for k in range(4)]
        for b in range(10):
            base = 16.0 * b if b < 8 else (-16.0 if b == 8 else 128.0)
            d = (dy0 + base).astype(BF)
            w = chain(d, yw, zero16)
            for l in range(4):
                at_row = 128 * l + 16 * b if b < 8 else 512 + 64 * (b - 8) + 16 * l
                wy_hot[pl.ds(at_row, 16), lanes] = w * lv[l]
        return 0

    lax.fori_loop(0, 16, operands, 0)

    for c in range(2):
        spread = lax.dot_general(
            left[pl.ds(96 * c, 96), :], wy_hot[...], (((1,), (1,)), ((), ())),
            preferred_element_type=F32,
        )
        mv[c] = spread
        for l in range(4):
            ls = slice(128 * l, 128 * l + 128)
            mv[c, 16:80, ls] = spread[16:80, ls] + vel[l, c]

    lane = lax.broadcasted_iota(jnp.int32, (96, LANES), 1)
    low = lane < 64
    b0 = mv[0, :, 512:640]
    b1 = mv[1, :, 512:640]
    pk16[0] = jnp.where(low, pltpu.roll(b0, 64, 1), b1)
    pk16[1] = jnp.where(low, b0, pltpu.roll(b1, 64, 1))
    lane24 = lax.broadcasted_iota(jnp.int32, (24, LANES), 1) // 4
    for side in range(2):
        packed = jnp.zeros((24, LANES), F32)
        for q in range(4):
            for l in range(4):
                for c in range(2):
                    spot = q * 8 + l * 2 + c
                    src = mv[c, 24 * q : 24 * q + 24, 128 * l : 128 * l + 128]
                    shift = (spot * 4 - (124 if side == 0 else 0)) % LANES
                    moved = pltpu.roll(src, shift, 1) if shift else src
                    packed = jnp.where(lane24 == spot, moved, packed)
        pk3[side] = packed

    pl.semaphore_wait(barrier, 8)

    first = []

    def send(n, src, dst, dx, dy, ss, rs):
        copy = pltpu.make_async_remote_copy(
            src_ref=src, dst_ref=dst, send_sem=ss.at[n], recv_sem=rs.at[n],
            device_id=at(dx, dy), device_id_type=pl.DeviceIdType.MESH,
        )
        copy.start()
        return copy

    for n, (dx, dy) in enumerate(SIDES):
        if dy == 0:
            continue
        side = 0 if dy == 1 else 1
        if dx == 0:
            first.append(send(2 * n, pk16.at[side, pl.ds(8, 80)], ry16.at[side], dx, dy, send1, recv1))
            first.append(send(2 * n + 1, pk3.at[side], ry3.at[side], dx, dy, send1, recv1))
        else:
            start = 72 if dx == 1 else 0
            first.append(send(2 * n, pk16.at[side, pl.ds(start, 24)], rc16.at[n - 4], dx, dy, send1, recv1))
            first.append(send(2 * n + 1, pk3.at[side], rc3.at[n - 4], dx, dy, send1, recv1))
    first.append(send(0, mv.at[:, pl.ds(72, 24), :], rx.at[0], 1, 0, send1, recv1))
    first.append(send(2, mv.at[:, pl.ds(0, 24), :], rx.at[1], -1, 0, send1, recv1))

    rows8 = lax.broadcasted_iota(jnp.int32, (8, LANES), 0).astype(F32)

    def x_hot(r, _):
        lanes = pl.ds(pl.multiple_of(r * LANES, LANES), LANES)

        def row(n):
            return jnp.broadcast_to(q32[n, pl.ds(r, 1), :], (8, LANES))

        d = rows8 - row(0)
        ww = [row(2 + k) * row(22) for k in range(4)]
        for b in range(12):
            wx_hot[pl.ds(8 * b, 8), lanes] = chain(d + 8.0 * b, ww, 0.0)
        return 0

    lax.fori_loop(0, 16, x_hot, 0)

    for copy in first:
        copy.wait()

    lane80 = lax.broadcasted_iota(jnp.int32, (80, LANES), 1)
    pack16 = []
    for side in range(2):
        total = ry16[side]
        for n in range(4):
            dx, dy = SIDES[4 + n]
            if (0 if dy == 1 else 1) == side:
                piece = rc16[n]
                zeros = jnp.zeros((56, LANES), F32)
                parts = [piece, zeros] if dx == 1 else [zeros, piece]
                total = total + jnp.concatenate(parts, axis=0)
        pack16.append(total)
    zeros32 = jnp.zeros((32, LANES), F32)

    def with_x(c, ls):
        a = mv[c, 8:88, ls]
        return jnp.concatenate(
            [a[0:24] + rx[0, c, :, ls], a[24:56], a[56:80] + rx[1, c, :, ls]], axis=0
        )

    for c in range(2):
        side_b = with_x(c, slice(512, 640))
        for l in range(4):
            g16 = c * 64 + l * 16
            a = with_x(c, slice(128 * l, 128 * l + 128))
            from_low = pltpu.roll(pack16[0], (LANES - g16) % LANES, 1) if g16 else pack16[0]
            from_high = pltpu.roll(pack16[1], (112 - g16) % LANES, 1) if g16 != 112 else pack16[1]
            a = a + jnp.where(lane80 < 16, from_low, 0.0)
            a = a + jnp.where(lane80 >= 112, from_high, 0.0)
            mt[c, l, 8:88, 0:128] = a
            own_low = pltpu.roll(side_b, (112 - 16 * l) % LANES, 1)
            own_high = pltpu.roll(side_b, (LANES - 64 - 16 * l) % LANES, 1)
            h = jnp.where(lane80 >= 64, own_low, own_high)
            pieces = []
            for q in range(4):
                spot4 = (q * 8 + l * 2 + c) * 4
                lo = pltpu.roll(ry3[0], (124 - spot4) % LANES, 1) if spot4 != 124 else ry3[0]
                hi = pltpu.roll(ry3[1], (LANES - spot4) % LANES, 1) if spot4 else ry3[1]
                pieces.append(jnp.where(lane24 >= 16, lo, hi))
            h = h + jnp.concatenate(pieces, axis=0)[8:88]
            ends = []
            for dx, q in ((1, 3), (-1, 0)):
                spot4 = (q * 8 + l * 2 + c) * 4
                n_low = SIDES.index((dx, 1)) - 4
                n_high = SIDES.index((dx, -1)) - 4
                lo = pltpu.roll(rc3[n_low], (124 - spot4) % LANES, 1) if spot4 != 124 else rc3[n_low]
                hi = pltpu.roll(rc3[n_high], (LANES - spot4) % LANES, 1) if spot4 else rc3[n_high]
                ends.append(jnp.where(lane24 >= 16, lo, hi))
            h = h + jnp.concatenate([ends[0], zeros32, ends[1]], axis=0)
            mt[c, l, 8:88, 128:256] = h
            for ref in (mt, ca, w1):
                ref[c, l, 0:8, :] = jnp.zeros((8, 256), F32)
                ref[c, l, 88:96, :] = jnp.zeros((8, 256), F32)

    def shifted(q, by):
        return pltpu.roll(q, by % 256, 1)

    for l in range(4):
        a = COURANT * mt[0, l, 8:88, :]
        b = COURANT * mt[1, l, 8:88, :]
        ap, am = jnp.maximum(a, 0.0), jnp.minimum(a, 0.0)
        bp, bm = jnp.maximum(b, 0.0), jnp.minimum(b, 0.0)
        for c in range(2):
            q = mt[c, l, 8:88, :]
            change = ap * (q - mt[c, l, 7:87, :]) + am * (mt[c, l, 9:89, :] - q)
            change = change + bp * (q - shifted(q, 1)) + bm * (shifted(q, -1) - q)
            ca[c, l, 8:88, :] = q - change

    for c in range(2):
        for l in range(4):
            q = ca[c, l, 8:88, :]
            total = ca[c, l, 7:87, :] + ca[c, l, 9:89, :]
            total = total + shifted(q, 1) + shifted(q, -1)
            total = total + ca[c, min(l + 1, 3), 8:88, :] + ca[c, max(l - 1, 0), 8:88, :]
            w1[c, l, 8:88, :] = (q + VISCOUS * total) * (1.0 / (1.0 + 6.0 * VISCOUS))
    for c in range(2):
        for l in range(4):
            q = w1[c, l, 16:80, :]
            total = w1[c, l, 15:79, 0:128] + w1[c, l, 17:81, 0:128]
            total = total + shifted(q, 1)[:, 0:128] + shifted(q, -1)[:, 0:128]
            total = total + w1[c, min(l + 1, 3), 16:80, 0:128] + w1[c, max(l - 1, 0), 16:80, 0:128]
            w2 = (ca[c, l, 16:80, 0:128] + VISCOUS * total) * (1.0 / (1.0 + 6.0 * VISCOUS))
            stage[l, c] = w2
            ta[c, 16:80, 128 * l : 128 * l + 128] = w2.astype(BF)

    out_copy = pltpu.make_async_copy(stage, out_v, out_sem)
    out_copy.start()

    lane64 = lax.broadcasted_iota(jnp.int32, (64, LANES), 1) // 16
    for side in range(2):
        packed = jnp.zeros((64, LANES), F32)
        for c in range(2):
            for l in range(4):
                spot = c * 4 + l
                shift = (spot * 16 - (112 if side == 0 else 0)) % LANES
                src = stage[l, c]
                moved = pltpu.roll(src, shift, 1) if shift else src
                packed = jnp.where(lane64 == spot, moved, packed)
        pks[side] = packed.astype(BF)
    second = []
    for n, (dx, dy) in enumerate(SIDES):
        if dy == 0:
            src, dst = (64, 0) if dx == 1 else (16, 80)
            second.append(
                send(n, ta.at[:, pl.ds(src, 16), :], ta.at[:, pl.ds(dst, 16), :], dx, dy, send2, recv2)
            )
            continue
        side = 0 if dy == 1 else 1
        if dx == 0:
            src, dst, size = 0, 16, 64
        elif dx == 1:
            src, dst, size = 48, 0, 16
        else:
            src, dst, size = 0, 80, 16
        second.append(
            send(n, pks.at[side, pl.ds(src, size)], rbs.at[side, pl.ds(dst, size)], dx, dy, send2, recv2)
        )
    for copy in second:
        copy.wait()

    below = rbs[0].astype(F32)
    above = rbs[1].astype(F32)
    tb[0] = jnp.where(low, below, pltpu.roll(above, 64, 1)).astype(BF)
    tb[1] = jnp.where(low, pltpu.roll(below, 64, 1), above).astype(BF)

    for r in range(4):
        lanes = slice(512 * r, 512 * r + 512)
        for c in range(2):
            part = jnp.dot(ta[c], wy_hot[0:512, lanes], preferred_element_type=F32)
            part = part + jnp.dot(tb[c], wy_hot[512:640, lanes], preferred_element_type=F32)
            summed = jnp.sum(part * wx_hot[:, lanes], axis=0, keepdims=True)
            for j in range(4):
                out_m[c, 4 * r + j : 4 * r + j + 1, :] = summed[:, LANES * j : LANES * j + LANES]
    out_copy.wait()


def body(velocity, marker_cell, marker_frac, marker_force, fish_owner):
    nx = lax.axis_size("gx")
    ny = lax.axis_size("gy")
    vm = pl.BlockSpec(memory_space=pltpu.VMEM)
    out_v, out_m = pl.pallas_call(
        functools.partial(kernel, nx, ny),
        out_shape=(
            jax.ShapeDtypeStruct((4, 2, 64, 128), F32),
            jax.ShapeDtypeStruct((2, 16, 128), F32),
        ),
        in_specs=[vm] * 5,
        out_specs=(pl.BlockSpec(memory_space=pl.ANY), vm),
        scratch_shapes=[
            pltpu.VMEM((23, 16, 128), F32),
            pltpu.VMEM((192, 2048), BF),
            pltpu.VMEM((96, 2048), F32),
            pltpu.VMEM((640, 2048), BF),
            pltpu.VMEM((2, 96, 640), F32),
            pltpu.VMEM((2, 96, 128), F32),
            pltpu.VMEM((2, 24, 128), F32),
            pltpu.VMEM((2, 2, 24, 640), F32),
            pltpu.VMEM((2, 80, 128), F32),
            pltpu.VMEM((2, 24, 128), F32),
            pltpu.VMEM((4, 24, 128), F32),
            pltpu.VMEM((4, 24, 128), F32),
            pltpu.VMEM((2, 4, 96, 256), F32),
            pltpu.VMEM((2, 4, 96, 256), F32),
            pltpu.VMEM((2, 4, 96, 256), F32),
            pltpu.VMEM((4, 2, 64, 128), F32),
            pltpu.VMEM((2, 96, 512), BF),
            pltpu.VMEM((2, 96, 128), BF),
            pltpu.VMEM((2, 64, 128), BF),
            pltpu.VMEM((2, 96, 128), BF),
            pltpu.SemaphoreType.DMA((16,)),
            pltpu.SemaphoreType.DMA((16,)),
            pltpu.SemaphoreType.DMA((8,)),
            pltpu.SemaphoreType.DMA((8,)),
            pltpu.SemaphoreType.DMA,
        ],
        compiler_params=pltpu.CompilerParams(
            collective_id=0, has_side_effects=True, vmem_limit_bytes=48 * 1024 * 1024
        ),
        name="fish_step",
    )(
        velocity,
        marker_cell.reshape(3, 16, 128),
        marker_frac.reshape(2, 16, 128),
        marker_force.reshape(2, 16, 128),
        fish_owner.reshape(6, 128),
    )
    return out_v, out_m.reshape(2, 1, 1, 2048)


def solution(mesh):
    placed = (
        P(None, None, "gx", "gy"),
        P(None, "gx", "gy", None),
        P(None, "gx", "gy", None),
        P(None, "gx", "gy", None),
        P(),
    )
    return jax.shard_map(
        body,
        mesh=mesh,
        in_specs=placed,
        out_specs=(P(None, None, "gx", "gy"), P(None, "gx", "gy", None)),
        check_vma=False,
    )
```

```python
import functools
import math

import jax
import jax.numpy as jnp
from jax import lax
from jax.experimental import pallas as pl
from jax.experimental.pallas import tpu as pltpu
from jax.sharding import PartitionSpec as P

MARGIN = 16
FISH_MARK = 1024
COURANT = 0.25
VISCOUS = 1.5
LANES = 128
BF = jnp.bfloat16
F32 = jnp.float32

SIDES = [(1, 0), (-1, 0), (0, 1), (0, -1), (1, 1), (-1, 1), (1, -1), (-1, -1)]


def half_angle(t):
    z = t * (0.5 * math.pi)
    q = z * z
    s = 1.0 / math.factorial(13)
    for n in (11, 9, 7, 5, 3, 1):
        s = s * q + (-1.0) ** ((n - 1) // 2) / math.factorial(n)
    c = 1.0 / math.factorial(12)
    for n in (10, 8, 6, 4, 2, 0):
        c = c * q + (-1.0) ** (n // 2) / math.factorial(n)
    return s * z, c


def weights(t):
    s, c = half_angle(t)
    return (0.25 * (1.0 - s), 0.25 * (1.0 + c), 0.25 * (1.0 + s), 0.25 * (1.0 - c))


def chain(d, values, zero):
    out = jnp.where(d == 2.0, values[3], zero)
    out = jnp.where(d == 1.0, values[2], out)
    out = jnp.where(d == 0.0, values[1], out)
    return jnp.where(d == -1.0, values[0], out)


def kernel(
    nx, ny,
    vel_h, cell_h, frac_h, force_h, owner_h,
    out_v, out_m,
    vel, cell, frac, force, owner,
    q32, left, wx_hot, wy_hot, mv, pk16, pko, rx, ry16, ryo, rc16, rco,
    mt, ca, w1, ta,
    in_sem, send1, recv1,
):
    ix = lax.axis_index("gx")
    iy = lax.axis_index("gy")

    def at(dx, dy):
        return {"gx": lax.rem(ix + dx + nx, nx), "gy": lax.rem(iy + dy + ny, ny)}

    barrier = pltpu.get_barrier_semaphore()
    for dx, dy in SIDES:
        pl.semaphore_signal(
            barrier, inc=1, device_id=at(dx, dy), device_id_type=pl.DeviceIdType.MESH
        )
    loads = []
    for n, (src, dst) in enumerate(
        ((cell_h, cell), (frac_h, frac), (force_h, force), (owner_h, owner), (vel_h, vel))
    ):
        loads.append(pltpu.make_async_copy(src, dst, in_sem.at[n]))
        loads[-1].start()
    for load in loads[:4]:
        load.wait()

    mine = jnp.where(owner[...] == ix * ny + iy, 1.0, 0.0)
    count = jnp.sum(jnp.sum(mine, axis=1, keepdims=True), axis=0, keepdims=True)
    slot = lax.broadcasted_iota(jnp.int32, (16, LANES), 0) * LANES + lax.broadcasted_iota(
        jnp.int32, (16, LANES), 1
    )
    alive = jnp.where(slot.astype(F32) < FISH_MARK * count, 1.0, 0.0)
    rel_x = lax.rem(cell[0] - ix * 64 + (MARGIN + nx * 64), nx * 64)
    rel_y = lax.rem(cell[1] - iy * 128 + (MARGIN + ny * 128), ny * 128) - MARGIN
    q32[0] = rel_x.astype(F32)
    q32[1] = rel_y.astype(F32)
    wx = weights(frac[0])
    wy = weights(frac[1])
    for k in range(4):
        q32[2 + k] = wx[k]
        q32[6 + k] = wy[k]
        for c in range(2):
            q32[10 + 4 * c + k] = force[c] * alive * wx[k]
        q32[18 + k] = jnp.where(cell[2] == k, 1.0, 0.0)
    q32[22] = alive

    rows16 = lax.broadcasted_iota(jnp.int32, (16, LANES), 0).astype(F32)
    zero16 = jnp.zeros((16, LANES), BF)
    strips = ((512, -26.0), (528, -10.0), (640, 122.0), (656, 138.0))

    def operands(r, _):
        lanes = pl.ds(pl.multiple_of(r * LANES, LANES), LANES)

        def row(n):
            return jnp.broadcast_to(q32[n, pl.ds(r, 1), :], (16, LANES))

        dx0 = rows16 - row(0)
        lw = [[row(10 + 4 * c + k).astype(BF) for k in range(4)] for c in range(2)]
        for b in range(6):
            d = (dx0 + 16.0 * b).astype(BF)
            for c in range(2):
                left[pl.ds(96 * c + 16 * b, 16), lanes] = chain(d, lw[c], zero16)
        dy0 = rows16 - row(1)
        yw = [row(6 + k).astype(BF) for k in range(4)]
        lv = [row(18 + k).astype(BF) for k in range(4)]
        for b in range(12):
            base, step = (16.0 * b, 128) if b < 8 else (strips[b - 8][1], 32)
            first_row = 16 * b if b < 8 else strips[b - 8][0]
            d = (dy0 + base).astype(BF)
            w = chain(d, yw, zero16)
            for l in range(4):
                wy_hot[pl.ds(first_row + step * l, 16), lanes] = w * lv[l]
        return 0

    lax.fori_loop(0, 16, operands, 0)

    loads[4].wait()
    lane64 = lax.broadcasted_iota(jnp.int32, (64, LANES), 1)
    level64, j64 = lane64 // 32, lane64 % 32
    for c in range(2):
        spread = lax.dot_general(
            left[pl.ds(96 * c, 96), :], wy_hot[...], (((1,), (1,)), ((), ())),
            preferred_element_type=F32,
        )
        mv[c] = spread
        low_part = jnp.zeros((64, LANES), F32)
        high_part = jnp.zeros((64, LANES), F32)
        for l in range(4):
            ls = slice(128 * l, 128 * l + 128)
            v = vel[l, c]
            mv[c, 16:80, ls] = spread[16:80, ls] + v
            low_part = jnp.where(
                (level64 == l) & (j64 >= 26), pltpu.roll(v, 32 * l + 26, 1), low_part
            )
            high_part = jnp.where(
                (level64 == l) & (j64 < 6), pltpu.roll(v, 32 * l + 6, 1), high_part
            )
        mv[c, 16:80, 512:640] = spread[16:80, 512:640] + low_part
        mv[c, 16:80, 640:768] = spread[16:80, 640:768] + high_part

    lane = lax.broadcasted_iota(jnp.int32, (96, LANES), 1)
    level, j = lane // 32, lane % 32
    strip0 = [mv[c, :, 512:640] for c in range(2)]
    strip1 = [mv[c, :, 640:768] for c in range(2)]
    near = j < 16
    pk16[0] = jnp.where(near, pltpu.roll(strip1[0], 122, 1), pltpu.roll(strip1[1], 10, 1)).astype(BF)
    pk16[1] = jnp.where(near, pltpu.roll(strip0[0], 118, 1), pltpu.roll(strip0[1], 6, 1)).astype(BF)
    for c in range(2):
        up = pltpu.roll(strip1[c], 20, 1)
        down = pltpu.roll(strip0[c], 108, 1)
        for l in range(4):
            t = mv[c, :, 128 * l : 128 * l + 128]
            up = jnp.where((level == l) & (j < 26), pltpu.roll(t, (32 * l + 26) % LANES, 1), up)
            down = jnp.where((level == l) & (j >= 6), pltpu.roll(t, 32 * l + 6, 1), down)
        pko[0, c] = up
        pko[1, c] = down

    pl.semaphore_wait(barrier, 8)

    copies = []

    def send(n, src, dst, dx, dy):
        copy = pltpu.make_async_remote_copy(
            src_ref=src, dst_ref=dst, send_sem=send1.at[n], recv_sem=recv1.at[n],
            device_id=at(dx, dy), device_id_type=pl.DeviceIdType.MESH,
        )
        copy.start()
        copies.append(copy)

    for n, (dx, dy) in enumerate(SIDES):
        if dy == 0:
            continue
        side = 0 if dy == 1 else 1
        if dx == 0:
            send(2 * n, pko.at[side], ryo.at[side], dx, dy)
            send(2 * n + 1, pk16.at[side], ry16.at[side], dx, dy)
        else:
            send(2 * n, pko.at[side, :, pl.ds(56 if dx == 1 else 0, 40)], rco.at[n - 4], dx, dy)
            send(2 * n + 1, pk16.at[side, pl.ds(48 if dx == 1 else 0, 48)], rc16.at[n - 4], dx, dy)
    send(0, mv.at[:, pl.ds(56, 40), :], rx.at[0], 1, 0)
    send(2, mv.at[:, pl.ds(0, 40), :], rx.at[1], -1, 0)

    rows8 = lax.broadcasted_iota(jnp.int32, (8, LANES), 0).astype(F32)

    def x_hot(r, _):
        lanes = pl.ds(pl.multiple_of(r * LANES, LANES), LANES)

        def row(n):
            return jnp.broadcast_to(q32[n, pl.ds(r, 1), :], (8, LANES))

        d = rows8 - row(0)
        ww = [row(2 + k) * row(22) for k in range(4)]
        for b in range(12):
            wx_hot[pl.ds(8 * b, 8), lanes] = chain(d + 8.0 * b, ww, 0.0)
        return 0

    lax.fori_loop(0, 16, x_hot, 0)
    for ref in (mt, ca, w1):
        for c in range(2):
            for t in range(6):
                ref[c, t, 0:8, :] = jnp.zeros((8, LANES), F32)
                ref[c, t, 120:128, :] = jnp.zeros((8, LANES), F32)

    for copy in copies:
        copy.wait()

    corner = {}
    for n in range(4):
        dx, dy = SIDES[4 + n]
        corner[0 if dx == 1 else 1, 0 if dy == 1 else 1] = n

    def joined(mid, first, last):
        return [
            first[0:8], mid[0:32] + first[8:40], mid[32:64], mid[64:96] + last[0:32], last[32:40]
        ]

    pack16 = [
        jnp.concatenate(
            joined(
                ry16[side].astype(F32),
                rc16[corner[0, side]].astype(F32)[8:48],
                rc16[corner[1, side]].astype(F32)[0:40],
            ),
            axis=0,
        )
        for side in range(2)
    ]
    lane112 = lax.broadcasted_iota(jnp.int32, (112, LANES), 1)

    def rolled(q, by):
        return pltpu.roll(q, by % LANES, 1) if by % LANES else q

    for c in range(2):
        for t in range(6):
            ls = slice(128 * t, 128 * t + 128)
            mid, first, last = mv[c, :, ls], rx[0, c, :, ls], rx[1, c, :, ls]
            if t < 4:
                a = jnp.concatenate(joined(mid, first, last), axis=0)
                g = 32 * t + 16 * c
                a = a + jnp.where(lane112 < 16, rolled(pack16[0], -g), 0.0)
                a = a + jnp.where(lane112 >= 112, rolled(pack16[1], 112 - g), 0.0)
            else:
                side = t - 4
                mid = mid + ryo[side, c]
                first = first + rco[corner[0, side], c]
                last = last + rco[corner[1, side], c]
                a = jnp.concatenate(joined(mid, first, last), axis=0)
            mt[c, t, 8:120, :] = a

    for t in range(6):
        a = COURANT * mt[0, t, 8:120, :]
        b = COURANT * mt[1, t, 8:120, :]
        ap, am = jnp.maximum(a, 0.0), jnp.minimum(a, 0.0)
        bp, bm = jnp.maximum(b, 0.0), jnp.minimum(b, 0.0)
        for c in range(2):
            q = mt[c, t, 8:120, :]
            change = ap * (q - mt[c, t, 7:119, :]) + am * (mt[c, t, 9:121, :] - q)
            change = change + bp * (q - rolled(q, 1)) + bm * (rolled(q, -1) - q)
            ca[c, t, 8:120, :] = q - change

    def around(ref, c, t, lo, hi):
        q = ref[c, t, lo:hi, :]
        total = ref[c, t, lo - 1 : hi - 1, :] + ref[c, t, lo + 1 : hi + 1, :]
        total = total + rolled(q, 1) + rolled(q, -1)
        if t < 4:
            return total + ref[c, min(t + 1, 3), lo:hi, :] + ref[c, max(t - 1, 0), lo:hi, :]
        lanes = lax.broadcasted_iota(jnp.int32, (hi - lo, LANES), 1)
        total = total + jnp.where(lanes >= 96, q, rolled(q, -32))
        return total + jnp.where(lanes < 32, q, rolled(q, 32))

    scale = 1.0 / (1.0 + 6.0 * VISCOUS)
    for c in range(2):
        for t in range(6):
            w1[c, t, 8:120, :] = (ca[c, t, 8:120, :] + VISCOUS * around(ca, c, t, 8, 120)) * scale
    for c in range(2):
        done = [
            (ca[c, t, 16:112, :] + VISCOUS * around(w1, c, t, 16, 112)) * scale for t in (4, 5)
        ]
        for l in range(4):
            w2 = (ca[c, l, 16:112, :] + VISCOUS * around(w1, c, l, 16, 112)) * scale
            w2 = jnp.where(lane < 3, rolled(done[0], -(32 * l + 26)), w2)
            w2 = jnp.where(lane >= 125, rolled(done[1], 122 - 32 * l), w2)
            out_v[l, c] = w2[16:80]
            ta[c, :, 128 * l : 128 * l + 128] = w2.astype(BF)
        ta[c, :, 512:640] = jnp.where((j >= 10) & (j < 26), done[0], 0.0).astype(BF)
        ta[c, :, 640:768] = jnp.where((j >= 6) & (j < 22), done[1], 0.0).astype(BF)

    for r in range(4):
        lanes = slice(512 * r, 512 * r + 512)
        for c in range(2):
            part = jnp.dot(ta[c], wy_hot[:, lanes], preferred_element_type=F32)
            summed = jnp.sum(part * wx_hot[:, lanes], axis=0, keepdims=True)
            for i in range(4):
                out_m[c, 4 * r + i : 4 * r + i + 1, :] = summed[:, LANES * i : LANES * i + LANES]


def body(velocity, marker_cell, marker_frac, marker_force, fish_owner):
    nx = lax.axis_size("gx")
    ny = lax.axis_size("gy")
    vm = pl.BlockSpec(memory_space=pltpu.VMEM)
    out_v, out_m = pl.pallas_call(
        functools.partial(kernel, nx, ny),
        out_shape=(
            jax.ShapeDtypeStruct((4, 2, 64, 128), F32),
            jax.ShapeDtypeStruct((2, 16, 128), F32),
        ),
        in_specs=[pl.BlockSpec(memory_space=pltpu.HBM)] * 5,
        out_specs=(vm, vm),
        scratch_shapes=[
            pltpu.VMEM((4, 2, 64, 128), F32),
            pltpu.VMEM((3, 16, 128), jnp.int32),
            pltpu.VMEM((2, 16, 128), F32),
            pltpu.VMEM((2, 16, 128), F32),
            pltpu.VMEM((6, 128), jnp.int32),
            pltpu.VMEM((23, 16, 128), F32),
            pltpu.VMEM((192, 2048), BF),
            pltpu.VMEM((96, 2048), F32),
            pltpu.VMEM((768, 2048), BF),
            pltpu.VMEM((2, 96, 768), F32),
            pltpu.VMEM((2, 96, 128), BF),
            pltpu.VMEM((2, 2, 96, 128), F32),
            pltpu.VMEM((2, 2, 40, 768), F32),
            pltpu.VMEM((2, 96, 128), BF),
            pltpu.VMEM((2, 2, 96, 128), F32),
            pltpu.VMEM((4, 48, 128), BF),
            pltpu.VMEM((4, 2, 40, 128), F32),
            pltpu.VMEM((2, 6, 128, 128), F32),
            pltpu.VMEM((2, 6, 128, 128), F32),
            pltpu.VMEM((2, 6, 128, 128), F32),
            pltpu.VMEM((2, 96, 768), BF),
            pltpu.SemaphoreType.DMA((5,)),
            pltpu.SemaphoreType.DMA((16,)),
            pltpu.SemaphoreType.DMA((16,)),
        ],
        compiler_params=pltpu.CompilerParams(
            collective_id=0, has_side_effects=True, vmem_limit_bytes=32 * 1024 * 1024
        ),
        name="fish_step",
    )(
        velocity,
        marker_cell.reshape(3, 16, 128),
        marker_frac.reshape(2, 16, 128),
        marker_force.reshape(2, 16, 128),
        fish_owner.reshape(6, 128),
    )
    return out_v, out_m.reshape(2, 1, 1, 2048)


def solution(mesh):
    placed = (
        P(None, None, "gx", "gy"),
        P(None, "gx", "gy", None),
        P(None, "gx", "gy", None),
        P(None, "gx", "gy", None),
        P(),
    )
    return jax.shard_map(
        body,
        mesh=mesh,
        in_specs=placed,
        out_specs=(P(None, None, "gx", "gy"), P(None, "gx", "gy", None)),
        check_vma=False,
    )
```

```python
import functools
import math

import jax
import jax.numpy as jnp
from jax import lax
from jax.experimental import pallas as pl
from jax.experimental.pallas import tpu as pltpu
from jax.sharding import PartitionSpec as P

MARGIN = 16
FISH_MARK = 1024
COURANT = 0.25
VISCOUS = 1.5
LANES = 128
BF = jnp.bfloat16
F32 = jnp.float32

SIDES = [(1, 0), (-1, 0), (0, 1), (0, -1), (1, 1), (-1, 1), (1, -1), (-1, -1)]


def half_angle(t):
    z = t * (0.5 * math.pi)
    q = z * z
    s = 1.0 / math.factorial(13)
    for n in (11, 9, 7, 5, 3, 1):
        s = s * q + (-1.0) ** ((n - 1) // 2) / math.factorial(n)
    c = 1.0 / math.factorial(12)
    for n in (10, 8, 6, 4, 2, 0):
        c = c * q + (-1.0) ** (n // 2) / math.factorial(n)
    return s * z, c


def weights(t):
    s, c = half_angle(t)
    return (0.25 * (1.0 - s), 0.25 * (1.0 + c), 0.25 * (1.0 + s), 0.25 * (1.0 - c))


def chain(d, values, zero):
    out = jnp.where(d == 2.0, values[3], zero)
    out = jnp.where(d == 1.0, values[2], out)
    out = jnp.where(d == 0.0, values[1], out)
    return jnp.where(d == -1.0, values[0], out)


def kernel(
    nx, ny,
    vel_h, cell_h, frac_h, force_h, owner_h,
    out_v, out_m,
    vel, cell, frac, force, owner,
    q32, left, wx_hot, wy_hot, mv, px, py, pc, rx, ry, rc,
    mt, ca, w1, ta,
    in_sem, send1, recv1,
):
    ix = lax.axis_index("gx")
    iy = lax.axis_index("gy")

    def at(dx, dy):
        return {"gx": lax.rem(ix + dx + nx, nx), "gy": lax.rem(iy + dy + ny, ny)}

    barrier = pltpu.get_barrier_semaphore()
    for dx, dy in SIDES:
        pl.semaphore_signal(
            barrier, inc=1, device_id=at(dx, dy), device_id_type=pl.DeviceIdType.MESH
        )
    loads = []
    for n, (src, dst) in enumerate(
        ((cell_h, cell), (frac_h, frac), (force_h, force), (owner_h, owner), (vel_h, vel))
    ):
        loads.append(pltpu.make_async_copy(src, dst, in_sem.at[n]))
        loads[-1].start()
    for load in loads[:4]:
        load.wait()

    mine = jnp.where(owner[...] == ix * ny + iy, 1.0, 0.0)
    count = jnp.sum(jnp.sum(mine, axis=1, keepdims=True), axis=0, keepdims=True)
    slot = lax.broadcasted_iota(jnp.int32, (16, LANES), 0) * LANES + lax.broadcasted_iota(
        jnp.int32, (16, LANES), 1
    )
    alive = jnp.where(slot.astype(F32) < FISH_MARK * count, 1.0, 0.0)
    rel_x = lax.rem(cell[0] - ix * 64 + (MARGIN + nx * 64), nx * 64)
    rel_y = lax.rem(cell[1] - iy * 128 + (MARGIN + ny * 128), ny * 128) - MARGIN
    q32[0] = rel_x.astype(F32)
    q32[1] = rel_y.astype(F32)
    wx = weights(frac[0])
    wy = weights(frac[1])
    for k in range(4):
        q32[2 + k] = wx[k]
        q32[6 + k] = wy[k]
        for c in range(2):
            q32[10 + 4 * c + k] = force[c] * alive * wx[k]
        q32[18 + k] = jnp.where(cell[2] == k, 1.0, 0.0)
    q32[22] = alive

    rows16 = lax.broadcasted_iota(jnp.int32, (16, LANES), 0).astype(F32)
    zero16 = jnp.zeros((16, LANES), BF)
    strips = ((512, -26.0), (528, -10.0), (640, 122.0), (656, 138.0))

    def operands(r, _):
        lanes = pl.ds(pl.multiple_of(r * LANES, LANES), LANES)

        def row(n):
            return jnp.broadcast_to(q32[n, pl.ds(r, 1), :], (16, LANES))

        dx0 = rows16 - row(0)
        lw = [[row(10 + 4 * c + k).astype(BF) for k in range(4)] for c in range(2)]
        for b in range(6):
            d = (dx0 + 16.0 * b).astype(BF)
            for c in range(2):
                left[pl.ds(96 * c + 16 * b, 16), lanes] = chain(d, lw[c], zero16)
        dy0 = rows16 - row(1)
        yw = [row(6 + k).astype(BF) for k in range(4)]
        lv = [row(18 + k).astype(BF) for k in range(4)]
        for b in range(12):
            base, step = (16.0 * b, 128) if b < 8 else (strips[b - 8][1], 32)
            first_row = 16 * b if b < 8 else strips[b - 8][0]
            d = (dy0 + base).astype(BF)
            w = chain(d, yw, zero16)
            for l in range(4):
                wy_hot[pl.ds(first_row + step * l, 16), lanes] = w * lv[l]
        return 0

    lax.fori_loop(0, 16, operands, 0)

    loads[4].wait()
    lane64 = lax.broadcasted_iota(jnp.int32, (64, LANES), 1)
    level64, j64 = lane64 // 32, lane64 % 32
    for c in range(2):
        spread = lax.dot_general(
            left[pl.ds(96 * c, 96), :], wy_hot[...], (((1,), (1,)), ((), ())),
            preferred_element_type=F32,
        )
        mv[c] = spread
        low_part = jnp.zeros((64, LANES), F32)
        high_part = jnp.zeros((64, LANES), F32)
        for l in range(4):
            ls = slice(128 * l, 128 * l + 128)
            v = vel[l, c]
            mv[c, 16:80, ls] = spread[16:80, ls] + v
            low_part = jnp.where(
                (level64 == l) & (j64 >= 26), pltpu.roll(v, 32 * l + 26, 1), low_part
            )
            high_part = jnp.where(
                (level64 == l) & (j64 < 6), pltpu.roll(v, 32 * l + 6, 1), high_part
            )
        mv[c, 16:80, 512:640] = spread[16:80, 512:640] + low_part
        mv[c, 16:80, 640:768] = spread[16:80, 640:768] + high_part

    lane = lax.broadcasted_iota(jnp.int32, (96, LANES), 1)
    level, j = lane // 32, lane % 32
    strip0 = [mv[c, :, 512:640] for c in range(2)]
    strip1 = [mv[c, :, 640:768] for c in range(2)]
    near = j < 16
    outer = [
        jnp.where(near, pltpu.roll(strip1[0], 122, 1), pltpu.roll(strip1[1], 10, 1)),
        jnp.where(near, pltpu.roll(strip0[0], 118, 1), pltpu.roll(strip0[1], 6, 1)),
    ]
    inner = [[], []]
    for c in range(2):
        up = pltpu.roll(strip1[c], 20, 1)
        down = pltpu.roll(strip0[c], 108, 1)
        for l in range(4):
            t = mv[c, :, 128 * l : 128 * l + 128]
            up = jnp.where((level == l) & (j < 26), pltpu.roll(t, (32 * l + 26) % LANES, 1), up)
            down = jnp.where((level == l) & (j >= 6), pltpu.roll(t, 32 * l + 6, 1), down)
        inner[0].append(up)
        inner[1].append(down)
    filler = jnp.zeros((8, LANES), F32)
    for side in range(2):
        parts = [inner[side][0], inner[side][1], outer[side]]
        py[side] = jnp.concatenate(parts, axis=0).astype(BF)
        for n in range(4):
            dx, dy = SIDES[4 + n]
            if (0 if dy == 1 else 1) == side:
                lo = 56 if dx == 1 else 0
                pc[n] = jnp.concatenate([p[lo : lo + 40] for p in parts] + [filler], axis=0).astype(BF)
    for n, lo in enumerate((56, 0)):
        px[n] = jnp.concatenate([mv[0, lo : lo + 40, :], mv[1, lo : lo + 40, :]], axis=0).astype(BF)

    pl.semaphore_wait(barrier, 8)

    copies = []

    def send(n, src, dst, dx, dy):
        copy = pltpu.make_async_remote_copy(
            src_ref=src, dst_ref=dst, send_sem=send1.at[n], recv_sem=recv1.at[n],
            device_id=at(dx, dy), device_id_type=pl.DeviceIdType.MESH,
        )
        copy.start()
        copies.append(copy)

    for n in range(4):
        send(4 + n, pc.at[n], rc.at[n], *SIDES[4 + n])
    for n in range(2):
        send(2 + n, py.at[n], ry.at[n], *SIDES[2 + n])
    for n in range(2):
        send(n, px.at[n], rx.at[n], *SIDES[n])

    rows8 = lax.broadcasted_iota(jnp.int32, (8, LANES), 0).astype(F32)

    def x_hot(r, _):
        lanes = pl.ds(pl.multiple_of(r * LANES, LANES), LANES)

        def row(n):
            return jnp.broadcast_to(q32[n, pl.ds(r, 1), :], (8, LANES))

        d = rows8 - row(0)
        ww = [row(2 + k) * row(22) for k in range(4)]
        for b in range(12):
            wx_hot[pl.ds(8 * b, 8), lanes] = chain(d + 8.0 * b, ww, 0.0)
        return 0

    lax.fori_loop(0, 16, x_hot, 0)
    for ref in (mt, ca, w1):
        for c in range(2):
            for t in range(6):
                ref[c, t, 0:8, :] = jnp.zeros((8, LANES), F32)
                ref[c, t, 120:128, :] = jnp.zeros((8, LANES), F32)

    for copy in copies:
        copy.wait()

    corner = {}
    for n in range(4):
        dx, dy = SIDES[4 + n]
        corner[0 if dx == 1 else 1, 0 if dy == 1 else 1] = n

    def joined(mid, first, last):
        return [
            first[0:8], mid[0:32] + first[8:40], mid[32:64], mid[64:96] + last[0:32], last[32:40]
        ]

    ryf = [ry[side].astype(F32) for side in range(2)]
    rcf = [rc[n].astype(F32) for n in range(4)]
    rxf = [rx[n].astype(F32) for n in range(2)]
    from_y = [[r[96 * p : 96 * p + 96] for p in range(3)] for r in ryf]
    from_c = [[r[40 * p : 40 * p + 40] for p in range(3)] for r in rcf]
    pack16 = [
        jnp.concatenate(
            joined(from_y[side][2], from_c[corner[0, side]][2], from_c[corner[1, side]][2]), axis=0
        )
        for side in range(2)
    ]
    lane112 = lax.broadcasted_iota(jnp.int32, (112, LANES), 1)

    def rolled(q, by):
        return pltpu.roll(q, by % LANES, 1) if by % LANES else q

    for c in range(2):
        for t in range(6):
            ls = slice(128 * t, 128 * t + 128)
            mid = mv[c, :, ls]
            first, last = (r[40 * c : 40 * c + 40, ls] for r in rxf)
            if t < 4:
                a = jnp.concatenate(joined(mid, first, last), axis=0)
                g = 32 * t + 16 * c
                a = a + jnp.where(lane112 < 16, rolled(pack16[0], -g), 0.0)
                a = a + jnp.where(lane112 >= 112, rolled(pack16[1], 112 - g), 0.0)
            else:
                side = t - 4
                mid = mid + from_y[side][c]
                first = first + from_c[corner[0, side]][c]
                last = last + from_c[corner[1, side]][c]
                a = jnp.concatenate(joined(mid, first, last), axis=0)
            mt[c, t, 8:120, :] = a

    for t in range(6):
        a = COURANT * mt[0, t, 8:120, :]
        b = COURANT * mt[1, t, 8:120, :]
        ap, am = jnp.maximum(a, 0.0), jnp.minimum(a, 0.0)
        bp, bm = jnp.maximum(b, 0.0), jnp.minimum(b, 0.0)
        for c in range(2):
            q = mt[c, t, 8:120, :]
            change = ap * (q - mt[c, t, 7:119, :]) + am * (mt[c, t, 9:121, :] - q)
            change = change + bp * (q - rolled(q, 1)) + bm * (rolled(q, -1) - q)
            ca[c, t, 8:120, :] = q - change

    def around(ref, c, t, lo, hi):
        q = ref[c, t, lo:hi, :]
        total = ref[c, t, lo - 1 : hi - 1, :] + ref[c, t, lo + 1 : hi + 1, :]
        total = total + rolled(q, 1) + rolled(q, -1)
        if t < 4:
            return total + ref[c, min(t + 1, 3), lo:hi, :] + ref[c, max(t - 1, 0), lo:hi, :]
        lanes = lax.broadcasted_iota(jnp.int32, (hi - lo, LANES), 1)
        total = total + jnp.where(lanes >= 96, q, rolled(q, -32))
        return total + jnp.where(lanes < 32, q, rolled(q, 32))

    scale = 1.0 / (1.0 + 6.0 * VISCOUS)
    for c in range(2):
        for t in range(6):
            w1[c, t, 8:120, :] = (ca[c, t, 8:120, :] + VISCOUS * around(ca, c, t, 8, 120)) * scale
    for c in range(2):
        done = [
            (ca[c, t, 16:112, :] + VISCOUS * around(w1, c, t, 16, 112)) * scale for t in (4, 5)
        ]
        for l in range(4):
            w2 = (ca[c, l, 16:112, :] + VISCOUS * around(w1, c, l, 16, 112)) * scale
            w2 = jnp.where(lane < 3, rolled(done[0], -(32 * l + 26)), w2)
            w2 = jnp.where(lane >= 125, rolled(done[1], 122 - 32 * l), w2)
            out_v[l, c] = w2[16:80]
            ta[c, :, 128 * l : 128 * l + 128] = w2.astype(BF)
        ta[c, :, 512:640] = jnp.where((j >= 10) & (j < 26), done[0], 0.0).astype(BF)
        ta[c, :, 640:768] = jnp.where((j >= 6) & (j < 22), done[1], 0.0).astype(BF)

    for r in range(4):
        lanes = slice(512 * r, 512 * r + 512)
        for c in range(2):
            part = jnp.dot(ta[c], wy_hot[:, lanes], preferred_element_type=F32)
            summed = jnp.sum(part * wx_hot[:, lanes], axis=0, keepdims=True)
            for i in range(4):
                out_m[c, 4 * r + i : 4 * r + i + 1, :] = summed[:, LANES * i : LANES * i + LANES]


def body(velocity, marker_cell, marker_frac, marker_force, fish_owner):
    nx = lax.axis_size("gx")
    ny = lax.axis_size("gy")
    vm = pl.BlockSpec(memory_space=pltpu.VMEM)
    out_v, out_m = pl.pallas_call(
        functools.partial(kernel, nx, ny),
        out_shape=(
            jax.ShapeDtypeStruct((4, 2, 64, 128), F32),
            jax.ShapeDtypeStruct((2, 16, 128), F32),
        ),
        in_specs=[pl.BlockSpec(memory_space=pltpu.HBM)] * 5,
        out_specs=(vm, vm),
        scratch_shapes=[
            pltpu.VMEM((4, 2, 64, 128), F32),
            pltpu.VMEM((3, 16, 128), jnp.int32),
            pltpu.VMEM((2, 16, 128), F32),
            pltpu.VMEM((2, 16, 128), F32),
            pltpu.VMEM((6, 128), jnp.int32),
            pltpu.VMEM((23, 16, 128), F32),
            pltpu.VMEM((192, 2048), BF),
            pltpu.VMEM((96, 2048), F32),
            pltpu.VMEM((768, 2048), BF),
            pltpu.VMEM((2, 96, 768), F32),
            pltpu.VMEM((2, 80, 768), BF),
            pltpu.VMEM((2, 288, 128), BF),
            pltpu.VMEM((4, 128, 128), BF),
            pltpu.VMEM((2, 80, 768), BF),
            pltpu.VMEM((2, 288, 128), BF),
            pltpu.VMEM((4, 128, 128), BF),
            pltpu.VMEM((2, 6, 128, 128), F32),
            pltpu.VMEM((2, 6, 128, 128), F32),
            pltpu.VMEM((2, 6, 128, 128), F32),
            pltpu.VMEM((2, 96, 768), BF),
            pltpu.SemaphoreType.DMA((5,)),
            pltpu.SemaphoreType.DMA((8,)),
            pltpu.SemaphoreType.DMA((8,)),
        ],
        compiler_params=pltpu.CompilerParams(
            collective_id=0, has_side_effects=True, vmem_limit_bytes=32 * 1024 * 1024
        ),
        name="fish_step",
    )(
        pltpu.with_memory_space_constraint(velocity, pltpu.HBM),
        pltpu.with_memory_space_constraint(marker_cell.reshape(3, 16, 128), pltpu.HBM),
        pltpu.with_memory_space_constraint(marker_frac.reshape(2, 16, 128), pltpu.HBM),
        pltpu.with_memory_space_constraint(marker_force.reshape(2, 16, 128), pltpu.HBM),
        pltpu.with_memory_space_constraint(fish_owner.reshape(6, 128), pltpu.HBM),
    )
    return out_v, out_m.reshape(2, 1, 1, 2048)


def solution(mesh):
    placed = (
        P(None, None, "gx", "gy"),
        P(None, "gx", "gy", None),
        P(None, "gx", "gy", None),
        P(None, "gx", "gy", None),
        P(),
    )
    return jax.shard_map(
        body,
        mesh=mesh,
        in_specs=placed,
        out_specs=(P(None, None, "gx", "gy"), P(None, "gx", "gy", None)),
        check_vma=False,
    )
```

```python
import functools
import math

import jax
import jax.numpy as jnp
from jax import lax
from jax.experimental import pallas as pl
from jax.experimental.pallas import tpu as pltpu
from jax.sharding import PartitionSpec as P

MARGIN = 16
FISH_MARK = 1024
COURANT = 0.25
VISCOUS = 1.5
LANES = 128
BF = jnp.bfloat16
F32 = jnp.float32

SIDES = [(1, 0), (-1, 0), (0, 1), (0, -1), (1, 1), (-1, 1), (1, -1), (-1, -1)]


def half_angle(t):
    z = t * (0.5 * math.pi)
    q = z * z
    s = 1.0 / math.factorial(13)
    for n in (11, 9, 7, 5, 3, 1):
        s = s * q + (-1.0) ** ((n - 1) // 2) / math.factorial(n)
    c = 1.0 / math.factorial(12)
    for n in (10, 8, 6, 4, 2, 0):
        c = c * q + (-1.0) ** (n // 2) / math.factorial(n)
    return s * z, c


def weights(t):
    s, c = half_angle(t)
    return (0.25 * (1.0 - s), 0.25 * (1.0 + c), 0.25 * (1.0 + s), 0.25 * (1.0 - c))


def chain(d, values, zero):
    out = jnp.where(d == 2.0, values[3], zero)
    out = jnp.where(d == 1.0, values[2], out)
    out = jnp.where(d == 0.0, values[1], out)
    return jnp.where(d == -1.0, values[0], out)


def pick(ref, source):
    rows, columns = ref.shape
    n = lax.broadcasted_iota(jnp.int32, (16, columns), 1)
    below = source(n) - lax.broadcasted_iota(jnp.int32, (16, columns), 0)
    for lo in range(0, rows, 16):
        ref[lo : lo + 16, :] = jnp.where(below == lo, 1.0, 0.0).astype(BF)


def matrices(w_in, w_out, w_place, w_adv, w_t, w_s, w_fix):
    def inner_of(n):
        p, l = n % 32, (n // 32) % 4
        up = jnp.where(p < 26, 128 * l + p + 102, 640 + 32 * l + p - 20)
        down = jnp.where(p < 6, 512 + 32 * l + p + 20, 128 * l + p - 6)
        return jnp.where(n < 128, up, down)

    def outer_of(n):
        i, c, l = n % 16, (n // 16) % 2, (n // 32) % 4
        return 256 * c + 32 * l + i + jnp.where(n < 128, 128 + 6, 10)

    def place_of(n):
        y, l, c = n % 128, (n // 128) % 4, n // 512
        at = 32 * l + 16 * c
        return jnp.where(y < 16, at + y, jnp.where(y >= 112, 128 + at + y - 112, -1))

    def fix_of(n):
        y, l = n % 128, n // 128
        return jnp.where(
            y < 3, 32 * l + 26 + y, jnp.where(y >= 125, 128 + 32 * l + y - 122, -1)
        )

    pick(w_in, inner_of)
    pick(w_out, outer_of)
    pick(w_place, place_of)
    pick(w_fix, fix_of)
    y = lax.broadcasted_iota(jnp.int32, (16, LANES), 1)
    r = lax.broadcasted_iota(jnp.int32, (16, LANES), 0)

    def one(of):
        return jnp.where(of == r, 1.0, 0.0)

    for lo in range(0, 256, 16):
        base = lo % LANES
        here, prev, after = one(y - base), one((y + 127) % 128 - base), one((y + 1) % 128 - base)
        w_adv[lo : lo + 16, 0:128] = (here - prev).astype(BF)
        w_adv[lo : lo + 16, 128:256] = (after - here).astype(BF)
        w_t[lo : lo + 16, :] = (prev + after).astype(BF)
        upper = one(jnp.where(y < 96, y + 32, y) - base)
        lower = one(jnp.where(y >= 32, y - 32, y) - base)
        w_s[lo : lo + 16, :] = (prev + after + upper + lower).astype(BF)


def pieces(v):
    high = v.astype(BF)
    return high, (v - high.astype(F32)).astype(BF)


def kernel(
    nx, ny,
    vel_h, cell_h, frac_h, force_h, owner_h,
    out_v, out_m,
    vel, cell, frac, force, owner,
    q32, left, wx_hot, wy_hot, mv, mvb, px, py, pc, rx, ry, rc,
    mt, ca, w1, sp, ws, ta, w_in, w_out, w_place, w_adv, w_t, w_s, w_fix,
    in_sem, send1, recv1,
):
    ix = lax.axis_index("gx")
    iy = lax.axis_index("gy")

    def at(dx, dy):
        return {"gx": lax.rem(ix + dx + nx, nx), "gy": lax.rem(iy + dy + ny, ny)}

    loads = []
    for n, (src, dst) in enumerate(
        ((cell_h, cell), (frac_h, frac), (force_h, force), (owner_h, owner), (vel_h, vel))
    ):
        loads.append(pltpu.make_async_copy(src, dst, in_sem.at[n]))
        loads[-1].start()
    barrier = pltpu.get_barrier_semaphore()
    for dx, dy in SIDES:
        pl.semaphore_signal(
            barrier, inc=1, device_id=at(dx, dy), device_id_type=pl.DeviceIdType.MESH
        )
    matrices(w_in, w_out, w_place, w_adv, w_t, w_s, w_fix)
    for load in loads:
        load.wait()

    mine = jnp.where(owner[...] == ix * ny + iy, 1.0, 0.0)
    count = jnp.sum(jnp.sum(mine, axis=1, keepdims=True), axis=0, keepdims=True)
    slot = lax.broadcasted_iota(jnp.int32, (16, LANES), 0) * LANES + lax.broadcasted_iota(
        jnp.int32, (16, LANES), 1
    )
    alive = jnp.where(slot.astype(F32) < FISH_MARK * count, 1.0, 0.0)
    rel_x = lax.rem(cell[0] - ix * 64 + (MARGIN + nx * 64), nx * 64)
    rel_y = lax.rem(cell[1] - iy * 128 + (MARGIN + ny * 128), ny * 128) - MARGIN
    q32[0] = rel_x.astype(F32)
    q32[1] = rel_y.astype(F32)
    wx = weights(frac[0])
    wy = weights(frac[1])
    for k in range(4):
        q32[2 + k] = wx[k]
        q32[6 + k] = wy[k]
        for c in range(2):
            q32[10 + 4 * c + k] = force[c] * alive * wx[k]
        q32[18 + k] = jnp.where(cell[2] == k, 1.0, 0.0)
    q32[22] = alive

    rows16 = lax.broadcasted_iota(jnp.int32, (16, LANES), 0).astype(F32)
    zero16 = jnp.zeros((16, LANES), BF)
    strips = ((512, -26.0), (528, -10.0), (640, 122.0), (656, 138.0))

    def operands(r, _):
        lanes = slice(r * LANES, r * LANES + LANES)

        def row(n):
            return jnp.broadcast_to(q32[n, r : r + 1, :], (16, LANES))

        dx0 = rows16 - row(0)
        lw = [[row(10 + 4 * c + k).astype(BF) for k in range(4)] for c in range(2)]
        for b in range(6):
            d = (dx0 + 16.0 * b).astype(BF)
            for c in range(2):
                left[pl.ds(96 * c + 16 * b, 16), lanes] = chain(d, lw[c], zero16)
        dy0 = rows16 - row(1)
        yw = [row(6 + k).astype(BF) for k in range(4)]
        lv = [row(18 + k).astype(BF) for k in range(4)]
        for b in range(12):
            base, step = (16.0 * b, 128) if b < 8 else (strips[b - 8][1], 32)
            first_row = 16 * b if b < 8 else strips[b - 8][0]
            d = (dy0 + base).astype(BF)
            w = chain(d, yw, zero16)
            for l in range(4):
                wy_hot[pl.ds(first_row + step * l, 16), lanes] = w * lv[l]
        return 0

    for r in range(16):
        operands(r, 0)

    lane64 = lax.broadcasted_iota(jnp.int32, (64, LANES), 1)
    level64, j64 = lane64 // 32, lane64 % 32
    both = lax.dot_general(
        left[...], wy_hot[...], (((1,), (1,)), ((), ())), preferred_element_type=F32
    )
    for c in range(2):
        spread = both[96 * c : 96 * c + 96]
        mv[c] = spread
        low_part = jnp.zeros((64, LANES), F32)
        high_part = jnp.zeros((64, LANES), F32)
        for l in range(4):
            ls = slice(128 * l, 128 * l + 128)
            v = vel[l, c]
            mv[c, 16:80, ls] = spread[16:80, ls] + v
            low_part = jnp.where(
                (level64 == l) & (j64 >= 26), pltpu.roll(v, 32 * l + 26, 1), low_part
            )
            high_part = jnp.where(
                (level64 == l) & (j64 < 6), pltpu.roll(v, 32 * l + 6, 1), high_part
            )
        mv[c, 16:80, 512:640] = spread[16:80, 512:640] + low_part
        mv[c, 16:80, 640:768] = spread[16:80, 640:768] + high_part

    for c in range(2):
        mvb[96 * c : 96 * c + 96, :] = mv[c].astype(BF)
    inner = jnp.dot(mvb[...], w_in[...], preferred_element_type=F32)
    outer = jnp.dot(mvb[0:96, 512:768], w_out[0:256, :], preferred_element_type=F32)
    outer = outer + jnp.dot(mvb[96:192, 512:768], w_out[256:512, :], preferred_element_type=F32)
    filler = jnp.zeros((8, LANES), F32)
    for side in range(2):
        ls = slice(128 * side, 128 * side + 128)
        parts = [inner[0:96, ls], inner[96:192, ls], outer[:, ls]]
        py[side] = jnp.concatenate(parts, axis=0).astype(BF)
        for n in range(4):
            dx, dy = SIDES[4 + n]
            if (0 if dy == 1 else 1) == side:
                lo = 56 if dx == 1 else 0
                pc[n] = jnp.concatenate([p[lo : lo + 40] for p in parts] + [filler], axis=0).astype(BF)
    for n, lo in enumerate((56, 0)):
        px[n] = jnp.concatenate([mv[0, lo : lo + 40, :], mv[1, lo : lo + 40, :]], axis=0).astype(BF)

    pl.semaphore_wait(barrier, 8)

    copies = []

    def send(n, src, dst, dx, dy):
        copy = pltpu.make_async_remote_copy(
            src_ref=src, dst_ref=dst, send_sem=send1.at[n], recv_sem=recv1.at[n],
            device_id=at(dx, dy), device_id_type=pl.DeviceIdType.MESH,
        )
        copy.start()
        copies.append(copy)

    for n in range(4):
        send(4 + n, pc.at[n], rc.at[n], *SIDES[4 + n])
    for n in range(2):
        send(2 + n, py.at[n], ry.at[n], *SIDES[2 + n])
    for n in range(2):
        send(n, px.at[n], rx.at[n], *SIDES[n])

    rows8 = lax.broadcasted_iota(jnp.int32, (8, LANES), 0).astype(F32)

    def x_hot(r, _):
        lanes = pl.ds(pl.multiple_of(r * LANES, LANES), LANES)

        def row(n):
            return jnp.broadcast_to(q32[n, pl.ds(r, 1), :], (8, LANES))

        d = rows8 - row(0)
        ww = [row(2 + k) * row(22) for k in range(4)]
        for b in range(12):
            wx_hot[pl.ds(8 * b, 8), lanes] = chain(d + 8.0 * b, ww, 0.0)
        return 0

    lax.fori_loop(0, 16, x_hot, 0)
    for ref in (mt, ca, w1):
        for c in range(2):
            for t in range(6):
                ref[c, t, 0:8, :] = jnp.zeros((8, LANES), F32)
                ref[c, t, 120:128, :] = jnp.zeros((8, LANES), F32)

    for copy in copies:
        copy.wait()

    corner = {}
    for n in range(4):
        dx, dy = SIDES[4 + n]
        corner[0 if dx == 1 else 1, 0 if dy == 1 else 1] = n

    def joined(mid, first, last):
        return [
            first[0:8], mid[0:32] + first[8:40], mid[32:64], mid[64:96] + last[0:32], last[32:40]
        ]

    ryf = [ry[side].astype(F32) for side in range(2)]
    rcf = [rc[n].astype(F32) for n in range(4)]
    rxf = [rx[n].astype(F32) for n in range(2)]
    from_y = [[r[96 * p : 96 * p + 96] for p in range(3)] for r in ryf]
    from_c = [[r[40 * p : 40 * p + 40] for p in range(3)] for r in rcf]
    placed = jnp.dot(
        jnp.concatenate(
            [
                jnp.concatenate([ry[side, 192:288, :] for side in range(2)], axis=1),
                jnp.concatenate([rc[corner[0, side], 80:128, :] for side in range(2)], axis=1),
                jnp.concatenate([rc[corner[1, side], 80:128, :] for side in range(2)], axis=1),
            ],
            axis=0,
        ),
        w_place[...],
        preferred_element_type=F32,
    )

    for t in range(6):
        for c in range(2):
            ls = slice(128 * t, 128 * t + 128)
            mid = mv[c, :, ls]
            first, last = (r[40 * c : 40 * c + 40, ls] for r in rxf)
            if t < 4:
                ps = slice(512 * c + 128 * t, 512 * c + 128 * t + 128)
                mid = mid + placed[0:96, ps]
                first = first + placed[96:136, ps]
                last = last + placed[144:184, ps]
            else:
                side = t - 4
                mid = mid + from_y[side][c]
                first = first + from_c[corner[0, side]][c]
                last = last + from_c[corner[1, side]][c]
            a = jnp.concatenate(joined(mid, first, last), axis=0)
            mt[c, t, 8:120, :] = a
            high, low = pieces(a)
            sp[t, 112 * c : 112 * c + 112, 0:128] = high
            sp[t, 112 * c : 112 * c + 112, 128:256] = low

    for t in range(6):
        steps = jnp.dot(sp[t], w_adv[...], preferred_element_type=F32)
        for lo in range(0, 112, 16):
            here = slice(lo + 8, lo + 24)
            a = COURANT * mt[0, t, here, :]
            b = COURANT * mt[1, t, here, :]
            ap, am = jnp.maximum(a, 0.0), jnp.minimum(a, 0.0)
            bp, bm = jnp.maximum(b, 0.0), jnp.minimum(b, 0.0)
            for c in range(2):
                q = mt[c, t, here, :]
                row = 112 * c + lo
                change = ap * (q - mt[c, t, lo + 7 : lo + 23, :]) + am * (mt[c, t, lo + 9 : lo + 25, :] - q)
                change = change + bp * steps[row : row + 16, 0:128] + bm * steps[row : row + 16, 128:256]
                value = q - change
                ca[c, t, here, :] = value
                high, low = pieces(value)
                ws[t, row : row + 16, 0:128] = high
                ws[t, row : row + 16, 128:256] = low

    scale = 1.0 / (1.0 + 6.0 * VISCOUS)

    def sweep(ref, beside, t, c, lo, row):
        here = slice(lo + 8, lo + 24)
        total = ref[c, t, lo + 7 : lo + 23, :] + ref[c, t, lo + 9 : lo + 25, :]
        total = total + beside[row : row + 16]
        if t < 4:
            total = total + (ref[c, min(t + 1, 3), here, :] + ref[c, max(t - 1, 0), here, :])
        return scale * ca[c, t, here, :] + (scale * VISCOUS) * total

    for t in range(6):
        beside = jnp.dot(ws[t], (w_t if t < 4 else w_s)[...], preferred_element_type=F32)
        for c in range(2):
            for lo in range(0, 112, 16):
                value = sweep(ca, beside, t, c, lo, 112 * c + lo)
                w1[c, t, lo + 8 : lo + 24, :] = value
                high, low = pieces(value)
                sp[t, 112 * c + lo : 112 * c + lo + 16, 0:128] = high
                sp[t, 112 * c + lo : 112 * c + lo + 16, 128:256] = low

    lane16 = lax.broadcasted_iota(jnp.int32, (16, LANES), 1)
    j16 = lane16 % 32
    keep = ((j16 >= 10) & (j16 < 26), (j16 >= 6) & (j16 < 22))
    for t in (4, 5):
        ls = slice(128 * (t - 4), 128 * (t - 4) + 128)
        beside = jnp.dot(sp[t], w_s[...], preferred_element_type=F32)
        for c in range(2):
            values = [
                sweep(w1, beside, t, c, lo, 112 * c + lo) for lo in range(0, 112, 16)
            ]
            whole = jnp.concatenate(values, axis=0)[8:104]
            high, low = pieces(whole)
            ws[0, 96 * c : 96 * c + 96, ls] = high
            ws[1, 96 * c : 96 * c + 96, ls] = low
            kept = jnp.where(keep[t - 4], whole.reshape(6, 16, LANES), 0.0).reshape(96, LANES)
            ta[96 * c : 96 * c + 96, 128 * t : 128 * t + 128] = kept.astype(BF)
    ends = jnp.dot(ws[0, 0:192, :], w_fix[...], preferred_element_type=F32)
    ends = ends + jnp.dot(ws[1, 0:192, :], w_fix[...], preferred_element_type=F32)
    lane = lax.broadcasted_iota(jnp.int32, (96, LANES), 1)
    inside = (lane >= 3) & (lane < 125)
    for t in range(4):
        ls = slice(128 * t, 128 * t + 128)
        beside = jnp.dot(sp[t], w_t[...], preferred_element_type=F32)
        for c in range(2):
            values = [
                sweep(w1, beside, t, c, lo, 112 * c + lo) for lo in range(0, 112, 16)
            ]
            whole = jnp.concatenate(values, axis=0)[8:104]
            whole = jnp.where(inside, whole, ends[96 * c : 96 * c + 96, ls])
            out_v[t, c] = whole[16:80]
            ta[96 * c : 96 * c + 96, ls] = whole.astype(BF)

    for r in range(4):
        lanes = slice(512 * r, 512 * r + 512)
        both = jnp.dot(ta[...], wy_hot[:, lanes], preferred_element_type=F32)
        for c in range(2):
            part = both[96 * c : 96 * c + 96]
            summed = jnp.sum(part * wx_hot[:, lanes], axis=0, keepdims=True)
            for i in range(4):
                out_m[c, 4 * r + i : 4 * r + i + 1, :] = summed[:, LANES * i : LANES * i + LANES]


def body(velocity, marker_cell, marker_frac, marker_force, fish_owner):
    nx = lax.axis_size("gx")
    ny = lax.axis_size("gy")
    vm = pl.BlockSpec(memory_space=pltpu.VMEM)
    out_v, out_m = pl.pallas_call(
        functools.partial(kernel, nx, ny),
        out_shape=(
            jax.ShapeDtypeStruct((4, 2, 64, 128), F32),
            jax.ShapeDtypeStruct((2, 16, 128), F32),
        ),
        in_specs=[pl.BlockSpec(memory_space=pltpu.HBM)] * 5,
        out_specs=(vm, vm),
        scratch_shapes=[
            pltpu.VMEM((4, 2, 64, 128), F32),
            pltpu.VMEM((3, 16, 128), jnp.int32),
            pltpu.VMEM((2, 16, 128), F32),
            pltpu.VMEM((2, 16, 128), F32),
            pltpu.VMEM((6, 128), jnp.int32),
            pltpu.VMEM((23, 16, 128), F32),
            pltpu.VMEM((192, 2048), BF),
            pltpu.VMEM((96, 2048), F32),
            pltpu.VMEM((768, 2048), BF),
            pltpu.VMEM((2, 96, 768), F32),
            pltpu.VMEM((192, 768), BF),
            pltpu.VMEM((2, 80, 768), BF),
            pltpu.VMEM((2, 288, 128), BF),
            pltpu.VMEM((4, 128, 128), BF),
            pltpu.VMEM((2, 80, 768), BF),
            pltpu.VMEM((2, 288, 128), BF),
            pltpu.VMEM((4, 128, 128), BF),
            pltpu.VMEM((2, 6, 128, 128), F32),
            pltpu.VMEM((2, 6, 128, 128), F32),
            pltpu.VMEM((2, 6, 128, 128), F32),
            pltpu.VMEM((6, 224, 256), BF),
            pltpu.VMEM((6, 224, 256), BF),
            pltpu.VMEM((192, 768), BF),
            pltpu.VMEM((768, 256), BF),
            pltpu.VMEM((512, 256), BF),
            pltpu.VMEM((256, 1024), BF),
            pltpu.VMEM((256, 256), BF),
            pltpu.VMEM((256, 128), BF),
            pltpu.VMEM((256, 128), BF),
            pltpu.VMEM((256, 512), BF),
            pltpu.SemaphoreType.DMA((5,)),
            pltpu.SemaphoreType.DMA((8,)),
            pltpu.SemaphoreType.DMA((8,)),
        ],
        compiler_params=pltpu.CompilerParams(
            collective_id=0, has_side_effects=True, vmem_limit_bytes=32 * 1024 * 1024
        ),
        name="fish_step",
    )(
        pltpu.with_memory_space_constraint(velocity, pltpu.HBM),
        pltpu.with_memory_space_constraint(marker_cell.reshape(3, 16, 128), pltpu.HBM),
        pltpu.with_memory_space_constraint(marker_frac.reshape(2, 16, 128), pltpu.HBM),
        pltpu.with_memory_space_constraint(marker_force.reshape(2, 16, 128), pltpu.HBM),
        pltpu.with_memory_space_constraint(fish_owner.reshape(6, 128), pltpu.HBM),
    )
    return out_v, out_m.reshape(2, 1, 1, 2048)


def solution(mesh):
    placed = (
        P(None, None, "gx", "gy"),
        P(None, "gx", "gy", None),
        P(None, "gx", "gy", None),
        P(None, "gx", "gy", None),
        P(),
    )
    return jax.shard_map(
        body,
        mesh=mesh,
        in_specs=placed,
        out_specs=(P(None, None, "gx", "gy"), P(None, "gx", "gy", None)),
        check_vma=False,
    )
```

```python
import functools
import math

import jax
import jax.numpy as jnp
from jax import lax
from jax.experimental import pallas as pl
from jax.experimental.pallas import tpu as pltpu
from jax.sharding import PartitionSpec as P

MARGIN = 16
FISH_MARK = 1024
COURANT = 0.25
VISCOUS = 1.5
LANES = 128
BF = jnp.bfloat16
F32 = jnp.float32

SIDES = [(1, 0), (-1, 0), (0, 1), (0, -1), (1, 1), (-1, 1), (1, -1), (-1, -1)]
UPPER = [(1, 0), (1, 1), (1, -1), (0, 1)]


def half_angle(t):
    z = t * (0.5 * math.pi)
    q = z * z
    s = 1.0 / math.factorial(13)
    for n in (11, 9, 7, 5, 3, 1):
        s = s * q + (-1.0) ** ((n - 1) // 2) / math.factorial(n)
    c = 1.0 / math.factorial(12)
    for n in (10, 8, 6, 4, 2, 0):
        c = c * q + (-1.0) ** (n // 2) / math.factorial(n)
    return s * z, c


def weights(t):
    s, c = half_angle(t)
    return (0.25 * (1.0 - s), 0.25 * (1.0 + c), 0.25 * (1.0 + s), 0.25 * (1.0 - c))


def chain(d, values, zero):
    out = jnp.where(d == 2.0, values[3], zero)
    out = jnp.where(d == 1.0, values[2], out)
    out = jnp.where(d == 0.0, values[1], out)
    return jnp.where(d == -1.0, values[0], out)


def pick(ref, source):
    rows, columns = ref.shape
    n = lax.broadcasted_iota(jnp.int32, (16, columns), 1)
    below = source(n) - lax.broadcasted_iota(jnp.int32, (16, columns), 0)
    for lo in range(0, rows, 16):
        ref[lo : lo + 16, :] = jnp.where(below == lo, 1.0, 0.0).astype(BF)


def matrices(w_in, w_out, w_place, w_adv, w_t, w_s, w_fix):
    def inner_of(n):
        p, l = n % 32, (n // 32) % 4
        up = jnp.where(p < 26, 128 * l + p + 102, 640 + 32 * l + p - 20)
        down = jnp.where(p < 6, 512 + 32 * l + p + 20, 128 * l + p - 6)
        return jnp.where(n < 128, up, down)

    def outer_of(n):
        i, c, l = n % 16, (n // 16) % 2, (n // 32) % 4
        return 256 * c + 32 * l + i + jnp.where(n < 128, 128 + 6, 10)

    def place_of(n):
        y, l, c = n % 128, (n // 128) % 4, n // 512
        at = 32 * l + 16 * c
        return jnp.where(y < 16, at + y, jnp.where(y >= 112, 128 + at + y - 112, -1))

    def fix_of(n):
        y, l = n % 128, n // 128
        return jnp.where(
            y < 3, 32 * l + 26 + y, jnp.where(y >= 125, 128 + 32 * l + y - 122, -1)
        )

    pick(w_in, inner_of)
    pick(w_out, outer_of)
    pick(w_place, place_of)
    pick(w_fix, fix_of)
    y = lax.broadcasted_iota(jnp.int32, (16, LANES), 1)
    r = lax.broadcasted_iota(jnp.int32, (16, LANES), 0)

    def one(of):
        return jnp.where(of == r, 1.0, 0.0)

    for lo in range(0, 256, 16):
        base = lo % LANES
        here, prev, after = one(y - base), one((y + 127) % 128 - base), one((y + 1) % 128 - base)
        w_adv[lo : lo + 16, 0:128] = (here - prev).astype(BF)
        w_adv[lo : lo + 16, 128:256] = (after - here).astype(BF)
        w_t[lo : lo + 16, :] = (prev + after).astype(BF)
        upper = one(jnp.where(y < 96, y + 32, y) - base)
        lower = one(jnp.where(y >= 32, y - 32, y) - base)
        w_s[lo : lo + 16, :] = (prev + after + upper + lower).astype(BF)


def pieces(v):
    high = v.astype(BF)
    return high, (v - high.astype(F32)).astype(BF)


def kernel(
    nx, ny,
    vel_h, cell_h, frac_h, force_h, owner_h,
    out_v, out_m,
    vel, cell, frac, force, owner,
    q32, left, wx_hot, wy_hot, mv, mvb, px, py, pc, rx, ry, rc,
    mt, ca, w1, sp, ws, ta, w_in, w_out, w_place, w_adv, w_t, w_s, w_fix,
    in_sem, send1, recv1, here_sem,
):
    ix = lax.axis_index("gx")
    iy = lax.axis_index("gy")

    def at(dx, dy):
        return {"gx": lax.rem(ix + dx + nx, nx), "gy": lax.rem(iy + dy + ny, ny)}

    loads = []
    for n, (src, dst) in enumerate(
        ((cell_h, cell), (frac_h, frac), (force_h, force), (owner_h, owner), (vel_h, vel))
    ):
        loads.append(pltpu.make_async_copy(src, dst, in_sem.at[n]))
        loads[-1].start()
    barrier = pltpu.get_barrier_semaphore()
    for dx, dy in UPPER:
        pl.semaphore_signal(
            barrier, inc=1, device_id=at(-dx, -dy), device_id_type=pl.DeviceIdType.MESH
        )
    matrices(w_in, w_out, w_place, w_adv, w_t, w_s, w_fix)
    for load in loads:
        load.wait()

    mine = jnp.where(owner[...] == ix * ny + iy, 1.0, 0.0)
    count = jnp.sum(jnp.sum(mine, axis=1, keepdims=True), axis=0, keepdims=True)
    slot = lax.broadcasted_iota(jnp.int32, (16, LANES), 0) * LANES + lax.broadcasted_iota(
        jnp.int32, (16, LANES), 1
    )
    alive = jnp.where(slot.astype(F32) < FISH_MARK * count, 1.0, 0.0)
    rel_x = lax.rem(cell[0] - ix * 64 + (MARGIN + nx * 64), nx * 64)
    rel_y = lax.rem(cell[1] - iy * 128 + (MARGIN + ny * 128), ny * 128) - MARGIN
    q32[0] = rel_x.astype(F32)
    q32[1] = rel_y.astype(F32)
    wx = weights(frac[0])
    wy = weights(frac[1])
    for k in range(4):
        q32[2 + k] = wx[k]
        q32[6 + k] = wy[k]
        for c in range(2):
            q32[10 + 4 * c + k] = force[c] * alive * wx[k]
        q32[18 + k] = jnp.where(cell[2] == k, 1.0, 0.0)
    q32[22] = alive

    rows16 = lax.broadcasted_iota(jnp.int32, (16, LANES), 0).astype(F32)
    zero16 = jnp.zeros((16, LANES), BF)
    strips = ((512, -26.0), (528, -10.0), (640, 122.0), (656, 138.0))

    def operands(r, _):
        lanes = slice(r * LANES, r * LANES + LANES)

        def row(n):
            return jnp.broadcast_to(q32[n, r : r + 1, :], (16, LANES))

        dx0 = rows16 - row(0)
        lw = [[row(10 + 4 * c + k).astype(BF) for k in range(4)] for c in range(2)]
        for b in range(6):
            d = (dx0 + 16.0 * b).astype(BF)
            for c in range(2):
                left[pl.ds(96 * c + 16 * b, 16), lanes] = chain(d, lw[c], zero16)
        dy0 = rows16 - row(1)
        yw = [row(6 + k).astype(BF) for k in range(4)]
        lv = [row(18 + k).astype(BF) for k in range(4)]
        for b in range(12):
            base, step = (16.0 * b, 128) if b < 8 else (strips[b - 8][1], 32)
            first_row = 16 * b if b < 8 else strips[b - 8][0]
            d = (dy0 + base).astype(BF)
            w = chain(d, yw, zero16)
            for l in range(4):
                wy_hot[pl.ds(first_row + step * l, 16), lanes] = w * lv[l]
        return 0

    for r in range(16):
        operands(r, 0)

    lane64 = lax.broadcasted_iota(jnp.int32, (64, LANES), 1)
    level64, j64 = lane64 // 32, lane64 % 32
    both = lax.dot_general(
        left[...], wy_hot[...], (((1,), (1,)), ((), ())), preferred_element_type=F32
    )
    for c in range(2):
        spread = both[96 * c : 96 * c + 96]
        mv[c] = spread
        low_part = jnp.zeros((64, LANES), F32)
        high_part = jnp.zeros((64, LANES), F32)
        for l in range(4):
            ls = slice(128 * l, 128 * l + 128)
            v = vel[l, c]
            mv[c, 16:80, ls] = spread[16:80, ls] + v
            low_part = jnp.where(
                (level64 == l) & (j64 >= 26), pltpu.roll(v, 32 * l + 26, 1), low_part
            )
            high_part = jnp.where(
                (level64 == l) & (j64 < 6), pltpu.roll(v, 32 * l + 6, 1), high_part
            )
        mv[c, 16:80, 512:640] = spread[16:80, 512:640] + low_part
        mv[c, 16:80, 640:768] = spread[16:80, 640:768] + high_part

    for c in range(2):
        mvb[96 * c : 96 * c + 96, :] = mv[c].astype(BF)
    inner = jnp.dot(mvb[...], w_in[...], preferred_element_type=F32)
    outer = jnp.dot(mvb[0:96, 512:768], w_out[0:256, :], preferred_element_type=F32)
    outer = outer + jnp.dot(mvb[96:192, 512:768], w_out[256:512, :], preferred_element_type=F32)
    filler = jnp.zeros((8, LANES), F32)
    for side in range(2):
        ls = slice(128 * side, 128 * side + 128)
        parts = [inner[0:96, ls], inner[96:192, ls], outer[:, ls]]
        py[side] = jnp.concatenate(parts, axis=0).astype(BF)
        for n in range(4):
            dx, dy = SIDES[4 + n]
            if (0 if dy == 1 else 1) == side:
                lo = 56 if dx == 1 else 0
                pc[n] = jnp.concatenate([p[lo : lo + 40] for p in parts] + [filler], axis=0).astype(BF)
    for n, lo in enumerate((56, 0)):
        px[n] = jnp.concatenate([mv[0, lo : lo + 40, :], mv[1, lo : lo + 40, :]], axis=0).astype(BF)

    pl.semaphore_wait(barrier, 4)
    for n, (dx, dy) in enumerate(UPPER):
        pl.semaphore_signal(
            here_sem.at[n], inc=1, device_id=at(dx, dy), device_id_type=pl.DeviceIdType.MESH
        )

    copies = []

    def send(n, src, dst, dx, dy):
        copy = pltpu.make_async_remote_copy(
            src_ref=src, dst_ref=dst, send_sem=send1.at[n], recv_sem=recv1.at[n],
            device_id=at(dx, dy), device_id_type=pl.DeviceIdType.MESH,
        )
        copy.start()
        copies.append(copy)

    def send_to(dx, dy):
        n = SIDES.index((dx, dy))
        if n < 2:
            send(n, px.at[n], rx.at[n], dx, dy)
        elif n < 4:
            send(n, py.at[n - 2], ry.at[n - 2], dx, dy)
        else:
            send(n, pc.at[n - 4], rc.at[n - 4], dx, dy)

    for dx, dy in UPPER:
        send_to(dx, dy)

    rows8 = lax.broadcasted_iota(jnp.int32, (8, LANES), 0).astype(F32)

    def x_hot(r, _):
        lanes = pl.ds(pl.multiple_of(r * LANES, LANES), LANES)

        def row(n):
            return jnp.broadcast_to(q32[n, pl.ds(r, 1), :], (8, LANES))

        d = rows8 - row(0)
        ww = [row(2 + k) * row(22) for k in range(4)]
        for b in range(12):
            wx_hot[pl.ds(8 * b, 8), lanes] = chain(d + 8.0 * b, ww, 0.0)
        return 0

    lax.fori_loop(0, 16, x_hot, 0)
    for ref in (mt, ca, w1):
        for c in range(2):
            for t in range(6):
                ref[c, t, 0:8, :] = jnp.zeros((8, LANES), F32)
                ref[c, t, 120:128, :] = jnp.zeros((8, LANES), F32)

    for n, (dx, dy) in enumerate(UPPER):
        pl.semaphore_wait(here_sem.at[n], 1)
        send_to(-dx, -dy)

    for copy in copies:
        copy.wait()

    corner = {}
    for n in range(4):
        dx, dy = SIDES[4 + n]
        corner[0 if dx == 1 else 1, 0 if dy == 1 else 1] = n

    def joined(mid, first, last):
        return [
            first[0:8], mid[0:32] + first[8:40], mid[32:64], mid[64:96] + last[0:32], last[32:40]
        ]

    ryf = [ry[side].astype(F32) for side in range(2)]
    rcf = [rc[n].astype(F32) for n in range(4)]
    rxf = [rx[n].astype(F32) for n in range(2)]
    from_y = [[r[96 * p : 96 * p + 96] for p in range(3)] for r in ryf]
    from_c = [[r[40 * p : 40 * p + 40] for p in range(3)] for r in rcf]
    placed = jnp.dot(
        jnp.concatenate(
            [
                jnp.concatenate([ry[side, 192:288, :] for side in range(2)], axis=1),
                jnp.concatenate([rc[corner[0, side], 80:128, :] for side in range(2)], axis=1),
                jnp.concatenate([rc[corner[1, side], 80:128, :] for side in range(2)], axis=1),
            ],
            axis=0,
        ),
        w_place[...],
        preferred_element_type=F32,
    )

    for t in range(6):
        for c in range(2):
            ls = slice(128 * t, 128 * t + 128)
            mid = mv[c, :, ls]
            first, last = (r[40 * c : 40 * c + 40, ls] for r in rxf)
            if t < 4:
                ps = slice(512 * c + 128 * t, 512 * c + 128 * t + 128)
                mid = mid + placed[0:96, ps]
                first = first + placed[96:136, ps]
                last = last + placed[144:184, ps]
            else:
                side = t - 4
                mid = mid + from_y[side][c]
                first = first + from_c[corner[0, side]][c]
                last = last + from_c[corner[1, side]][c]
            a = jnp.concatenate(joined(mid, first, last), axis=0)
            mt[c, t, 8:120, :] = a
            high, low = pieces(a)
            sp[t, 112 * c : 112 * c + 112, 0:128] = high
            sp[t, 112 * c : 112 * c + 112, 128:256] = low

    for t in range(6):
        steps = jnp.dot(sp[t], w_adv[...], preferred_element_type=F32)
        for lo in range(0, 112, 16):
            here = slice(lo + 8, lo + 24)
            a = COURANT * mt[0, t, here, :]
            b = COURANT * mt[1, t, here, :]
            ap, am = jnp.maximum(a, 0.0), jnp.minimum(a, 0.0)
            bp, bm = jnp.maximum(b, 0.0), jnp.minimum(b, 0.0)
            for c in range(2):
                q = mt[c, t, here, :]
                row = 112 * c + lo
                change = ap * (q - mt[c, t, lo + 7 : lo + 23, :]) + am * (mt[c, t, lo + 9 : lo + 25, :] - q)
                change = change + bp * steps[row : row + 16, 0:128] + bm * steps[row : row + 16, 128:256]
                value = q - change
                ca[c, t, here, :] = value
                high, low = pieces(value)
                ws[t, row : row + 16, 0:128] = high
                ws[t, row : row + 16, 128:256] = low

    scale = 1.0 / (1.0 + 6.0 * VISCOUS)

    def sweep(ref, beside, t, c, lo, row):
        here = slice(lo + 8, lo + 24)
        total = ref[c, t, lo + 7 : lo + 23, :] + ref[c, t, lo + 9 : lo + 25, :]
        total = total + beside[row : row + 16]
        if t < 4:
            total = total + (ref[c, min(t + 1, 3), here, :] + ref[c, max(t - 1, 0), here, :])
        return scale * ca[c, t, here, :] + (scale * VISCOUS) * total

    for t in range(6):
        beside = jnp.dot(ws[t], (w_t if t < 4 else w_s)[...], preferred_element_type=F32)
        for c in range(2):
            for lo in range(0, 112, 16):
                value = sweep(ca, beside, t, c, lo, 112 * c + lo)
                w1[c, t, lo + 8 : lo + 24, :] = value
                high, low = pieces(value)
                sp[t, 112 * c + lo : 112 * c + lo + 16, 0:128] = high
                sp[t, 112 * c + lo : 112 * c + lo + 16, 128:256] = low

    lane16 = lax.broadcasted_iota(jnp.int32, (16, LANES), 1)
    j16 = lane16 % 32
    keep = ((j16 >= 10) & (j16 < 26), (j16 >= 6) & (j16 < 22))
    for t in (4, 5):
        ls = slice(128 * (t - 4), 128 * (t - 4) + 128)
        beside = jnp.dot(sp[t], w_s[...], preferred_element_type=F32)
        for c in range(2):
            values = [
                sweep(w1, beside, t, c, lo, 112 * c + lo) for lo in range(0, 112, 16)
            ]
            whole = jnp.concatenate(values, axis=0)[8:104]
            high, low = pieces(whole)
            ws[0, 96 * c : 96 * c + 96, ls] = high
            ws[1, 96 * c : 96 * c + 96, ls] = low
            kept = jnp.where(keep[t - 4], whole.reshape(6, 16, LANES), 0.0).reshape(96, LANES)
            ta[96 * c : 96 * c + 96, 128 * t : 128 * t + 128] = kept.astype(BF)
    ends = jnp.dot(ws[0, 0:192, :], w_fix[...], preferred_element_type=F32)
    ends = ends + jnp.dot(ws[1, 0:192, :], w_fix[...], preferred_element_type=F32)
    lane = lax.broadcasted_iota(jnp.int32, (96, LANES), 1)
    inside = (lane >= 3) & (lane < 125)
    for t in range(4):
        ls = slice(128 * t, 128 * t + 128)
        beside = jnp.dot(sp[t], w_t[...], preferred_element_type=F32)
        for c in range(2):
            values = [
                sweep(w1, beside, t, c, lo, 112 * c + lo) for lo in range(0, 112, 16)
            ]
            whole = jnp.concatenate(values, axis=0)[8:104]
            whole = jnp.where(inside, whole, ends[96 * c : 96 * c + 96, ls])
            out_v[t, c] = whole[16:80]
            ta[96 * c : 96 * c + 96, ls] = whole.astype(BF)

    for r in range(4):
        lanes = slice(512 * r, 512 * r + 512)
        both = jnp.dot(ta[...], wy_hot[:, lanes], preferred_element_type=F32)
        for c in range(2):
            part = both[96 * c : 96 * c + 96]
            summed = jnp.sum(part * wx_hot[:, lanes], axis=0, keepdims=True)
            for i in range(4):
                out_m[c, 4 * r + i : 4 * r + i + 1, :] = summed[:, LANES * i : LANES * i + LANES]


def body(velocity, marker_cell, marker_frac, marker_force, fish_owner):
    nx = lax.axis_size("gx")
    ny = lax.axis_size("gy")
    vm = pl.BlockSpec(memory_space=pltpu.VMEM)
    out_v, out_m = pl.pallas_call(
        functools.partial(kernel, nx, ny),
        out_shape=(
            jax.ShapeDtypeStruct((4, 2, 64, 128), F32),
            jax.ShapeDtypeStruct((2, 16, 128), F32),
        ),
        in_specs=[pl.BlockSpec(memory_space=pltpu.HBM)] * 5,
        out_specs=(vm, vm),
        scratch_shapes=[
            pltpu.VMEM((4, 2, 64, 128), F32),
            pltpu.VMEM((3, 16, 128), jnp.int32),
            pltpu.VMEM((2, 16, 128), F32),
            pltpu.VMEM((2, 16, 128), F32),
            pltpu.VMEM((6, 128), jnp.int32),
            pltpu.VMEM((23, 16, 128), F32),
            pltpu.VMEM((192, 2048), BF),
            pltpu.VMEM((96, 2048), F32),
            pltpu.VMEM((768, 2048), BF),
            pltpu.VMEM((2, 96, 768), F32),
            pltpu.VMEM((192, 768), BF),
            pltpu.VMEM((2, 80, 768), BF),
            pltpu.VMEM((2, 288, 128), BF),
            pltpu.VMEM((4, 128, 128), BF),
            pltpu.VMEM((2, 80, 768), BF),
            pltpu.VMEM((2, 288, 128), BF),
            pltpu.VMEM((4, 128, 128), BF),
            pltpu.VMEM((2, 6, 128, 128), F32),
            pltpu.VMEM((2, 6, 128, 128), F32),
            pltpu.VMEM((2, 6, 128, 128), F32),
            pltpu.VMEM((6, 224, 256), BF),
            pltpu.VMEM((6, 224, 256), BF),
            pltpu.VMEM((192, 768), BF),
            pltpu.VMEM((768, 256), BF),
            pltpu.VMEM((512, 256), BF),
            pltpu.VMEM((256, 1024), BF),
            pltpu.VMEM((256, 256), BF),
            pltpu.VMEM((256, 128), BF),
            pltpu.VMEM((256, 128), BF),
            pltpu.VMEM((256, 512), BF),
            pltpu.SemaphoreType.DMA((5,)),
            pltpu.SemaphoreType.DMA((8,)),
            pltpu.SemaphoreType.DMA((8,)),
            pltpu.SemaphoreType.REGULAR((4,)),
        ],
        compiler_params=pltpu.CompilerParams(
            collective_id=0, has_side_effects=True, vmem_limit_bytes=32 * 1024 * 1024
        ),
        name="fish_step",
    )(
        pltpu.with_memory_space_constraint(velocity, pltpu.HBM),
        pltpu.with_memory_space_constraint(marker_cell.reshape(3, 16, 128), pltpu.HBM),
        pltpu.with_memory_space_constraint(marker_frac.reshape(2, 16, 128), pltpu.HBM),
        pltpu.with_memory_space_constraint(marker_force.reshape(2, 16, 128), pltpu.HBM),
        pltpu.with_memory_space_constraint(fish_owner.reshape(6, 128), pltpu.HBM),
    )
    return out_v, out_m.reshape(2, 1, 1, 2048)


def solution(mesh):
    placed = (
        P(None, None, "gx", "gy"),
        P(None, "gx", "gy", None),
        P(None, "gx", "gy", None),
        P(None, "gx", "gy", None),
        P(),
    )
    return jax.shard_map(
        body,
        mesh=mesh,
        in_specs=placed,
        out_specs=(P(None, None, "gx", "gy"), P(None, "gx", "gy", None)),
        check_vma=False,
    )
```

```python
import functools
import math

import jax
import jax.numpy as jnp
from jax import lax
from jax.experimental import pallas as pl
from jax.experimental.pallas import tpu as pltpu
from jax.sharding import PartitionSpec as P

MARGIN = 16
FISH_MARK = 1024
COURANT = 0.25
VISCOUS = 1.5
LANES = 128
BF = jnp.bfloat16
F32 = jnp.float32

SIDES = [(1, 0), (-1, 0), (0, 1), (0, -1), (1, 1), (-1, 1), (1, -1), (-1, -1)]
UPPER = [(0, 1), (1, 0), (1, 1), (1, -1)]


def half_angle(t):
    z = t * (0.5 * math.pi)
    q = z * z
    s = 1.0 / math.factorial(13)
    for n in (11, 9, 7, 5, 3, 1):
        s = s * q + (-1.0) ** ((n - 1) // 2) / math.factorial(n)
    c = 1.0 / math.factorial(12)
    for n in (10, 8, 6, 4, 2, 0):
        c = c * q + (-1.0) ** (n // 2) / math.factorial(n)
    return s * z, c


def weights(t):
    s, c = half_angle(t)
    return (0.25 * (1.0 - s), 0.25 * (1.0 + c), 0.25 * (1.0 + s), 0.25 * (1.0 - c))


def chain(d, values, zero):
    out = jnp.where(d == 2.0, values[3], zero)
    out = jnp.where(d == 1.0, values[2], out)
    out = jnp.where(d == 0.0, values[1], out)
    return jnp.where(d == -1.0, values[0], out)


def pick(ref, source):
    rows, columns = ref.shape
    n = lax.broadcasted_iota(jnp.int32, (16, columns), 1)
    below = source(n) - lax.broadcasted_iota(jnp.int32, (16, columns), 0)
    for lo in range(0, rows, 16):
        ref[lo : lo + 16, :] = jnp.where(below == lo, 1.0, 0.0).astype(BF)


def matrices(w_in, w_out, w_place, w_adv, w_t, w_s, w_fix):
    def inner_of(n):
        p, l = n % 32, (n // 32) % 4
        up = jnp.where(p < 26, 128 * l + p + 102, 640 + 32 * l + p - 20)
        down = jnp.where(p < 6, 512 + 32 * l + p + 20, 128 * l + p - 6)
        return jnp.where(n < 128, up, down)

    def outer_of(n):
        i, c, l = n % 16, (n // 16) % 2, (n // 32) % 4
        return 256 * c + 32 * l + i + jnp.where(n < 128, 128 + 6, 10)

    def place_of(n):
        y, l, c = n % 128, (n // 128) % 4, n // 512
        at = 32 * l + 16 * c
        return jnp.where(y < 16, at + y, jnp.where(y >= 112, 128 + at + y - 112, -1))

    def fix_of(n):
        y, l = n % 128, n // 128
        return jnp.where(
            y < 3, 32 * l + 26 + y, jnp.where(y >= 125, 128 + 32 * l + y - 122, -1)
        )

    pick(w_in, inner_of)
    pick(w_out, outer_of)
    pick(w_place, place_of)
    pick(w_fix, fix_of)
    y = lax.broadcasted_iota(jnp.int32, (16, LANES), 1)
    r = lax.broadcasted_iota(jnp.int32, (16, LANES), 0)

    def one(of):
        return jnp.where(of == r, 1.0, 0.0)

    for lo in range(0, 256, 16):
        base = lo % LANES
        here, prev, after = one(y - base), one((y + 127) % 128 - base), one((y + 1) % 128 - base)
        w_adv[lo : lo + 16, 0:128] = (here - prev).astype(BF)
        w_adv[lo : lo + 16, 128:256] = (after - here).astype(BF)
        w_t[lo : lo + 16, :] = (prev + after).astype(BF)
        upper = one(jnp.where(y < 96, y + 32, y) - base)
        lower = one(jnp.where(y >= 32, y - 32, y) - base)
        w_s[lo : lo + 16, :] = (prev + after + upper + lower).astype(BF)


def pieces(v):
    high = v.astype(BF)
    return high, (v - high.astype(F32)).astype(BF)


def kernel(
    nx, ny,
    vel_h, cell_h, frac_h, force_h, owner_h,
    out_v, ta, wy_hot, wx_hot,
    vel, cell, frac, force, owner,
    q32, left, mv, mvb, px, py, pc, rx, ry, rc,
    mt, ca, w1, sp, ws, ends_in, w_in, w_out, w_place, w_adv, w_t, w_s, w_fix,
    in_sem, send1, recv1, here_sem,
):
    ix = lax.axis_index("gx")
    iy = lax.axis_index("gy")

    def at(dx, dy):
        return {"gx": lax.rem(ix + dx + nx, nx), "gy": lax.rem(iy + dy + ny, ny)}

    loads = []
    for n, (src, dst) in enumerate(
        ((cell_h, cell), (frac_h, frac), (force_h, force), (owner_h, owner), (vel_h, vel))
    ):
        loads.append(pltpu.make_async_copy(src, dst, in_sem.at[n]))
        loads[-1].start()
    barrier = pltpu.get_barrier_semaphore()
    for dx, dy in UPPER:
        pl.semaphore_signal(
            barrier, inc=1, device_id=at(-dx, -dy), device_id_type=pl.DeviceIdType.MESH
        )
    matrices(w_in, w_out, w_place, w_adv, w_t, w_s, w_fix)
    for load in loads:
        load.wait()

    mine = jnp.where(owner[...] == ix * ny + iy, 1.0, 0.0)
    count = jnp.sum(jnp.sum(mine, axis=1, keepdims=True), axis=0, keepdims=True)
    slot = lax.broadcasted_iota(jnp.int32, (16, LANES), 0) * LANES + lax.broadcasted_iota(
        jnp.int32, (16, LANES), 1
    )
    alive = jnp.where(slot.astype(F32) < FISH_MARK * count, 1.0, 0.0)
    rel_x = lax.rem(cell[0] - ix * 64 + (MARGIN + nx * 64), nx * 64)
    rel_y = lax.rem(cell[1] - iy * 128 + (MARGIN + ny * 128), ny * 128) - MARGIN
    q32[0] = rel_x.astype(F32)
    q32[1] = rel_y.astype(F32)
    wx = weights(frac[0])
    wy = weights(frac[1])
    for k in range(4):
        q32[2 + k] = wx[k]
        q32[6 + k] = wy[k]
        for c in range(2):
            q32[10 + 4 * c + k] = force[c] * alive * wx[k]
        q32[18 + k] = jnp.where(cell[2] == k, 1.0, 0.0)
    q32[22] = alive

    rows16 = lax.broadcasted_iota(jnp.int32, (16, LANES), 0).astype(F32)
    zero16 = jnp.zeros((16, LANES), BF)
    strips = ((512, -26.0), (528, -10.0), (640, 122.0), (656, 138.0))

    def operands(r, _):
        lanes = slice(r * LANES, r * LANES + LANES)

        def row(n):
            return jnp.broadcast_to(q32[n, r : r + 1, :], (16, LANES))

        dx0 = rows16 - row(0)
        lw = [[row(10 + 4 * c + k).astype(BF) for k in range(4)] for c in range(2)]
        for b in range(6):
            d = (dx0 + 16.0 * b).astype(BF)
            for c in range(2):
                left[pl.ds(96 * c + 16 * b, 16), lanes] = chain(d, lw[c], zero16)
        dy0 = rows16 - row(1)
        yw = [row(6 + k).astype(BF) for k in range(4)]
        lv = [row(18 + k).astype(BF) for k in range(4)]
        for b in range(12):
            base, step = (16.0 * b, 128) if b < 8 else (strips[b - 8][1], 32)
            first_row = 16 * b if b < 8 else strips[b - 8][0]
            d = (dy0 + base).astype(BF)
            w = chain(d, yw, zero16)
            for l in range(4):
                wy_hot[pl.ds(first_row + step * l, 16), lanes] = w * lv[l]
        return 0

    for r in range(16):
        operands(r, 0)

    lane64 = lax.broadcasted_iota(jnp.int32, (64, LANES), 1)
    level64, j64 = lane64 // 32, lane64 % 32
    both = lax.dot_general(
        left[...], wy_hot[...], (((1,), (1,)), ((), ())), preferred_element_type=F32
    )
    for c in range(2):
        spread = both[96 * c : 96 * c + 96]
        mv[c] = spread
        low_part = jnp.zeros((64, LANES), F32)
        high_part = jnp.zeros((64, LANES), F32)
        for l in range(4):
            ls = slice(128 * l, 128 * l + 128)
            v = vel[l, c]
            mv[c, 16:80, ls] = spread[16:80, ls] + v
            low_part = jnp.where(
                (level64 == l) & (j64 >= 26), pltpu.roll(v, 32 * l + 26, 1), low_part
            )
            high_part = jnp.where(
                (level64 == l) & (j64 < 6), pltpu.roll(v, 32 * l + 6, 1), high_part
            )
        mv[c, 16:80, 512:640] = spread[16:80, 512:640] + low_part
        mv[c, 16:80, 640:768] = spread[16:80, 640:768] + high_part

    for c in range(2):
        mvb[96 * c : 96 * c + 96, :] = mv[c].astype(BF)
    inner = jnp.dot(mvb[...], w_in[...], preferred_element_type=F32)
    outer = jnp.dot(mvb[0:96, 512:768], w_out[0:256, :], preferred_element_type=F32)
    outer = outer + jnp.dot(mvb[96:192, 512:768], w_out[256:512, :], preferred_element_type=F32)
    filler = jnp.zeros((8, LANES), F32)
    for side in range(2):
        ls = slice(128 * side, 128 * side + 128)
        parts = [inner[0:96, ls], inner[96:192, ls], outer[:, ls]]
        py[side] = jnp.concatenate(parts, axis=0).astype(BF)
        for n in range(4):
            dx, dy = SIDES[4 + n]
            if (0 if dy == 1 else 1) == side:
                lo = 56 if dx == 1 else 0
                pc[n] = jnp.concatenate([p[lo : lo + 40] for p in parts] + [filler], axis=0).astype(BF)
    for n, lo in enumerate((56, 0)):
        px[n] = jnp.concatenate([mv[0, lo : lo + 40, :], mv[1, lo : lo + 40, :]], axis=0).astype(BF)

    pl.semaphore_wait(barrier, 4)
    for n, (dx, dy) in enumerate(UPPER):
        pl.semaphore_signal(
            here_sem.at[n], inc=1, device_id=at(dx, dy), device_id_type=pl.DeviceIdType.MESH
        )

    copies = []

    def send(n, src, dst, dx, dy):
        copy = pltpu.make_async_remote_copy(
            src_ref=src, dst_ref=dst, send_sem=send1.at[n], recv_sem=recv1.at[n],
            device_id=at(dx, dy), device_id_type=pl.DeviceIdType.MESH,
        )
        copy.start()
        copies.append(copy)

    def send_to(dx, dy):
        n = SIDES.index((dx, dy))
        if n < 2:
            send(n, px.at[n], rx.at[n], dx, dy)
        elif n < 4:
            send(n, py.at[n - 2], ry.at[n - 2], dx, dy)
        else:
            send(n, pc.at[n - 4], rc.at[n - 4], dx, dy)

    for dx, dy in UPPER[1:] + UPPER[:1]:
        send_to(dx, dy)

    for n, (dx, dy) in enumerate(UPPER):
        pl.semaphore_wait(here_sem.at[n], 1)
        send_to(-dx, -dy)

    rows8 = lax.broadcasted_iota(jnp.int32, (8, LANES), 0).astype(F32)

    def x_hot(r, _):
        lanes = pl.ds(pl.multiple_of(r * LANES, LANES), LANES)

        def row(n):
            return jnp.broadcast_to(q32[n, pl.ds(r, 1), :], (8, LANES))

        d = rows8 - row(0)
        ww = [row(2 + k) * row(22) for k in range(4)]
        for b in range(12):
            wx_hot[pl.ds(8 * b, 8), lanes] = chain(d + 8.0 * b, ww, 0.0)
        return 0

    lax.fori_loop(0, 16, x_hot, 0)
    for ref in (mt, ca, w1):
        for c in range(2):
            for t in range(6):
                ref[c, t, 0:8, :] = jnp.zeros((8, LANES), F32)
                ref[c, t, 120:128, :] = jnp.zeros((8, LANES), F32)

    for copy in copies:
        copy.wait()

    corner = {}
    for n in range(4):
        dx, dy = SIDES[4 + n]
        corner[0 if dx == 1 else 1, 0 if dy == 1 else 1] = n

    def joined(mid, first, last):
        return [
            first[0:8], mid[0:32] + first[8:40], mid[32:64], mid[64:96] + last[0:32], last[32:40]
        ]

    ryf = [ry[side].astype(F32) for side in range(2)]
    rcf = [rc[n].astype(F32) for n in range(4)]
    rxf = [rx[n].astype(F32) for n in range(2)]
    from_y = [[r[96 * p : 96 * p + 96] for p in range(3)] for r in ryf]
    from_c = [[r[40 * p : 40 * p + 40] for p in range(3)] for r in rcf]
    placed = jnp.dot(
        jnp.concatenate(
            [
                jnp.concatenate([ry[side, 192:288, :] for side in range(2)], axis=1),
                jnp.concatenate([rc[corner[0, side], 80:128, :] for side in range(2)], axis=1),
                jnp.concatenate([rc[corner[1, side], 80:128, :] for side in range(2)], axis=1),
            ],
            axis=0,
        ),
        w_place[...],
        preferred_element_type=F32,
    )

    def assemble(t):
        for c in range(2):
            ls = slice(128 * t, 128 * t + 128)
            mid = mv[c, :, ls]
            first, last = (r[40 * c : 40 * c + 40, ls] for r in rxf)
            if t < 4:
                ps = slice(512 * c + 128 * t, 512 * c + 128 * t + 128)
                mid = mid + placed[0:96, ps]
                first = first + placed[96:136, ps]
                last = last + placed[144:184, ps]
            else:
                side = t - 4
                mid = mid + from_y[side][c]
                first = first + from_c[corner[0, side]][c]
                last = last + from_c[corner[1, side]][c]
            a = jnp.concatenate(joined(mid, first, last), axis=0)
            mt[c, t, 8:120, :] = a
            high, low = pieces(a)
            sp[t, 112 * c : 112 * c + 112, 0:128] = high
            sp[t, 112 * c : 112 * c + 112, 128:256] = low

    def advect(t):
        steps = jnp.dot(sp[t], w_adv[...], preferred_element_type=F32)
        for lo in range(0, 112, 16):
            here = slice(lo + 8, lo + 24)
            a = COURANT * mt[0, t, here, :]
            b = COURANT * mt[1, t, here, :]
            forth, right = a > 0.0, b > 0.0
            for c in range(2):
                q = mt[c, t, here, :]
                row = 112 * c + lo
                step_x = jnp.where(
                    forth, q - mt[c, t, lo + 7 : lo + 23, :], mt[c, t, lo + 9 : lo + 25, :] - q
                )
                step_y = jnp.where(
                    right, steps[row : row + 16, 0:128], steps[row : row + 16, 128:256]
                )
                value = q - (a * step_x + b * step_y)
                ca[c, t, here, :] = value
                high, low = pieces(value)
                ws[t, row : row + 16, 0:128] = high
                ws[t, row : row + 16, 128:256] = low

    scale = 1.0 / (1.0 + 6.0 * VISCOUS)

    def sweep(ref, beside, t, c, lo, row):
        here = slice(lo + 8, lo + 24)
        total = ref[c, t, lo + 7 : lo + 23, :] + ref[c, t, lo + 9 : lo + 25, :]
        total = total + beside[row : row + 16]
        if t < 4:
            total = total + (ref[c, min(t + 1, 3), here, :] + ref[c, max(t - 1, 0), here, :])
        return scale * ca[c, t, here, :] + (scale * VISCOUS) * total

    def first_sweep(t):
        beside = jnp.dot(ws[t], (w_t if t < 4 else w_s)[...], preferred_element_type=F32)
        for c in range(2):
            for lo in range(0, 112, 16):
                value = sweep(ca, beside, t, c, lo, 112 * c + lo)
                w1[c, t, lo + 8 : lo + 24, :] = value
                high, low = pieces(value)
                sp[t, 112 * c + lo : 112 * c + lo + 16, 0:128] = high
                sp[t, 112 * c + lo : 112 * c + lo + 16, 128:256] = low

    def second_sweep(t, c, beside):
        values = [sweep(w1, beside, t, c, lo, 112 * c + lo) for lo in range(0, 112, 16)]
        return jnp.concatenate(values, axis=0)[8:104]

    lane16 = lax.broadcasted_iota(jnp.int32, (16, LANES), 1)
    j16 = lane16 % 32
    keep = ((j16 >= 10) & (j16 < 26), (j16 >= 6) & (j16 < 22))
    assemble(4)
    assemble(5)
    advect(4)
    advect(5)
    assemble(0)
    first_sweep(4)
    first_sweep(5)
    for t in (1, 2, 3):
        assemble(t)
    for t in (4, 5):
        ls = slice(128 * (t - 4), 128 * (t - 4) + 128)
        beside = jnp.dot(sp[t], w_s[...], preferred_element_type=F32)
        for c in range(2):
            whole = second_sweep(t, c, beside)
            high, low = pieces(whole)
            ends_in[0, 96 * c : 96 * c + 96, ls] = high
            ends_in[1, 96 * c : 96 * c + 96, ls] = low
            kept = jnp.where(keep[t - 4], whole.reshape(6, 16, LANES), 0.0).reshape(96, LANES)
            ta[96 * c : 96 * c + 96, 128 * t : 128 * t + 128] = kept.astype(BF)
    for t in range(4):
        advect(t)
    ends = jnp.dot(ends_in[0], w_fix[...], preferred_element_type=F32)
    ends = ends + jnp.dot(ends_in[1], w_fix[...], preferred_element_type=F32)
    for t in range(4):
        first_sweep(t)
    lane = lax.broadcasted_iota(jnp.int32, (96, LANES), 1)
    inside = (lane >= 3) & (lane < 125)
    for t in range(4):
        ls = slice(128 * t, 128 * t + 128)
        beside = jnp.dot(sp[t], w_t[...], preferred_element_type=F32)
        for c in range(2):
            whole = second_sweep(t, c, beside)
            whole = jnp.where(inside, whole, ends[96 * c : 96 * c + 96, ls])
            out_v[t, c] = whole[16:80]
            ta[96 * c : 96 * c + 96, ls] = whole.astype(BF)


def sampling(v, ta, wy_hot, wx_hot, out_v, out_m, out_sem):
    copy = pltpu.make_async_copy(v, out_v, out_sem)
    copy.start()
    for r in range(4):
        lanes = slice(512 * r, 512 * r + 512)
        both = jnp.dot(ta[...], wy_hot[:, lanes], preferred_element_type=F32)
        for c in range(2):
            part = both[96 * c : 96 * c + 96]
            summed = jnp.sum(part * wx_hot[:, lanes], axis=0, keepdims=True)
            for i in range(4):
                out_m[c, 4 * r + i : 4 * r + i + 1, :] = summed[:, LANES * i : LANES * i + LANES]
    copy.wait()


def body(velocity, marker_cell, marker_frac, marker_force, fish_owner):
    nx = lax.axis_size("gx")
    ny = lax.axis_size("gy")
    vm = pl.BlockSpec(memory_space=pltpu.VMEM)
    v, ta, wy_hot, wx_hot = pl.pallas_call(
        functools.partial(kernel, nx, ny),
        out_shape=(
            jax.ShapeDtypeStruct((4, 2, 64, 128), F32),
            jax.ShapeDtypeStruct((192, 768), BF),
            jax.ShapeDtypeStruct((768, 2048), BF),
            jax.ShapeDtypeStruct((96, 2048), F32),
        ),
        in_specs=[pl.BlockSpec(memory_space=pltpu.HBM)] * 5,
        out_specs=(vm, vm, vm, vm),
        scratch_shapes=[
            pltpu.VMEM((4, 2, 64, 128), F32),
            pltpu.VMEM((3, 16, 128), jnp.int32),
            pltpu.VMEM((2, 16, 128), F32),
            pltpu.VMEM((2, 16, 128), F32),
            pltpu.VMEM((6, 128), jnp.int32),
            pltpu.VMEM((23, 16, 128), F32),
            pltpu.VMEM((192, 2048), BF),
            pltpu.VMEM((2, 96, 768), F32),
            pltpu.VMEM((192, 768), BF),
            pltpu.VMEM((2, 80, 768), BF),
            pltpu.VMEM((2, 288, 128), BF),
            pltpu.VMEM((4, 128, 128), BF),
            pltpu.VMEM((2, 80, 768), BF),
            pltpu.VMEM((2, 288, 128), BF),
            pltpu.VMEM((4, 128, 128), BF),
            pltpu.VMEM((2, 6, 128, 128), F32),
            pltpu.VMEM((2, 6, 128, 128), F32),
            pltpu.VMEM((2, 6, 128, 128), F32),
            pltpu.VMEM((6, 224, 256), BF),
            pltpu.VMEM((6, 224, 256), BF),
            pltpu.VMEM((2, 192, 256), BF),
            pltpu.VMEM((768, 256), BF),
            pltpu.VMEM((512, 256), BF),
            pltpu.VMEM((256, 1024), BF),
            pltpu.VMEM((256, 256), BF),
            pltpu.VMEM((256, 128), BF),
            pltpu.VMEM((256, 128), BF),
            pltpu.VMEM((256, 512), BF),
            pltpu.SemaphoreType.DMA((5,)),
            pltpu.SemaphoreType.DMA((8,)),
            pltpu.SemaphoreType.DMA((8,)),
            pltpu.SemaphoreType.REGULAR((4,)),
        ],
        compiler_params=pltpu.CompilerParams(
            collective_id=0, has_side_effects=True, vmem_limit_bytes=24 * 1024 * 1024
        ),
        name="fish_step",
    )(
        pltpu.with_memory_space_constraint(velocity, pltpu.HBM),
        pltpu.with_memory_space_constraint(marker_cell.reshape(3, 16, 128), pltpu.HBM),
        pltpu.with_memory_space_constraint(marker_frac.reshape(2, 16, 128), pltpu.HBM),
        pltpu.with_memory_space_constraint(marker_force.reshape(2, 16, 128), pltpu.HBM),
        pltpu.with_memory_space_constraint(fish_owner.reshape(6, 128), pltpu.HBM),
    )
    out_v, out_m = pl.pallas_call(
        sampling,
        out_shape=(
            jax.ShapeDtypeStruct((4, 2, 64, 128), F32),
            jax.ShapeDtypeStruct((2, 16, 128), F32),
        ),
        in_specs=[vm] * 4,
        out_specs=(pl.BlockSpec(memory_space=pltpu.HBM), vm),
        scratch_shapes=[pltpu.SemaphoreType.DMA],
        compiler_params=pltpu.CompilerParams(vmem_limit_bytes=8 * 1024 * 1024),
        name="fish_sample",
    )(v, ta, wy_hot, wx_hot)
    return out_v, out_m.reshape(2, 1, 1, 2048)


def solution(mesh):
    placed = (
        P(None, None, "gx", "gy"),
        P(None, "gx", "gy", None),
        P(None, "gx", "gy", None),
        P(None, "gx", "gy", None),
        P(),
    )
    return jax.shard_map(
        body,
        mesh=mesh,
        in_specs=placed,
        out_specs=(P(None, None, "gx", "gy"), P(None, "gx", "gy", None)),
        check_vma=False,
    )
```

```python
import functools
import math

import jax
import jax.numpy as jnp
from jax import lax
from jax.experimental import pallas as pl
from jax.experimental.pallas import tpu as pltpu
from jax.sharding import PartitionSpec as P

MARGIN = 16
FISH_MARK = 1024
COURANT = 0.25
VISCOUS = 1.5
LANES = 128
BF = jnp.bfloat16
F32 = jnp.float32

SIDES = [(1, 0), (-1, 0), (0, 1), (0, -1), (1, 1), (-1, 1), (1, -1), (-1, -1)]
UPPER = [(0, 1), (1, 1), (1, -1), (1, 0)]


def half_angle(t):
    z = t * (0.5 * math.pi)
    q = z * z
    s = 1.0 / math.factorial(13)
    for n in (11, 9, 7, 5, 3, 1):
        s = s * q + (-1.0) ** ((n - 1) // 2) / math.factorial(n)
    c = 1.0 / math.factorial(12)
    for n in (10, 8, 6, 4, 2, 0):
        c = c * q + (-1.0) ** (n // 2) / math.factorial(n)
    return s * z, c


def weights(t):
    s, c = half_angle(t)
    return (0.25 * (1.0 - s), 0.25 * (1.0 + c), 0.25 * (1.0 + s), 0.25 * (1.0 - c))


def chain(d, values, zero):
    out = jnp.where(d == 2.0, values[3], zero)
    out = jnp.where(d == 1.0, values[2], out)
    out = jnp.where(d == 0.0, values[1], out)
    return jnp.where(d == -1.0, values[0], out)


def pick(ref, source):
    rows, columns = ref.shape
    n = lax.broadcasted_iota(jnp.int32, (16, columns), 1)
    below = source(n) - lax.broadcasted_iota(jnp.int32, (16, columns), 0)
    for lo in range(0, rows, 16):
        ref[lo : lo + 16, :] = jnp.where(below == lo, 1.0, 0.0).astype(BF)


def matrices(w_in, w_out, w_place, w_adv, w_t, w_s, w_fix):
    def inner_of(n):
        p, l = n % 32, (n // 32) % 4
        up = jnp.where(p < 26, 128 * l + p + 102, 640 + 32 * l + p - 20)
        down = jnp.where(p < 6, 512 + 32 * l + p + 20, 128 * l + p - 6)
        return jnp.where(n < 128, up, down)

    def outer_of(n):
        i, c, l = n % 16, (n // 16) % 2, (n // 32) % 4
        return 256 * c + 32 * l + i + jnp.where(n < 128, 128 + 6, 10)

    def place_of(n):
        y, l, c = n % 128, (n // 128) % 4, n // 512
        at = 32 * l + 16 * c
        return jnp.where(y < 16, at + y, jnp.where(y >= 112, 128 + at + y - 112, -1))

    def fix_of(n):
        y, l = n % 128, n // 128
        return jnp.where(
            y < 3, 32 * l + 26 + y, jnp.where(y >= 125, 128 + 32 * l + y - 122, -1)
        )

    pick(w_in, inner_of)
    pick(w_out, outer_of)
    pick(w_place, place_of)
    pick(w_fix, fix_of)
    y = lax.broadcasted_iota(jnp.int32, (16, LANES), 1)
    r = lax.broadcasted_iota(jnp.int32, (16, LANES), 0)

    def one(of):
        return jnp.where(of == r, 1.0, 0.0)

    for lo in range(0, 256, 16):
        base = lo % LANES
        here, prev, after = one(y - base), one((y + 127) % 128 - base), one((y + 1) % 128 - base)
        w_adv[lo : lo + 16, 0:128] = (here - prev).astype(BF)
        w_adv[lo : lo + 16, 128:256] = (after - here).astype(BF)
        w_t[lo : lo + 16, :] = (prev + after).astype(BF)
        upper = one(jnp.where(y < 96, y + 32, y) - base)
        lower = one(jnp.where(y >= 32, y - 32, y) - base)
        w_s[lo : lo + 16, :] = (prev + after + upper + lower).astype(BF)


def pieces(v):
    high = v.astype(BF)
    return high, (v - high.astype(F32)).astype(BF)


def kernel(
    nx, ny,
    vel_h, cell_h, frac_h, force_h, owner_h,
    out_v, ta, wy_hot, wx_hot,
    vel, cell, frac, force, owner,
    q32, left, mv, mvb, px, py, pc, rx, ry, rc,
    mt, ca, w1, sp, ws, ends_in, w_in, w_out, w_place, w_adv, w_t, w_s, w_fix,
    in_sem, send1, recv1, here_sem,
):
    ix = lax.axis_index("gx")
    iy = lax.axis_index("gy")

    def at(dx, dy):
        return {"gx": lax.rem(ix + dx + nx, nx), "gy": lax.rem(iy + dy + ny, ny)}

    loads = []
    for n, (src, dst) in enumerate(
        ((cell_h, cell), (frac_h, frac), (force_h, force), (owner_h, owner), (vel_h, vel))
    ):
        loads.append(pltpu.make_async_copy(src, dst, in_sem.at[n]))
        loads[-1].start()
    barrier = pltpu.get_barrier_semaphore()
    for dx, dy in UPPER:
        pl.semaphore_signal(
            barrier, inc=1, device_id=at(-dx, -dy), device_id_type=pl.DeviceIdType.MESH
        )
    matrices(w_in, w_out, w_place, w_adv, w_t, w_s, w_fix)
    for load in loads:
        load.wait()

    mine = jnp.where(owner[...] == ix * ny + iy, 1.0, 0.0)
    count = jnp.sum(jnp.sum(mine, axis=1, keepdims=True), axis=0, keepdims=True)
    slot = lax.broadcasted_iota(jnp.int32, (16, LANES), 0) * LANES + lax.broadcasted_iota(
        jnp.int32, (16, LANES), 1
    )
    alive = jnp.where(slot.astype(F32) < FISH_MARK * count, 1.0, 0.0)
    rel_x = lax.rem(cell[0] - ix * 64 + (MARGIN + nx * 64), nx * 64)
    rel_y = lax.rem(cell[1] - iy * 128 + (MARGIN + ny * 128), ny * 128) - MARGIN
    q32[0] = rel_x.astype(F32)
    q32[1] = rel_y.astype(F32)
    wx = weights(frac[0])
    wy = weights(frac[1])
    for k in range(4):
        q32[2 + k] = wx[k]
        q32[6 + k] = wy[k]
        for c in range(2):
            q32[10 + 4 * c + k] = force[c] * alive * wx[k]
        q32[18 + k] = jnp.where(cell[2] == k, 1.0, 0.0)
    q32[22] = alive

    rows16 = lax.broadcasted_iota(jnp.int32, (16, LANES), 0).astype(F32)
    zero16 = jnp.zeros((16, LANES), BF)
    strips = ((512, -26.0), (528, -10.0), (640, 122.0), (656, 138.0))

    def operands(r, _):
        lanes = slice(r * LANES, r * LANES + LANES)

        def row(n):
            return jnp.broadcast_to(q32[n, r : r + 1, :], (16, LANES))

        dx0 = rows16 - row(0)
        lw = [[row(10 + 4 * c + k).astype(BF) for k in range(4)] for c in range(2)]
        for b in range(6):
            d = (dx0 + 16.0 * b).astype(BF)
            for c in range(2):
                left[pl.ds(96 * c + 16 * b, 16), lanes] = chain(d, lw[c], zero16)
        dy0 = rows16 - row(1)
        yw = [row(6 + k).astype(BF) for k in range(4)]
        lv = [row(18 + k).astype(BF) for k in range(4)]
        for b in range(12):
            base, step = (16.0 * b, 128) if b < 8 else (strips[b - 8][1], 32)
            first_row = 16 * b if b < 8 else strips[b - 8][0]
            d = (dy0 + base).astype(BF)
            w = chain(d, yw, zero16)
            for l in range(4):
                wy_hot[pl.ds(first_row + step * l, 16), lanes] = w * lv[l]
        return 0

    for r in range(16):
        operands(r, 0)

    lane64 = lax.broadcasted_iota(jnp.int32, (64, LANES), 1)
    level64, j64 = lane64 // 32, lane64 % 32
    both = lax.dot_general(
        left[...], wy_hot[...], (((1,), (1,)), ((), ())), preferred_element_type=F32
    )
    for c in range(2):
        spread = both[96 * c : 96 * c + 96]
        mv[c] = spread
        low_part = jnp.zeros((64, LANES), F32)
        high_part = jnp.zeros((64, LANES), F32)
        for l in range(4):
            ls = slice(128 * l, 128 * l + 128)
            v = vel[l, c]
            mv[c, 16:80, ls] = spread[16:80, ls] + v
            low_part = jnp.where(
                (level64 == l) & (j64 >= 26), pltpu.roll(v, 32 * l + 26, 1), low_part
            )
            high_part = jnp.where(
                (level64 == l) & (j64 < 6), pltpu.roll(v, 32 * l + 6, 1), high_part
            )
        mv[c, 16:80, 512:640] = spread[16:80, 512:640] + low_part
        mv[c, 16:80, 640:768] = spread[16:80, 640:768] + high_part

    for c in range(2):
        mvb[96 * c : 96 * c + 96, :] = mv[c].astype(BF)
    inner = jnp.dot(mvb[...], w_in[...], preferred_element_type=F32)
    outer = jnp.dot(mvb[0:96, 512:768], w_out[0:256, :], preferred_element_type=F32)
    outer = outer + jnp.dot(mvb[96:192, 512:768], w_out[256:512, :], preferred_element_type=F32)
    filler = jnp.zeros((8, LANES), F32)
    for side in range(2):
        ls = slice(128 * side, 128 * side + 128)
        parts = [inner[0:96, ls], inner[96:192, ls], outer[:, ls]]
        py[side] = jnp.concatenate(parts, axis=0).astype(BF)
        for n in range(4):
            dx, dy = SIDES[4 + n]
            if (0 if dy == 1 else 1) == side:
                lo = 56 if dx == 1 else 0
                pc[n] = jnp.concatenate([p[lo : lo + 40] for p in parts] + [filler], axis=0).astype(BF)
    for n, lo in enumerate((56, 0)):
        px[n] = jnp.concatenate([mv[0, lo : lo + 40, :], mv[1, lo : lo + 40, :]], axis=0).astype(BF)

    pl.semaphore_wait(barrier, 4)
    for n, (dx, dy) in enumerate(UPPER):
        pl.semaphore_signal(
            here_sem.at[n], inc=1, device_id=at(dx, dy), device_id_type=pl.DeviceIdType.MESH
        )

    def send(src, dst, dx, dy):
        copy = pltpu.make_async_remote_copy(
            src_ref=src, dst_ref=dst, send_sem=send1, recv_sem=recv1,
            device_id=at(dx, dy), device_id_type=pl.DeviceIdType.MESH,
        )
        copy.start()

    def send_to(dx, dy):
        n = SIDES.index((dx, dy))
        if n < 2:
            send(px.at[n], rx.at[n], dx, dy)
        elif n < 4:
            send(py.at[n - 2], ry.at[n - 2], dx, dy)
        else:
            send(pc.at[n - 4], rc.at[n - 4], dx, dy)

    for dx, dy in UPPER[1:] + UPPER[:1]:
        send_to(dx, dy)

    for n, (dx, dy) in enumerate(UPPER):
        pl.semaphore_wait(here_sem.at[n], 1)
        send_to(-dx, -dy)

    rows8 = lax.broadcasted_iota(jnp.int32, (8, LANES), 0).astype(F32)

    def x_hot(r, _):
        lanes = pl.ds(pl.multiple_of(r * LANES, LANES), LANES)

        def row(n):
            return jnp.broadcast_to(q32[n, pl.ds(r, 1), :], (8, LANES))

        d = rows8 - row(0)
        ww = [row(2 + k) * row(22) for k in range(4)]
        for b in range(12):
            wx_hot[pl.ds(8 * b, 8), lanes] = chain(d + 8.0 * b, ww, 0.0)
        return 0

    lax.fori_loop(0, 16, x_hot, 0)
    for ref in (mt, ca, w1):
        for c in range(2):
            for t in range(6):
                ref[c, t, 0:8, :] = jnp.zeros((8, LANES), F32)
                ref[c, t, 120:128, :] = jnp.zeros((8, LANES), F32)

    everything = wy_hot.at[pl.ds(0, 128)]
    pltpu.make_async_copy(everything, everything, recv1).wait()
    pltpu.make_async_copy(everything, everything, send1).wait()

    corner = {}
    for n in range(4):
        dx, dy = SIDES[4 + n]
        corner[0 if dx == 1 else 1, 0 if dy == 1 else 1] = n

    def joined(mid, first, last):
        return [
            first[0:8], mid[0:32] + first[8:40], mid[32:64], mid[64:96] + last[0:32], last[32:40]
        ]

    ryf = [ry[side].astype(F32) for side in range(2)]
    rcf = [rc[n].astype(F32) for n in range(4)]
    rxf = [rx[n].astype(F32) for n in range(2)]
    from_y = [[r[96 * p : 96 * p + 96] for p in range(3)] for r in ryf]
    from_c = [[r[40 * p : 40 * p + 40] for p in range(3)] for r in rcf]
    placed = jnp.dot(
        jnp.concatenate(
            [
                jnp.concatenate([ry[side, 192:288, :] for side in range(2)], axis=1),
                jnp.concatenate([rc[corner[0, side], 80:128, :] for side in range(2)], axis=1),
                jnp.concatenate([rc[corner[1, side], 80:128, :] for side in range(2)], axis=1),
            ],
            axis=0,
        ),
        w_place[...],
        preferred_element_type=F32,
    )

    def assemble(t):
        for c in range(2):
            ls = slice(128 * t, 128 * t + 128)
            mid = mv[c, :, ls]
            first, last = (r[40 * c : 40 * c + 40, ls] for r in rxf)
            if t < 4:
                ps = slice(512 * c + 128 * t, 512 * c + 128 * t + 128)
                mid = mid + placed[0:96, ps]
                first = first + placed[96:136, ps]
                last = last + placed[144:184, ps]
            else:
                side = t - 4
                mid = mid + from_y[side][c]
                first = first + from_c[corner[0, side]][c]
                last = last + from_c[corner[1, side]][c]
            a = jnp.concatenate(joined(mid, first, last), axis=0)
            mt[c, t, 8:120, :] = a
            high, low = pieces(a)
            sp[t, 112 * c : 112 * c + 112, 0:128] = high
            sp[t, 112 * c : 112 * c + 112, 128:256] = low

    def advect(t):
        steps = jnp.dot(sp[t], w_adv[...], preferred_element_type=F32)
        for lo in range(0, 112, 16):
            here = slice(lo + 8, lo + 24)
            a = COURANT * mt[0, t, here, :]
            b = COURANT * mt[1, t, here, :]
            forth, right = a > 0.0, b > 0.0
            for c in range(2):
                q = mt[c, t, here, :]
                row = 112 * c + lo
                step_x = jnp.where(
                    forth, q - mt[c, t, lo + 7 : lo + 23, :], mt[c, t, lo + 9 : lo + 25, :] - q
                )
                step_y = jnp.where(
                    right, steps[row : row + 16, 0:128], steps[row : row + 16, 128:256]
                )
                value = q - (a * step_x + b * step_y)
                ca[c, t, here, :] = value
                high, low = pieces(value)
                ws[t, row : row + 16, 0:128] = high
                ws[t, row : row + 16, 128:256] = low

    scale = 1.0 / (1.0 + 6.0 * VISCOUS)

    def sweep(ref, beside, t, c, lo, row):
        here = slice(lo + 8, lo + 24)
        total = ref[c, t, lo + 7 : lo + 23, :] + ref[c, t, lo + 9 : lo + 25, :]
        total = total + beside[row : row + 16]
        if t < 4:
            total = total + (ref[c, min(t + 1, 3), here, :] + ref[c, max(t - 1, 0), here, :])
        return scale * ca[c, t, here, :] + (scale * VISCOUS) * total

    def first_sweep(t):
        beside = jnp.dot(ws[t], (w_t if t < 4 else w_s)[...], preferred_element_type=F32)
        for c in range(2):
            for lo in range(0, 112, 16):
                value = sweep(ca, beside, t, c, lo, 112 * c + lo)
                w1[c, t, lo + 8 : lo + 24, :] = value
                high, low = pieces(value)
                sp[t, 112 * c + lo : 112 * c + lo + 16, 0:128] = high
                sp[t, 112 * c + lo : 112 * c + lo + 16, 128:256] = low

    def second_sweep(t, c, beside):
        values = [sweep(w1, beside, t, c, lo, 112 * c + lo) for lo in range(0, 112, 16)]
        return jnp.concatenate(values, axis=0)[8:104]

    lane16 = lax.broadcasted_iota(jnp.int32, (16, LANES), 1)
    j16 = lane16 % 32
    keep = ((j16 >= 10) & (j16 < 26), (j16 >= 6) & (j16 < 22))
    assemble(4)
    assemble(5)
    advect(4)
    advect(5)
    assemble(0)
    first_sweep(4)
    first_sweep(5)
    for t in (1, 2, 3):
        assemble(t)
    for t in (4, 5):
        ls = slice(128 * (t - 4), 128 * (t - 4) + 128)
        beside = jnp.dot(sp[t], w_s[...], preferred_element_type=F32)
        for c in range(2):
            whole = second_sweep(t, c, beside)
            high, low = pieces(whole)
            ends_in[0, 96 * c : 96 * c + 96, ls] = high
            ends_in[1, 96 * c : 96 * c + 96, ls] = low
            kept = jnp.where(keep[t - 4], whole.reshape(6, 16, LANES), 0.0).reshape(96, LANES)
            ta[96 * c : 96 * c + 96, 128 * t : 128 * t + 128] = kept.astype(BF)
    for t in range(4):
        advect(t)
    ends = jnp.dot(ends_in[0], w_fix[...], preferred_element_type=F32)
    ends = ends + jnp.dot(ends_in[1], w_fix[...], preferred_element_type=F32)
    for t in range(4):
        first_sweep(t)
    lane = lax.broadcasted_iota(jnp.int32, (96, LANES), 1)
    inside = (lane >= 3) & (lane < 125)
    for t in range(4):
        ls = slice(128 * t, 128 * t + 128)
        beside = jnp.dot(sp[t], w_t[...], preferred_element_type=F32)
        for c in range(2):
            whole = second_sweep(t, c, beside)
            whole = jnp.where(inside, whole, ends[96 * c : 96 * c + 96, ls])
            out_v[t, c] = whole[16:80]
            ta[96 * c : 96 * c + 96, ls] = whole.astype(BF)


def sampling(v, ta, wy_hot, wx_hot, out_v, out_m, out_sem):
    copy = pltpu.make_async_copy(v, out_v, out_sem)
    copy.start()
    for r in range(4):
        lanes = slice(512 * r, 512 * r + 512)
        both = jnp.dot(ta[...], wy_hot[:, lanes], preferred_element_type=F32)
        for c in range(2):
            part = both[96 * c : 96 * c + 96]
            summed = jnp.sum(part * wx_hot[:, lanes], axis=0, keepdims=True)
            for i in range(4):
                out_m[c, 4 * r + i : 4 * r + i + 1, :] = summed[:, LANES * i : LANES * i + LANES]
    copy.wait()


def body(velocity, marker_cell, marker_frac, marker_force, fish_owner):
    nx = lax.axis_size("gx")
    ny = lax.axis_size("gy")
    vm = pl.BlockSpec(memory_space=pltpu.VMEM)
    v, ta, wy_hot, wx_hot = pl.pallas_call(
        functools.partial(kernel, nx, ny),
        out_shape=(
            jax.ShapeDtypeStruct((4, 2, 64, 128), F32),
            jax.ShapeDtypeStruct((192, 768), BF),
            jax.ShapeDtypeStruct((768, 2048), BF),
            jax.ShapeDtypeStruct((96, 2048), F32),
        ),
        in_specs=[pl.BlockSpec(memory_space=pltpu.HBM)] * 5,
        out_specs=(vm, vm, vm, vm),
        scratch_shapes=[
            pltpu.VMEM((4, 2, 64, 128), F32),
            pltpu.VMEM((3, 16, 128), jnp.int32),
            pltpu.VMEM((2, 16, 128), F32),
            pltpu.VMEM((2, 16, 128), F32),
            pltpu.VMEM((6, 128), jnp.int32),
            pltpu.VMEM((23, 16, 128), F32),
            pltpu.VMEM((192, 2048), BF),
            pltpu.VMEM((2, 96, 768), F32),
            pltpu.VMEM((192, 768), BF),
            pltpu.VMEM((2, 80, 768), BF),
            pltpu.VMEM((2, 288, 128), BF),
            pltpu.VMEM((4, 128, 128), BF),
            pltpu.VMEM((2, 80, 768), BF),
            pltpu.VMEM((2, 288, 128), BF),
            pltpu.VMEM((4, 128, 128), BF),
            pltpu.VMEM((2, 6, 128, 128), F32),
            pltpu.VMEM((2, 6, 128, 128), F32),
            pltpu.VMEM((2, 6, 128, 128), F32),
            pltpu.VMEM((6, 224, 256), BF),
            pltpu.VMEM((6, 224, 256), BF),
            pltpu.VMEM((2, 192, 256), BF),
            pltpu.VMEM((768, 256), BF),
            pltpu.VMEM((512, 256), BF),
            pltpu.VMEM((256, 1024), BF),
            pltpu.VMEM((256, 256), BF),
            pltpu.VMEM((256, 128), BF),
            pltpu.VMEM((256, 128), BF),
            pltpu.VMEM((256, 512), BF),
            pltpu.SemaphoreType.DMA((5,)),
            pltpu.SemaphoreType.DMA,
            pltpu.SemaphoreType.DMA,
            pltpu.SemaphoreType.REGULAR((4,)),
        ],
        compiler_params=pltpu.CompilerParams(
            collective_id=0, has_side_effects=True, vmem_limit_bytes=24 * 1024 * 1024
        ),
        name="fish_step",
    )(
        pltpu.with_memory_space_constraint(velocity, pltpu.HBM),
        pltpu.with_memory_space_constraint(marker_cell.reshape(3, 16, 128), pltpu.HBM),
        pltpu.with_memory_space_constraint(marker_frac.reshape(2, 16, 128), pltpu.HBM),
        pltpu.with_memory_space_constraint(marker_force.reshape(2, 16, 128), pltpu.HBM),
        pltpu.with_memory_space_constraint(fish_owner.reshape(6, 128), pltpu.HBM),
    )
    out_v, out_m = pl.pallas_call(
        sampling,
        out_shape=(
            jax.ShapeDtypeStruct((4, 2, 64, 128), F32),
            jax.ShapeDtypeStruct((2, 16, 128), F32),
        ),
        in_specs=[vm] * 4,
        out_specs=(pl.BlockSpec(memory_space=pltpu.HBM), vm),
        scratch_shapes=[pltpu.SemaphoreType.DMA],
        compiler_params=pltpu.CompilerParams(vmem_limit_bytes=8 * 1024 * 1024),
        name="fish_sample",
    )(v, ta, wy_hot, wx_hot)
    return out_v, out_m.reshape(2, 1, 1, 2048)


def solution(mesh):
    placed = (
        P(None, None, "gx", "gy"),
        P(None, "gx", "gy", None),
        P(None, "gx", "gy", None),
        P(None, "gx", "gy", None),
        P(),
    )
    return jax.shard_map(
        body,
        mesh=mesh,
        in_specs=placed,
        out_specs=(P(None, None, "gx", "gy"), P(None, "gx", "gy", None)),
        check_vma=False,
    )
```

```python
import functools
import math

import jax
import jax.numpy as jnp
from jax import lax
from jax.experimental import pallas as pl
from jax.experimental.pallas import tpu as pltpu
from jax.sharding import PartitionSpec as P

MARGIN = 16
FISH_MARK = 1024
COURANT = 0.25
VISCOUS = 1.5
LANES = 128
BF = jnp.bfloat16
F32 = jnp.float32

SIDES = [(1, 0), (-1, 0), (0, 1), (0, -1), (1, 1), (-1, 1), (1, -1), (-1, -1)]
UPPER = [(0, 1), (1, 0), (1, 1), (1, -1)]


def half_angle(t):
    z = t * (0.5 * math.pi)
    q = z * z
    s = 1.0 / math.factorial(13)
    for n in (11, 9, 7, 5, 3, 1):
        s = s * q + (-1.0) ** ((n - 1) // 2) / math.factorial(n)
    c = 1.0 / math.factorial(12)
    for n in (10, 8, 6, 4, 2, 0):
        c = c * q + (-1.0) ** (n // 2) / math.factorial(n)
    return s * z, c


def weights(t):
    s, c = half_angle(t)
    return (0.25 * (1.0 - s), 0.25 * (1.0 + c), 0.25 * (1.0 + s), 0.25 * (1.0 - c))


def chain(d, values, zero):
    out = jnp.where(d == 2.0, values[3], zero)
    out = jnp.where(d == 1.0, values[2], out)
    out = jnp.where(d == 0.0, values[1], out)
    return jnp.where(d == -1.0, values[0], out)


def pick(ref, source):
    rows, columns = ref.shape
    n = lax.broadcasted_iota(jnp.int32, (16, columns), 1)
    below = source(n) - lax.broadcasted_iota(jnp.int32, (16, columns), 0)
    for lo in range(0, rows, 16):
        ref[lo : lo + 16, :] = jnp.where(below == lo, 1.0, 0.0).astype(BF)


def matrices(w_in, w_out, w_place, w_adv, w_t, w_s, w_fix):
    def inner_of(n):
        p, l = n % 32, (n // 32) % 4
        up = jnp.where(p < 26, 128 * l + p + 102, 640 + 32 * l + p - 20)
        down = jnp.where(p < 6, 512 + 32 * l + p + 20, 128 * l + p - 6)
        return jnp.where(n < 128, up, down)

    def outer_of(n):
        i, c, l = n % 16, (n // 16) % 2, (n // 32) % 4
        return 256 * c + 32 * l + i + jnp.where(n < 128, 128 + 6, 10)

    def place_of(n):
        y, l, c = n % 128, (n // 128) % 4, n // 512
        at = 32 * l + 16 * c
        return jnp.where(y < 16, at + y, jnp.where(y >= 112, 128 + at + y - 112, -1))

    def fix_of(n):
        y, l = n % 128, n // 128
        return jnp.where(
            y < 3, 32 * l + 26 + y, jnp.where(y >= 125, 128 + 32 * l + y - 122, -1)
        )

    pick(w_in, inner_of)
    pick(w_out, outer_of)
    pick(w_place, place_of)
    pick(w_fix, fix_of)
    y = lax.broadcasted_iota(jnp.int32, (16, LANES), 1)
    r = lax.broadcasted_iota(jnp.int32, (16, LANES), 0)

    def one(of):
        return jnp.where(of == r, 1.0, 0.0)

    for lo in range(0, 256, 16):
        base = lo % LANES
        here, prev, after = one(y - base), one((y + 127) % 128 - base), one((y + 1) % 128 - base)
        w_adv[lo : lo + 16, 0:128] = (here - prev).astype(BF)
        w_adv[lo : lo + 16, 128:256] = (after - here).astype(BF)
        w_t[lo : lo + 16, :] = (prev + after).astype(BF)
        upper = one(jnp.where(y < 96, y + 32, y) - base)
        lower = one(jnp.where(y >= 32, y - 32, y) - base)
        w_s[lo : lo + 16, :] = (prev + after + upper + lower).astype(BF)


def pieces(v):
    high = v.astype(BF)
    return high, (v - high.astype(F32)).astype(BF)


def kernel(
    nx, ny,
    vel_h, cell_h, frac_h, force_h, owner_h,
    out_v, ta, wy_hot, wx_hot,
    vel, cell, frac, force, owner,
    q32, left, mv, mvb, px, py, pc, rx, ry, rc,
    mt, ca, w1, sp, ws, ends_in, w_in, w_out, w_place, w_adv, w_t, w_s, w_fix,
    in_sem, send1, recv1, here_sem,
):
    ix = lax.axis_index("gx")
    iy = lax.axis_index("gy")

    def at(dx, dy):
        return {"gx": lax.rem(ix + dx + nx, nx), "gy": lax.rem(iy + dy + ny, ny)}

    loads = []
    for n, (src, dst) in enumerate(
        ((cell_h, cell), (frac_h, frac), (force_h, force), (owner_h, owner), (vel_h, vel))
    ):
        loads.append(pltpu.make_async_copy(src, dst, in_sem.at[n]))
        loads[-1].start()
    barrier = pltpu.get_barrier_semaphore()
    for dx, dy in UPPER:
        pl.semaphore_signal(
            barrier, inc=1, device_id=at(-dx, -dy), device_id_type=pl.DeviceIdType.MESH
        )
    matrices(w_in, w_out, w_place, w_adv, w_t, w_s, w_fix)
    for load in loads:
        load.wait()

    mine = jnp.where(owner[...] == ix * ny + iy, 1.0, 0.0)
    count = jnp.sum(jnp.sum(mine, axis=1, keepdims=True), axis=0, keepdims=True)
    slot = lax.broadcasted_iota(jnp.int32, (16, LANES), 0) * LANES + lax.broadcasted_iota(
        jnp.int32, (16, LANES), 1
    )
    alive = jnp.where(slot.astype(F32) < FISH_MARK * count, 1.0, 0.0)
    rel_x = lax.rem(cell[0] - ix * 64 + (MARGIN + nx * 64), nx * 64)
    rel_y = lax.rem(cell[1] - iy * 128 + (MARGIN + ny * 128), ny * 128) - MARGIN
    q32[0] = rel_x.astype(F32)
    q32[1] = rel_y.astype(F32)
    wx = weights(frac[0])
    wy = weights(frac[1])
    for k in range(4):
        q32[2 + k] = wx[k]
        q32[6 + k] = wy[k]
        for c in range(2):
            q32[10 + 4 * c + k] = force[c] * alive * wx[k]
        q32[18 + k] = jnp.where(cell[2] == k, 1.0, 0.0)
    q32[22] = alive

    rows16 = lax.broadcasted_iota(jnp.int32, (16, LANES), 0).astype(F32)
    zero16 = jnp.zeros((16, LANES), BF)
    strips = ((512, -26.0), (528, -10.0), (640, 122.0), (656, 138.0))

    def operands(r, _):
        lanes = slice(r * LANES, r * LANES + LANES)

        def row(n):
            return jnp.broadcast_to(q32[n, r : r + 1, :], (16, LANES))

        dx0 = rows16 - row(0)
        lw = [[row(10 + 4 * c + k).astype(BF) for k in range(4)] for c in range(2)]
        for b in range(6):
            d = (dx0 + 16.0 * b).astype(BF)
            for c in range(2):
                left[pl.ds(96 * c + 16 * b, 16), lanes] = chain(d, lw[c], zero16)
        dy0 = rows16 - row(1)
        yw = [row(6 + k).astype(BF) for k in range(4)]
        lv = [row(18 + k).astype(BF) for k in range(4)]
        for b in range(12):
            base, step = (16.0 * b, 128) if b < 8 else (strips[b - 8][1], 32)
            first_row = 16 * b if b < 8 else strips[b - 8][0]
            d = (dy0 + base).astype(BF)
            w = chain(d, yw, zero16)
            for l in range(4):
                wy_hot[pl.ds(first_row + step * l, 16), lanes] = w * lv[l]
        return 0

    for r in range(16):
        operands(r, 0)

    lane64 = lax.broadcasted_iota(jnp.int32, (64, LANES), 1)
    level64, j64 = lane64 // 32, lane64 % 32
    both = lax.dot_general(
        left[...], wy_hot[...], (((1,), (1,)), ((), ())), preferred_element_type=F32
    )
    for c in range(2):
        spread = both[96 * c : 96 * c + 96]
        mv[c] = spread
        low_part = jnp.zeros((64, LANES), F32)
        high_part = jnp.zeros((64, LANES), F32)
        for l in range(4):
            ls = slice(128 * l, 128 * l + 128)
            v = vel[l, c]
            mv[c, 16:80, ls] = spread[16:80, ls] + v
            low_part = jnp.where(
                (level64 == l) & (j64 >= 26), pltpu.roll(v, 32 * l + 26, 1), low_part
            )
            high_part = jnp.where(
                (level64 == l) & (j64 < 6), pltpu.roll(v, 32 * l + 6, 1), high_part
            )
        mv[c, 16:80, 512:640] = spread[16:80, 512:640] + low_part
        mv[c, 16:80, 640:768] = spread[16:80, 640:768] + high_part

    for c in range(2):
        mvb[96 * c : 96 * c + 96, :] = mv[c].astype(BF)
    inner = jnp.dot(mvb[...], w_in[...], preferred_element_type=F32)
    outer = jnp.dot(mvb[0:96, 512:768], w_out[0:256, :], preferred_element_type=F32)
    outer = outer + jnp.dot(mvb[96:192, 512:768], w_out[256:512, :], preferred_element_type=F32)
    filler = jnp.zeros((8, LANES), F32)
    for side in range(2):
        ls = slice(128 * side, 128 * side + 128)
        parts = [inner[0:96, ls], inner[96:192, ls], outer[:, ls]]
        py[side] = jnp.concatenate(parts, axis=0).astype(BF)
        for n in range(4):
            dx, dy = SIDES[4 + n]
            if (0 if dy == 1 else 1) == side:
                lo = 56 if dx == 1 else 0
                pc[n] = jnp.concatenate([p[lo : lo + 40] for p in parts] + [filler], axis=0).astype(BF)
    for n, lo in enumerate((56, 0)):
        px[n] = jnp.concatenate([mv[0, lo : lo + 40, :], mv[1, lo : lo + 40, :]], axis=0).astype(BF)

    pl.semaphore_wait(barrier, 4)
    for n, (dx, dy) in enumerate(UPPER):
        pl.semaphore_signal(
            here_sem.at[n], inc=1, device_id=at(dx, dy), device_id_type=pl.DeviceIdType.MESH
        )

    def send(src, dst, dx, dy):
        copy = pltpu.make_async_remote_copy(
            src_ref=src, dst_ref=dst, send_sem=send1, recv_sem=recv1,
            device_id=at(dx, dy), device_id_type=pl.DeviceIdType.MESH,
        )
        copy.start()

    def send_to(dx, dy):
        n = SIDES.index((dx, dy))
        if n < 2:
            send(px.at[n], rx.at[n], dx, dy)
        elif n < 4:
            send(py.at[n - 2], ry.at[n - 2], dx, dy)
        else:
            send(pc.at[n - 4], rc.at[n - 4], dx, dy)

    for dx, dy in UPPER[2:] + UPPER[:2][::-1]:
        send_to(dx, dy)

    for n, (dx, dy) in enumerate(UPPER):
        pl.semaphore_wait(here_sem.at[n], 1)
        send_to(-dx, -dy)

    rows8 = lax.broadcasted_iota(jnp.int32, (8, LANES), 0).astype(F32)

    def x_hot(r, _):
        lanes = pl.ds(pl.multiple_of(r * LANES, LANES), LANES)

        def row(n):
            return jnp.broadcast_to(q32[n, pl.ds(r, 1), :], (8, LANES))

        d = rows8 - row(0)
        ww = [row(2 + k) * row(22) for k in range(4)]
        for b in range(12):
            wx_hot[pl.ds(8 * b, 8), lanes] = chain(d + 8.0 * b, ww, 0.0)
        return 0

    lax.fori_loop(0, 16, x_hot, 0)
    for ref in (mt, ca, w1):
        for c in range(2):
            for t in range(6):
                ref[c, t, 0:8, :] = jnp.zeros((8, LANES), F32)
                ref[c, t, 120:128, :] = jnp.zeros((8, LANES), F32)

    everything = wy_hot.at[pl.ds(0, 128)]
    pltpu.make_async_copy(everything, everything, recv1).wait()
    pltpu.make_async_copy(everything, everything, send1).wait()

    corner = {}
    for n in range(4):
        dx, dy = SIDES[4 + n]
        corner[0 if dx == 1 else 1, 0 if dy == 1 else 1] = n

    def joined(mid, first, last):
        return [
            first[0:8], mid[0:32] + first[8:40], mid[32:64], mid[64:96] + last[0:32], last[32:40]
        ]

    ryf = [ry[side].astype(F32) for side in range(2)]
    rcf = [rc[n].astype(F32) for n in range(4)]
    rxf = [rx[n].astype(F32) for n in range(2)]
    from_y = [[r[96 * p : 96 * p + 96] for p in range(3)] for r in ryf]
    from_c = [[r[40 * p : 40 * p + 40] for p in range(3)] for r in rcf]
    placed = jnp.dot(
        jnp.concatenate(
            [
                jnp.concatenate([ry[side, 192:288, :] for side in range(2)], axis=1),
                jnp.concatenate([rc[corner[0, side], 80:128, :] for side in range(2)], axis=1),
                jnp.concatenate([rc[corner[1, side], 80:128, :] for side in range(2)], axis=1),
            ],
            axis=0,
        ),
        w_place[...],
        preferred_element_type=F32,
    )

    def assemble(t):
        for c in range(2):
            ls = slice(128 * t, 128 * t + 128)
            mid = mv[c, :, ls]
            first, last = (r[40 * c : 40 * c + 40, ls] for r in rxf)
            if t < 4:
                ps = slice(512 * c + 128 * t, 512 * c + 128 * t + 128)
                mid = mid + placed[0:96, ps]
                first = first + placed[96:136, ps]
                last = last + placed[144:184, ps]
            else:
                side = t - 4
                mid = mid + from_y[side][c]
                first = first + from_c[corner[0, side]][c]
                last = last + from_c[corner[1, side]][c]
            a = jnp.concatenate(joined(mid, first, last), axis=0)
            mt[c, t, 8:120, :] = a
            high, low = pieces(a)
            sp[t, 112 * c : 112 * c + 112, 0:128] = high
            sp[t, 112 * c : 112 * c + 112, 128:256] = low

    def advect(t):
        steps = jnp.dot(sp[t], w_adv[...], preferred_element_type=F32)
        for lo in range(0, 112, 16):
            here = slice(lo + 8, lo + 24)
            a = COURANT * mt[0, t, here, :]
            b = COURANT * mt[1, t, here, :]
            forth, right = a > 0.0, b > 0.0
            for c in range(2):
                q = mt[c, t, here, :]
                row = 112 * c + lo
                step_x = jnp.where(
                    forth, q - mt[c, t, lo + 7 : lo + 23, :], mt[c, t, lo + 9 : lo + 25, :] - q
                )
                step_y = jnp.where(
                    right, steps[row : row + 16, 0:128], steps[row : row + 16, 128:256]
                )
                value = q - (a * step_x + b * step_y)
                ca[c, t, here, :] = value
                high, low = pieces(value)
                ws[t, row : row + 16, 0:128] = high
                ws[t, row : row + 16, 128:256] = low

    scale = 1.0 / (1.0 + 6.0 * VISCOUS)

    def sweep(ref, beside, t, c, lo, row):
        here = slice(lo + 8, lo + 24)
        total = ref[c, t, lo + 7 : lo + 23, :] + ref[c, t, lo + 9 : lo + 25, :]
        total = total + beside[row : row + 16]
        if t < 4:
            total = total + (ref[c, min(t + 1, 3), here, :] + ref[c, max(t - 1, 0), here, :])
        return scale * ca[c, t, here, :] + (scale * VISCOUS) * total

    def first_sweep(t):
        beside = jnp.dot(ws[t], (w_t if t < 4 else w_s)[...], preferred_element_type=F32)
        for c in range(2):
            for lo in range(0, 112, 16):
                value = sweep(ca, beside, t, c, lo, 112 * c + lo)
                w1[c, t, lo + 8 : lo + 24, :] = value
                high, low = pieces(value)
                sp[t, 112 * c + lo : 112 * c + lo + 16, 0:128] = high
                sp[t, 112 * c + lo : 112 * c + lo + 16, 128:256] = low

    def second_sweep(t, c, beside):
        values = [sweep(w1, beside, t, c, lo, 112 * c + lo) for lo in range(0, 112, 16)]
        return jnp.concatenate(values, axis=0)[8:104]

    lane16 = lax.broadcasted_iota(jnp.int32, (16, LANES), 1)
    j16 = lane16 % 32
    keep = ((j16 >= 10) & (j16 < 26), (j16 >= 6) & (j16 < 22))
    assemble(4)
    assemble(5)
    advect(4)
    advect(5)
    assemble(0)
    first_sweep(4)
    first_sweep(5)
    for t in (1, 2, 3):
        assemble(t)
    for t in (4, 5):
        ls = slice(128 * (t - 4), 128 * (t - 4) + 128)
        beside = jnp.dot(sp[t], w_s[...], preferred_element_type=F32)
        for c in range(2):
            whole = second_sweep(t, c, beside)
            high, low = pieces(whole)
            ends_in[0, 96 * c : 96 * c + 96, ls] = high
            ends_in[1, 96 * c : 96 * c + 96, ls] = low
            kept = jnp.where(keep[t - 4], whole.reshape(6, 16, LANES), 0.0).reshape(96, LANES)
            ta[96 * c : 96 * c + 96, 128 * t : 128 * t + 128] = kept.astype(BF)
    for t in range(4):
        advect(t)
    ends = jnp.dot(ends_in[0], w_fix[...], preferred_element_type=F32)
    ends = ends + jnp.dot(ends_in[1], w_fix[...], preferred_element_type=F32)
    for t in range(4):
        first_sweep(t)
    lane = lax.broadcasted_iota(jnp.int32, (96, LANES), 1)
    inside = (lane >= 3) & (lane < 125)
    for t in range(4):
        ls = slice(128 * t, 128 * t + 128)
        beside = jnp.dot(sp[t], w_t[...], preferred_element_type=F32)
        for c in range(2):
            whole = second_sweep(t, c, beside)
            whole = jnp.where(inside, whole, ends[96 * c : 96 * c + 96, ls])
            out_v[t, c] = whole[16:80]
            ta[96 * c : 96 * c + 96, ls] = whole.astype(BF)


def sampling(v, ta, wy_hot, wx_hot, out_v, out_m, out_sem):
    copy = pltpu.make_async_copy(v, out_v, out_sem)
    copy.start()
    for r in range(4):
        lanes = slice(512 * r, 512 * r + 512)
        both = jnp.dot(ta[...], wy_hot[:, lanes], preferred_element_type=F32)
        for c in range(2):
            part = both[96 * c : 96 * c + 96]
            summed = jnp.sum(part * wx_hot[:, lanes], axis=0, keepdims=True)
            for i in range(4):
                out_m[c, 4 * r + i : 4 * r + i + 1, :] = summed[:, LANES * i : LANES * i + LANES]
    copy.wait()


def body(velocity, marker_cell, marker_frac, marker_force, fish_owner):
    nx = lax.axis_size("gx")
    ny = lax.axis_size("gy")
    vm = pl.BlockSpec(memory_space=pltpu.VMEM)
    v, ta, wy_hot, wx_hot = pl.pallas_call(
        functools.partial(kernel, nx, ny),
        out_shape=(
            jax.ShapeDtypeStruct((4, 2, 64, 128), F32),
            jax.ShapeDtypeStruct((192, 768), BF),
            jax.ShapeDtypeStruct((768, 2048), BF),
            jax.ShapeDtypeStruct((96, 2048), F32),
        ),
        in_specs=[pl.BlockSpec(memory_space=pltpu.HBM)] * 5,
        out_specs=(vm, vm, vm, vm),
        scratch_shapes=[
            pltpu.VMEM((4, 2, 64, 128), F32),
            pltpu.VMEM((3, 16, 128), jnp.int32),
            pltpu.VMEM((2, 16, 128), F32),
            pltpu.VMEM((2, 16, 128), F32),
            pltpu.VMEM((6, 128), jnp.int32),
            pltpu.VMEM((23, 16, 128), F32),
            pltpu.VMEM((192, 2048), BF),
            pltpu.VMEM((2, 96, 768), F32),
            pltpu.VMEM((192, 768), BF),
            pltpu.VMEM((2, 80, 768), BF),
            pltpu.VMEM((2, 288, 128), BF),
            pltpu.VMEM((4, 128, 128), BF),
            pltpu.VMEM((2, 80, 768), BF),
            pltpu.VMEM((2, 288, 128), BF),
            pltpu.VMEM((4, 128, 128), BF),
            pltpu.VMEM((2, 6, 128, 128), F32),
            pltpu.VMEM((2, 6, 128, 128), F32),
            pltpu.VMEM((2, 6, 128, 128), F32),
            pltpu.VMEM((6, 224, 256), BF),
            pltpu.VMEM((6, 224, 256), BF),
            pltpu.VMEM((2, 192, 256), BF),
            pltpu.VMEM((768, 256), BF),
            pltpu.VMEM((512, 256), BF),
            pltpu.VMEM((256, 1024), BF),
            pltpu.VMEM((256, 256), BF),
            pltpu.VMEM((256, 128), BF),
            pltpu.VMEM((256, 128), BF),
            pltpu.VMEM((256, 512), BF),
            pltpu.SemaphoreType.DMA((5,)),
            pltpu.SemaphoreType.DMA,
            pltpu.SemaphoreType.DMA,
            pltpu.SemaphoreType.REGULAR((4,)),
        ],
        compiler_params=pltpu.CompilerParams(
            collective_id=0, has_side_effects=True, vmem_limit_bytes=24 * 1024 * 1024
        ),
        name="fish_step",
    )(
        pltpu.with_memory_space_constraint(velocity, pltpu.HBM),
        pltpu.with_memory_space_constraint(marker_cell.reshape(3, 16, 128), pltpu.HBM),
        pltpu.with_memory_space_constraint(marker_frac.reshape(2, 16, 128), pltpu.HBM),
        pltpu.with_memory_space_constraint(marker_force.reshape(2, 16, 128), pltpu.HBM),
        pltpu.with_memory_space_constraint(fish_owner.reshape(6, 128), pltpu.HBM),
    )
    out_v, out_m = pl.pallas_call(
        sampling,
        out_shape=(
            jax.ShapeDtypeStruct((4, 2, 64, 128), F32),
            jax.ShapeDtypeStruct((2, 16, 128), F32),
        ),
        in_specs=[vm] * 4,
        out_specs=(pl.BlockSpec(memory_space=pltpu.HBM), vm),
        scratch_shapes=[pltpu.SemaphoreType.DMA],
        compiler_params=pltpu.CompilerParams(vmem_limit_bytes=8 * 1024 * 1024),
        name="fish_sample",
    )(v, ta, wy_hot, wx_hot)
    return out_v, out_m.reshape(2, 1, 1, 2048)


def solution(mesh):
    placed = (
        P(None, None, "gx", "gy"),
        P(None, "gx", "gy", None),
        P(None, "gx", "gy", None),
        P(None, "gx", "gy", None),
        P(),
    )
    return jax.shard_map(
        body,
        mesh=mesh,
        in_specs=placed,
        out_specs=(P(None, None, "gx", "gy"), P(None, "gx", "gy", None)),
        check_vma=False,
    )
```

```python
import functools
import math

import jax
import jax.numpy as jnp
from jax import lax
from jax.experimental import pallas as pl
from jax.experimental.pallas import tpu as pltpu
from jax.sharding import PartitionSpec as P

MARGIN = 16
FISH_MARK = 1024
COURANT = 0.25
VISCOUS = 1.5
LANES = 128
BF = jnp.bfloat16
F32 = jnp.float32

SIDES = [(1, 0), (-1, 0), (0, 1), (0, -1), (1, 1), (-1, 1), (1, -1), (-1, -1)]
UPPER = [(0, 1), (1, 0), (1, 1), (1, -1)]


def half_angle(t):
    z = t * (0.5 * math.pi)
    q = z * z
    s = 1.0 / math.factorial(13)
    for n in (11, 9, 7, 5, 3, 1):
        s = s * q + (-1.0) ** ((n - 1) // 2) / math.factorial(n)
    c = 1.0 / math.factorial(12)
    for n in (10, 8, 6, 4, 2, 0):
        c = c * q + (-1.0) ** (n // 2) / math.factorial(n)
    return s * z, c


def weights(t):
    s, c = half_angle(t)
    return (0.25 * (1.0 - s), 0.25 * (1.0 + c), 0.25 * (1.0 + s), 0.25 * (1.0 - c))


def chain(d, values, zero):
    out = jnp.where(d == 2.0, values[3], zero)
    out = jnp.where(d == 1.0, values[2], out)
    out = jnp.where(d == 0.0, values[1], out)
    return jnp.where(d == -1.0, values[0], out)


def pick(ref, source):
    rows, columns = ref.shape
    n = lax.broadcasted_iota(jnp.int32, (16, columns), 1)
    below = source(n) - lax.broadcasted_iota(jnp.int32, (16, columns), 0)
    for lo in range(0, rows, 16):
        ref[lo : lo + 16, :] = jnp.where(below == lo, 1.0, 0.0).astype(BF)


def matrices(w_in, w_out, w_place, w_adv, w_t, w_s, w_fix, w_strip, w_edge, w_cut):
    def inner_of(n):
        p, l = n % 32, (n // 32) % 4
        up = jnp.where(p < 26, 128 * l + p + 102, -1)
        down = jnp.where(p < 6, -1, 128 * l + p - 6)
        return jnp.where(n < 128, up, down)

    def outer_of(n):
        i, c, l = n % 16, (n // 16) % 2, (n // 32) % 4
        return 128 * c + 16 * l + i + jnp.where(n < 128, 64, 0)

    def place_of(n):
        y, l, c = n % 128, (n // 128) % 4, n // 512
        at = 32 * l + 16 * c
        return jnp.where(y < 16, at + y, jnp.where(y >= 112, 128 + at + y - 112, -1))

    def fix_of(n):
        y, l = n % 128, n // 128
        return jnp.where(
            y < 3, 32 * l + 26 + y, jnp.where(y >= 125, 128 + 32 * l + y - 122, -1)
        )

    def strip_of(n):
        j, l, side = n % 32, (n // 32) % 4, n // 128
        i = j - jnp.where(side == 0, 10, 6)
        return jnp.where((i >= 0) & (i < 16), 64 * side + 16 * l + i, -1)

    def edge_of(n):
        j, l = n % 32, (n // 32) % 4
        low = jnp.where(j >= 26, 256 * l + j - 26, -1)
        return jnp.where(n < 128, low, jnp.where(j < 6, 256 * l + j + 122, -1))

    def cut_of(n):
        i, l, side = n % 16, (n // 16) % 4, n // 64
        return 128 * side + 32 * l + i + jnp.where(side == 0, 10, 6)

    for half in range(2):
        pick(w_strip.at[pl.ds(128 * half, 128)], strip_of)
    for l in range(4):
        for half in range(2):
            rows = pl.ds(256 * l + 128 * half, 128)
            pick(w_edge.at[rows], lambda n: jnp.where(edge_of(n) // 256 == l, edge_of(n) - 256 * l, -1))
    pick(w_cut, cut_of)
    pick(w_in, inner_of)
    pick(w_out, outer_of)
    pick(w_place, place_of)
    pick(w_fix, fix_of)
    y = lax.broadcasted_iota(jnp.int32, (16, LANES), 1)
    r = lax.broadcasted_iota(jnp.int32, (16, LANES), 0)

    def one(of):
        return jnp.where(of == r, 1.0, 0.0)

    for lo in range(0, 256, 16):
        base = lo % LANES
        here, prev, after = one(y - base), one((y + 127) % 128 - base), one((y + 1) % 128 - base)
        w_adv[lo : lo + 16, 0:128] = (here - prev).astype(BF)
        w_adv[lo : lo + 16, 128:256] = (after - here).astype(BF)
        w_t[lo : lo + 16, :] = (prev + after).astype(BF)
        upper = one(jnp.where(y < 96, y + 32, y) - base)
        lower = one(jnp.where(y >= 32, y - 32, y) - base)
        w_s[lo : lo + 16, :] = (prev + after + upper + lower).astype(BF)


def pieces(v):
    high = v.astype(BF)
    return high, (v - high.astype(F32)).astype(BF)


def kernel(
    nx, ny,
    vel_h, cell_h, frac_h, force_h, owner_h,
    out_v, ta, wy_hot, wx_hot,
    vel, cell, frac, force, owner,
    q32, left, mv, mvb, px, py, pc, rx, ry, rc,
    mt, ca, w1, sp, ws, ends_in, beyond, w_in, w_out, w_place, w_adv, w_t, w_s, w_fix,
    w_strip, w_edge, w_cut,
    in_sem, send1, recv1, here_sem,
):
    ix = lax.axis_index("gx")
    iy = lax.axis_index("gy")

    def at(dx, dy):
        return {"gx": lax.rem(ix + dx + nx, nx), "gy": lax.rem(iy + dy + ny, ny)}

    loads = []
    for n, (src, dst) in enumerate(
        ((cell_h, cell), (frac_h, frac), (force_h, force), (owner_h, owner), (vel_h, vel))
    ):
        loads.append(pltpu.make_async_copy(src, dst, in_sem.at[n]))
        loads[-1].start()
    barrier = pltpu.get_barrier_semaphore()
    for dx, dy in UPPER:
        pl.semaphore_signal(
            barrier, inc=1, device_id=at(-dx, -dy), device_id_type=pl.DeviceIdType.MESH
        )
    matrices(w_in, w_out, w_place, w_adv, w_t, w_s, w_fix, w_strip, w_edge, w_cut)
    for load in loads:
        load.wait()

    mine = jnp.where(owner[...] == ix * ny + iy, 1.0, 0.0)
    count = jnp.sum(jnp.sum(mine, axis=1, keepdims=True), axis=0, keepdims=True)
    slot = lax.broadcasted_iota(jnp.int32, (16, LANES), 0) * LANES + lax.broadcasted_iota(
        jnp.int32, (16, LANES), 1
    )
    alive = jnp.where(slot.astype(F32) < FISH_MARK * count, 1.0, 0.0)
    rel_x = lax.rem(cell[0] - ix * 64 + (MARGIN + nx * 64), nx * 64)
    rel_y = lax.rem(cell[1] - iy * 128 + (MARGIN + ny * 128), ny * 128) - MARGIN
    q32[0] = rel_x.astype(F32)
    q32[1] = rel_y.astype(F32)
    wx = weights(frac[0])
    wy = weights(frac[1])
    for k in range(4):
        q32[2 + k] = wx[k]
        q32[6 + k] = wy[k]
        for c in range(2):
            q32[10 + 4 * c + k] = force[c] * alive * wx[k]
        q32[18 + k] = jnp.where(cell[2] == k, 1.0, 0.0)
    q32[22] = alive

    rows16 = lax.broadcasted_iota(jnp.int32, (16, LANES), 0).astype(F32)
    zero16 = jnp.zeros((16, LANES), BF)
    strips = ((512, -16.0), (576, 128.0))

    def operands(r, _):
        lanes = slice(r * LANES, r * LANES + LANES)

        def row(n):
            return jnp.broadcast_to(q32[n, r : r + 1, :], (16, LANES))

        dx0 = (rows16 - row(0)).astype(BF)
        lw = [[row(10 + 4 * c + k).astype(BF) for k in range(4)] for c in range(2)]
        for b in range(6):
            d = dx0 + jnp.asarray(16.0 * b, BF)
            for c in range(2):
                left[pl.ds(96 * c + 16 * b, 16), lanes] = chain(d, lw[c], zero16)
        dy0 = (rows16 - row(1)).astype(BF)
        yw = [row(6 + k).astype(BF) for k in range(4)]
        lv = [row(18 + k).astype(BF) for k in range(4)]
        for b in range(10):
            base, step = (16.0 * b, 128) if b < 8 else (strips[b - 8][1], 16)
            first_row = 16 * b if b < 8 else strips[b - 8][0]
            d = dy0 + jnp.asarray(base, BF)
            w = chain(d, yw, zero16)
            for l in range(4):
                wy_hot[pl.ds(first_row + step * l, 16), lanes] = w * lv[l]
        return 0

    for r in range(16):
        operands(r, 0)

    both = lax.dot_general(
        left[...], wy_hot[...], (((1,), (1,)), ((), ())), preferred_element_type=F32
    )
    for c in range(2):
        spread = both[96 * c : 96 * c + 96]
        mv[c] = spread
        for l in range(4):
            ls = slice(128 * l, 128 * l + 128)
            v = vel[l, c]
            mv[c, 16:80, ls] = spread[16:80, ls] + v

    for c in range(2):
        mvb[96 * c : 96 * c + 96, :] = mv[c].astype(BF)
    inner = jnp.dot(mvb[:, 0:512], w_in[...], preferred_element_type=F32)
    outer = jnp.dot(
        jnp.concatenate([mvb[0:96, 512:640], mvb[96:192, 512:640]], axis=1),
        w_out[...],
        preferred_element_type=F32,
    )
    filler = jnp.zeros((8, LANES), F32)
    for side in range(2):
        ls = slice(128 * side, 128 * side + 128)
        parts = [inner[0:96, ls], inner[96:192, ls], outer[:, ls]]
        py[side] = jnp.concatenate(parts, axis=0).astype(BF)
        for n in range(4):
            dx, dy = SIDES[4 + n]
            if (0 if dy == 1 else 1) == side:
                lo = 56 if dx == 1 else 0
                pc[n] = jnp.concatenate([p[lo : lo + 40] for p in parts] + [filler], axis=0).astype(BF)
    for n, lo in enumerate((56, 0)):
        px[n] = jnp.concatenate([mv[0, lo : lo + 40, :], mv[1, lo : lo + 40, :]], axis=0).astype(BF)

    pl.semaphore_wait(barrier, 4)
    for n, (dx, dy) in enumerate(UPPER):
        pl.semaphore_signal(
            here_sem.at[n], inc=1, device_id=at(dx, dy), device_id_type=pl.DeviceIdType.MESH
        )

    def send(src, dst, dx, dy):
        copy = pltpu.make_async_remote_copy(
            src_ref=src, dst_ref=dst, send_sem=send1, recv_sem=recv1,
            device_id=at(dx, dy), device_id_type=pl.DeviceIdType.MESH,
        )
        copy.start()

    def send_to(dx, dy):
        n = SIDES.index((dx, dy))
        if n < 2:
            send(px.at[n], rx.at[n], dx, dy)
        elif n < 4:
            send(py.at[n - 2], ry.at[n - 2], dx, dy)
        else:
            send(pc.at[n - 4], rc.at[n - 4], dx, dy)

    for dx, dy in UPPER[2:] + UPPER[:2][::-1]:
        send_to(dx, dy)

    for n, (dx, dy) in enumerate(UPPER):
        pl.semaphore_wait(here_sem.at[n], 1)
        send_to(-dx, -dy)

    rows8 = lax.broadcasted_iota(jnp.int32, (8, LANES), 0).astype(F32)

    def x_hot(r, _):
        lanes = pl.ds(pl.multiple_of(r * LANES, LANES), LANES)

        def row(n):
            return jnp.broadcast_to(q32[n, pl.ds(r, 1), :], (8, LANES))

        d = rows8 - row(0)
        ww = [row(2 + k) * row(22) for k in range(4)]
        for b in range(12):
            wx_hot[pl.ds(8 * b, 8), lanes] = chain(d + 8.0 * b, ww, 0.0)
        return 0

    lax.fori_loop(0, 16, x_hot, 0)
    for ref in (mt, ca, w1):
        for c in range(2):
            for t in range(6):
                ref[c, t, 0:8, :] = jnp.zeros((8, LANES), F32)
                ref[c, t, 120:128, :] = jnp.zeros((8, LANES), F32)

    everything = w_edge.at[pl.ds(0, 944)]
    pltpu.make_async_copy(everything, everything, recv1).wait()
    pltpu.make_async_copy(everything, everything, send1).wait()

    corner = {}
    for n in range(4):
        dx, dy = SIDES[4 + n]
        corner[0 if dx == 1 else 1, 0 if dy == 1 else 1] = n

    def joined(mid, first, last):
        return [
            first[0:8], mid[0:32] + first[8:40], mid[32:64], mid[64:96] + last[0:32], last[32:40]
        ]

    ryf = [ry[side].astype(F32) for side in range(2)]
    rcf = [rc[n].astype(F32) for n in range(4)]
    rxf = [rx[n].astype(F32) for n in range(2)]
    from_y = [[r[96 * p : 96 * p + 96] for p in range(3)] for r in ryf]
    from_c = [[r[40 * p : 40 * p + 40] for p in range(3)] for r in rcf]
    placed = jnp.dot(
        jnp.concatenate(
            [
                jnp.concatenate([ry[side, 192:288, :] for side in range(2)], axis=1),
                jnp.concatenate([rc[corner[0, side], 80:128, :] for side in range(2)], axis=1),
                jnp.concatenate([rc[corner[1, side], 80:128, :] for side in range(2)], axis=1),
            ],
            axis=0,
        ),
        w_place[...],
        preferred_element_type=F32,
    )

    def keep_pieces(t, c, a):
        mt[c, t, 8:120, :] = a
        high, low = pieces(a)
        sp[t, 112 * c : 112 * c + 112, 0:128] = high
        sp[t, 112 * c : 112 * c + 112, 128:256] = low

    def assemble(t):
        for c in range(2):
            ls = slice(128 * t, 128 * t + 128)
            first, last = (r[40 * c : 40 * c + 40, ls] for r in rxf)
            ps = slice(512 * c + 128 * t, 512 * c + 128 * t + 128)
            parts = joined(
                mv[c, :, ls] + placed[0:96, ps],
                first + placed[96:136, ps],
                last + placed[144:184, ps],
            )
            keep_pieces(t, c, jnp.concatenate(parts, axis=0))

    def outside_pieces():
        for c in range(2):
            first, last = (r[40 * c : 40 * c + 40, 512:640] for r in rxf)
            whole = jnp.concatenate(joined(mv[c, :, 512:640], first, last), axis=0)
            high, low = pieces(whole)
            beyond[112 * c : 112 * c + 112, 0:128] = high
            beyond[112 * c : 112 * c + 112, 128:256] = low

    def assemble_strips():
        total = jnp.dot(beyond[...], w_strip[...], preferred_element_type=F32)
        for l in range(4):
            total = total + jnp.dot(
                sp[l], w_edge[256 * l : 256 * l + 256, :], preferred_element_type=F32
            )
        for side in range(2):
            for c in range(2):
                inside = joined(
                    from_y[side][c], from_c[corner[0, side]][c], from_c[corner[1, side]][c]
                )
                own = total[112 * c : 112 * c + 112, 128 * side : 128 * side + 128]
                keep_pieces(4 + side, c, own + jnp.concatenate(inside, axis=0))

    def advect(t):
        steps = jnp.dot(sp[t], w_adv[...], preferred_element_type=F32)
        for lo in range(0, 112, 16):
            here = slice(lo + 8, lo + 24)
            a = COURANT * mt[0, t, here, :]
            b = COURANT * mt[1, t, here, :]
            forth, right = a > 0.0, b > 0.0
            for c in range(2):
                q = mt[c, t, here, :]
                row = 112 * c + lo
                step_x = jnp.where(
                    forth, q - mt[c, t, lo + 7 : lo + 23, :], mt[c, t, lo + 9 : lo + 25, :] - q
                )
                step_y = jnp.where(
                    right, steps[row : row + 16, 0:128], steps[row : row + 16, 128:256]
                )
                value = q - (a * step_x + b * step_y)
                ca[c, t, here, :] = value
                high, low = pieces(value)
                ws[t, row : row + 16, 0:128] = high
                ws[t, row : row + 16, 128:256] = low

    scale = 1.0 / (1.0 + 6.0 * VISCOUS)

    def sweep(ref, beside, t, c, lo, row):
        here = slice(lo + 8, lo + 24)
        total = ref[c, t, lo + 7 : lo + 23, :] + ref[c, t, lo + 9 : lo + 25, :]
        total = total + beside[row : row + 16]
        if t < 4:
            total = total + (ref[c, min(t + 1, 3), here, :] + ref[c, max(t - 1, 0), here, :])
        return scale * ca[c, t, here, :] + (scale * VISCOUS) * total

    def first_sweep(t):
        beside = jnp.dot(ws[t], (w_t if t < 4 else w_s)[...], preferred_element_type=F32)
        for c in range(2):
            for lo in range(0, 112, 16):
                value = sweep(ca, beside, t, c, lo, 112 * c + lo)
                w1[c, t, lo + 8 : lo + 24, :] = value
                high, low = pieces(value)
                sp[t, 112 * c + lo : 112 * c + lo + 16, 0:128] = high
                sp[t, 112 * c + lo : 112 * c + lo + 16, 128:256] = low

    def second_sweep(t, c, beside):
        values = [sweep(w1, beside, t, c, lo, 112 * c + lo) for lo in range(0, 112, 16)]
        return jnp.concatenate(values, axis=0)[8:104]

    outside_pieces()
    for t in range(4):
        assemble(t)
    advect(0)
    assemble_strips()
    advect(1)
    advect(4)
    advect(5)
    advect(2)
    first_sweep(4)
    first_sweep(5)
    advect(3)
    for t in (4, 5):
        ls = slice(128 * (t - 4), 128 * (t - 4) + 128)
        beside = jnp.dot(sp[t], w_s[...], preferred_element_type=F32)
        for c in range(2):
            whole = second_sweep(t, c, beside)
            high, low = pieces(whole)
            ends_in[0, 96 * c : 96 * c + 96, ls] = high
            ends_in[1, 96 * c : 96 * c + 96, ls] = low
    cut = jnp.dot(ends_in[0], w_cut[...], preferred_element_type=F32)
    ta[:, 512:640] = cut.astype(BF)
    first_sweep(0)
    first_sweep(1)
    ends = jnp.dot(ends_in[0], w_fix[...], preferred_element_type=F32)
    ends = ends + jnp.dot(ends_in[1], w_fix[...], preferred_element_type=F32)
    first_sweep(2)
    first_sweep(3)
    lane = lax.broadcasted_iota(jnp.int32, (96, LANES), 1)
    inside = (lane >= 3) & (lane < 125)
    for t in range(4):
        ls = slice(128 * t, 128 * t + 128)
        beside = jnp.dot(sp[t], w_t[...], preferred_element_type=F32)
        for c in range(2):
            whole = second_sweep(t, c, beside)
            whole = jnp.where(inside, whole, ends[96 * c : 96 * c + 96, ls])
            out_v[t, c] = whole[16:80]
            ta[96 * c : 96 * c + 96, ls] = whole.astype(BF)


def sampling(v, ta, wy_hot, wx_hot, out_v, out_m, out_sem):
    copy = pltpu.make_async_copy(v, out_v, out_sem)
    copy.start()
    for r in range(4):
        lanes = slice(512 * r, 512 * r + 512)
        both = jnp.dot(ta[...], wy_hot[:, lanes], preferred_element_type=F32)
        for c in range(2):
            part = both[96 * c : 96 * c + 96]
            summed = jnp.sum(part * wx_hot[:, lanes], axis=0, keepdims=True)
            for i in range(4):
                out_m[c, 4 * r + i : 4 * r + i + 1, :] = summed[:, LANES * i : LANES * i + LANES]
    copy.wait()


def body(velocity, marker_cell, marker_frac, marker_force, fish_owner):
    nx = lax.axis_size("gx")
    ny = lax.axis_size("gy")
    vm = pl.BlockSpec(memory_space=pltpu.VMEM)
    v, ta, wy_hot, wx_hot = pl.pallas_call(
        functools.partial(kernel, nx, ny),
        out_shape=(
            jax.ShapeDtypeStruct((4, 2, 64, 128), F32),
            jax.ShapeDtypeStruct((192, 640), BF),
            jax.ShapeDtypeStruct((640, 2048), BF),
            jax.ShapeDtypeStruct((96, 2048), F32),
        ),
        in_specs=[pl.BlockSpec(memory_space=pltpu.HBM)] * 5,
        out_specs=(vm, vm, vm, vm),
        scratch_shapes=[
            pltpu.VMEM((4, 2, 64, 128), F32),
            pltpu.VMEM((3, 16, 128), jnp.int32),
            pltpu.VMEM((2, 16, 128), F32),
            pltpu.VMEM((2, 16, 128), F32),
            pltpu.VMEM((6, 128), jnp.int32),
            pltpu.VMEM((23, 16, 128), F32),
            pltpu.VMEM((192, 2048), BF),
            pltpu.VMEM((2, 96, 640), F32),
            pltpu.VMEM((192, 640), BF),
            pltpu.VMEM((2, 80, 640), BF),
            pltpu.VMEM((2, 288, 128), BF),
            pltpu.VMEM((4, 128, 128), BF),
            pltpu.VMEM((2, 80, 640), BF),
            pltpu.VMEM((2, 288, 128), BF),
            pltpu.VMEM((4, 128, 128), BF),
            pltpu.VMEM((2, 6, 128, 128), F32),
            pltpu.VMEM((2, 6, 128, 128), F32),
            pltpu.VMEM((2, 6, 128, 128), F32),
            pltpu.VMEM((6, 224, 256), BF),
            pltpu.VMEM((6, 224, 256), BF),
            pltpu.VMEM((2, 192, 256), BF),
            pltpu.VMEM((224, 256), BF),
            pltpu.VMEM((512, 256), BF),
            pltpu.VMEM((256, 256), BF),
            pltpu.VMEM((256, 1024), BF),
            pltpu.VMEM((256, 256), BF),
            pltpu.VMEM((256, 128), BF),
            pltpu.VMEM((256, 128), BF),
            pltpu.VMEM((256, 512), BF),
            pltpu.VMEM((256, 256), BF),
            pltpu.VMEM((1024, 256), BF),
            pltpu.VMEM((256, 128), BF),
            pltpu.SemaphoreType.DMA((5,)),
            pltpu.SemaphoreType.DMA,
            pltpu.SemaphoreType.DMA,
            pltpu.SemaphoreType.REGULAR((4,)),
        ],
        compiler_params=pltpu.CompilerParams(
            collective_id=0, has_side_effects=True, vmem_limit_bytes=24 * 1024 * 1024
        ),
        name="fish_step",
    )(
        pltpu.with_memory_space_constraint(velocity, pltpu.HBM),
        pltpu.with_memory_space_constraint(marker_cell.reshape(3, 16, 128), pltpu.HBM),
        pltpu.with_memory_space_constraint(marker_frac.reshape(2, 16, 128), pltpu.HBM),
        pltpu.with_memory_space_constraint(marker_force.reshape(2, 16, 128), pltpu.HBM),
        pltpu.with_memory_space_constraint(fish_owner.reshape(6, 128), pltpu.HBM),
    )
    out_v, out_m = pl.pallas_call(
        sampling,
        out_shape=(
            jax.ShapeDtypeStruct((4, 2, 64, 128), F32),
            jax.ShapeDtypeStruct((2, 16, 128), F32),
        ),
        in_specs=[vm] * 4,
        out_specs=(pl.BlockSpec(memory_space=pltpu.HBM), vm),
        scratch_shapes=[pltpu.SemaphoreType.DMA],
        compiler_params=pltpu.CompilerParams(vmem_limit_bytes=8 * 1024 * 1024),
        name="fish_sample",
    )(v, ta, wy_hot, wx_hot)
    return out_v, out_m.reshape(2, 1, 1, 2048)


def solution(mesh):
    placed = (
        P(None, None, "gx", "gy"),
        P(None, "gx", "gy", None),
        P(None, "gx", "gy", None),
        P(None, "gx", "gy", None),
        P(),
    )
    return jax.shard_map(
        body,
        mesh=mesh,
        in_specs=placed,
        out_specs=(P(None, None, "gx", "gy"), P(None, "gx", "gy", None)),
        check_vma=False,
    )
```

```python
import functools
import math

import jax
import jax.numpy as jnp
from jax import lax
from jax.experimental import pallas as pl
from jax.experimental.pallas import tpu as pltpu
from jax.sharding import PartitionSpec as P

MARGIN = 16
FISH_MARK = 1024
COURANT = 0.25
VISCOUS = 1.5
LANES = 128
BF = jnp.bfloat16
F32 = jnp.float32

SIDES = [(1, 0), (-1, 0), (0, 1), (0, -1), (1, 1), (-1, 1), (1, -1), (-1, -1)]
UPPER = [(0, 1), (1, 0), (1, 1), (1, -1)]


def half_angle(t):
    z = t * (0.5 * math.pi)
    q = z * z
    s = 1.0 / math.factorial(13)
    for n in (11, 9, 7, 5, 3, 1):
        s = s * q + (-1.0) ** ((n - 1) // 2) / math.factorial(n)
    c = 1.0 / math.factorial(12)
    for n in (10, 8, 6, 4, 2, 0):
        c = c * q + (-1.0) ** (n // 2) / math.factorial(n)
    return s * z, c


def weights(t):
    s, c = half_angle(t)
    return (0.25 * (1.0 - s), 0.25 * (1.0 + c), 0.25 * (1.0 + s), 0.25 * (1.0 - c))


def chain(d, values, zero):
    out = jnp.where(d == 2.0, values[3], zero)
    out = jnp.where(d == 1.0, values[2], out)
    out = jnp.where(d == 0.0, values[1], out)
    return jnp.where(d == -1.0, values[0], out)


def pick(ref, source):
    rows, columns = ref.shape
    n = lax.broadcasted_iota(jnp.int32, (16, columns), 1)
    below = source(n) - lax.broadcasted_iota(jnp.int32, (16, columns), 0)
    for lo in range(0, rows, 16):
        ref[lo : lo + 16, :] = jnp.where(below == lo, 1.0, 0.0).astype(BF)


def matrices(w_in, w_out, w_place, w_adv, w_t, w_s, w_fix, w_strip, w_edge, w_cut):
    def inner_of(n):
        p, l = n % 32, (n // 32) % 4
        up = jnp.where(p < 26, 128 * l + p + 102, -1)
        down = jnp.where(p < 6, -1, 128 * l + p - 6)
        return jnp.where(n < 128, up, down)

    def outer_of(n):
        i, c, l = n % 16, (n // 16) % 2, (n // 32) % 4
        return 128 * c + 16 * l + i + jnp.where(n < 128, 64, 0)

    def place_of(n):
        y, l, c = n % 128, (n // 128) % 4, n // 512
        at = 32 * l + 16 * c
        return jnp.where(y < 16, at + y, jnp.where(y >= 112, 128 + at + y - 112, -1))

    def fix_of(n):
        y, l = n % 128, n // 128
        return jnp.where(
            y < 3, 32 * l + 26 + y, jnp.where(y >= 125, 128 + 32 * l + y - 122, -1)
        )

    def strip_of(n):
        j, l, side = n % 32, (n // 32) % 4, n // 128
        i = j - jnp.where(side == 0, 10, 6)
        return jnp.where((i >= 0) & (i < 16), 64 * side + 16 * l + i, -1)

    def edge_of(n):
        j, l = n % 32, (n // 32) % 4
        low = jnp.where(j >= 26, 256 * l + j - 26, -1)
        return jnp.where(n < 128, low, jnp.where(j < 6, 256 * l + j + 122, -1))

    def cut_of(n):
        i, l, side = n % 16, (n // 16) % 4, n // 64
        return 128 * side + 32 * l + i + jnp.where(side == 0, 10, 6)

    for half in range(2):
        pick(w_strip.at[pl.ds(128 * half, 128)], strip_of)
    for l in range(4):
        for half in range(2):
            rows = pl.ds(256 * l + 128 * half, 128)
            pick(w_edge.at[rows], lambda n: jnp.where(edge_of(n) // 256 == l, edge_of(n) - 256 * l, -1))
    pick(w_cut, cut_of)
    pick(w_in, inner_of)
    pick(w_out, outer_of)
    pick(w_place, place_of)
    pick(w_fix, fix_of)
    y = lax.broadcasted_iota(jnp.int32, (16, LANES), 1)
    r = lax.broadcasted_iota(jnp.int32, (16, LANES), 0)

    def one(of):
        return jnp.where(of == r, 1.0, 0.0)

    for lo in range(0, 256, 16):
        base = lo % LANES
        here, prev, after = one(y - base), one((y + 127) % 128 - base), one((y + 1) % 128 - base)
        w_adv[lo : lo + 16, 0:128] = (here - prev).astype(BF)
        w_adv[lo : lo + 16, 128:256] = (after - here).astype(BF)
        w_t[lo : lo + 16, :] = (prev + after).astype(BF)
        upper = one(jnp.where(y < 96, y + 32, y) - base)
        lower = one(jnp.where(y >= 32, y - 32, y) - base)
        w_s[lo : lo + 16, :] = (prev + after + upper + lower).astype(BF)


def pieces(v):
    high = v.astype(BF)
    return high, (v - high.astype(F32)).astype(BF)


def kernel(
    nx, ny,
    vel_h, cell_h, frac_h, force_h, owner_h,
    out_v, ta, wy_hot, wx_hot,
    vel, cell, frac, force, owner,
    q32, left, mv, mvb, px, py, pc, rx, ry, rc,
    mt, ca, w1, sp, ws, ends_in, beyond, w_in, w_out, w_place, w_adv, w_t, w_s, w_fix,
    w_strip, w_edge, w_cut,
    in_sem, send1, recv1, here_sem,
):
    ix = lax.axis_index("gx")
    iy = lax.axis_index("gy")

    def at(dx, dy):
        return {"gx": lax.rem(ix + dx + nx, nx), "gy": lax.rem(iy + dy + ny, ny)}

    loads = []
    for n, (src, dst) in enumerate(
        ((cell_h, cell), (frac_h, frac), (force_h, force), (owner_h, owner), (vel_h, vel))
    ):
        loads.append(pltpu.make_async_copy(src, dst, in_sem.at[n]))
        loads[-1].start()
    barrier = pltpu.get_barrier_semaphore()
    for dx, dy in UPPER:
        pl.semaphore_signal(
            barrier, inc=1, device_id=at(-dx, -dy), device_id_type=pl.DeviceIdType.MESH
        )
    matrices(w_in, w_out, w_place, w_adv, w_t, w_s, w_fix, w_strip, w_edge, w_cut)
    for load in loads[:4]:
        load.wait()

    mine = jnp.where(owner[...] == ix * ny + iy, 1.0, 0.0)
    count = jnp.sum(jnp.sum(mine, axis=1, keepdims=True), axis=0, keepdims=True)
    slot = lax.broadcasted_iota(jnp.int32, (16, LANES), 0) * LANES + lax.broadcasted_iota(
        jnp.int32, (16, LANES), 1
    )
    alive = jnp.where(slot.astype(F32) < FISH_MARK * count, 1.0, 0.0)
    rel_x = lax.rem(cell[0] - ix * 64 + (MARGIN + nx * 64), nx * 64)
    rel_y = lax.rem(cell[1] - iy * 128 + (MARGIN + ny * 128), ny * 128) - MARGIN
    q32[0] = rel_x.astype(F32)
    q32[1] = rel_y.astype(F32)
    wx = weights(frac[0])
    wy = weights(frac[1])
    for k in range(4):
        q32[2 + k] = wx[k]
        q32[6 + k] = wy[k]
        for c in range(2):
            q32[10 + 4 * c + k] = force[c] * alive * wx[k]
        q32[18 + k] = jnp.where(cell[2] == k, 1.0, 0.0)
    q32[22] = alive

    loads[4].wait()

    rows16 = lax.broadcasted_iota(jnp.int32, (16, LANES), 0).astype(F32)
    zero16 = jnp.zeros((16, LANES), BF)
    strips = ((512, -16.0), (576, 128.0))

    def operands(r, _):
        lanes = slice(r * LANES, r * LANES + LANES)

        def row(n):
            return jnp.broadcast_to(q32[n, r : r + 1, :], (16, LANES))

        dx0 = (rows16 - row(0)).astype(BF)
        lw = [[row(10 + 4 * c + k).astype(BF) for k in range(4)] for c in range(2)]
        for b in range(6):
            d = dx0 + jnp.asarray(16.0 * b, BF)
            for c in range(2):
                left[pl.ds(96 * c + 16 * b, 16), lanes] = chain(d, lw[c], zero16)
        dy0 = (rows16 - row(1)).astype(BF)
        yw = [row(6 + k).astype(BF) for k in range(4)]
        lv = [row(18 + k).astype(BF) for k in range(4)]
        for b in range(10):
            base, step = (16.0 * b, 128) if b < 8 else (strips[b - 8][1], 16)
            first_row = 16 * b if b < 8 else strips[b - 8][0]
            d = dy0 + jnp.asarray(base, BF)
            w = chain(d, yw, zero16)
            for l in range(4):
                wy_hot[pl.ds(first_row + step * l, 16), lanes] = w * lv[l]
        return 0

    for r in range(16):
        operands(r, 0)

    both = lax.dot_general(
        left[...], wy_hot[...], (((1,), (1,)), ((), ())), preferred_element_type=F32
    )
    for c in range(2):
        spread = both[96 * c : 96 * c + 96]
        mv[c] = spread
        for l in range(4):
            ls = slice(128 * l, 128 * l + 128)
            v = vel[l, c]
            mv[c, 16:80, ls] = spread[16:80, ls] + v

    for c in range(2):
        mvb[96 * c : 96 * c + 96, :] = mv[c].astype(BF)
    inner = jnp.dot(mvb[:, 0:512], w_in[...], preferred_element_type=F32)
    outer = jnp.dot(
        jnp.concatenate([mvb[0:96, 512:640], mvb[96:192, 512:640]], axis=1),
        w_out[...],
        preferred_element_type=F32,
    )
    filler = jnp.zeros((8, LANES), F32)
    for side in range(2):
        ls = slice(128 * side, 128 * side + 128)
        parts = [inner[0:96, ls], inner[96:192, ls], outer[:, ls]]
        py[side] = jnp.concatenate(parts, axis=0).astype(BF)
        for n in range(4):
            dx, dy = SIDES[4 + n]
            if (0 if dy == 1 else 1) == side:
                lo = 56 if dx == 1 else 0
                pc[n] = jnp.concatenate([p[lo : lo + 40] for p in parts] + [filler], axis=0).astype(BF)
    for n, lo in enumerate((56, 0)):
        px[n] = jnp.concatenate([mv[0, lo : lo + 40, :], mv[1, lo : lo + 40, :]], axis=0).astype(BF)

    pl.semaphore_wait(barrier, 4)
    for n, (dx, dy) in enumerate(UPPER):
        pl.semaphore_signal(
            here_sem.at[n], inc=1, device_id=at(dx, dy), device_id_type=pl.DeviceIdType.MESH
        )

    def send(src, dst, dx, dy):
        copy = pltpu.make_async_remote_copy(
            src_ref=src, dst_ref=dst, send_sem=send1, recv_sem=recv1,
            device_id=at(dx, dy), device_id_type=pl.DeviceIdType.MESH,
        )
        copy.start()

    def send_to(dx, dy):
        n = SIDES.index((dx, dy))
        if n < 2:
            send(px.at[n], rx.at[n], dx, dy)
        elif n < 4:
            send(py.at[n - 2], ry.at[n - 2], dx, dy)
        else:
            send(pc.at[n - 4], rc.at[n - 4], dx, dy)

    for dx, dy in UPPER[2:] + UPPER[:2][::-1]:
        send_to(dx, dy)

    for n, (dx, dy) in enumerate(UPPER):
        pl.semaphore_wait(here_sem.at[n], 1)
        send_to(-dx, -dy)

    rows8 = lax.broadcasted_iota(jnp.int32, (8, LANES), 0).astype(F32)

    def x_hot(r, _):
        lanes = pl.ds(pl.multiple_of(r * LANES, LANES), LANES)

        def row(n):
            return jnp.broadcast_to(q32[n, pl.ds(r, 1), :], (8, LANES))

        d = rows8 - row(0)
        ww = [row(2 + k) * row(22) for k in range(4)]
        for b in range(12):
            wx_hot[pl.ds(8 * b, 8), lanes] = chain(d + 8.0 * b, ww, 0.0)
        return 0

    lax.fori_loop(0, 16, x_hot, 0)
    for ref in (mt, ca, w1):
        for c in range(2):
            for t in range(6):
                ref[c, t, 0:8, :] = jnp.zeros((8, LANES), F32)
                ref[c, t, 120:128, :] = jnp.zeros((8, LANES), F32)

    everything = w_edge.at[pl.ds(0, 944)]
    pltpu.make_async_copy(everything, everything, recv1).wait()
    pltpu.make_async_copy(everything, everything, send1).wait()

    corner = {}
    for n in range(4):
        dx, dy = SIDES[4 + n]
        corner[0 if dx == 1 else 1, 0 if dy == 1 else 1] = n

    def joined(mid, first, last):
        return [
            first[0:8], mid[0:32] + first[8:40], mid[32:64], mid[64:96] + last[0:32], last[32:40]
        ]

    ryf = [ry[side].astype(F32) for side in range(2)]
    rcf = [rc[n].astype(F32) for n in range(4)]
    rxf = [rx[n].astype(F32) for n in range(2)]
    from_y = [[r[96 * p : 96 * p + 96] for p in range(3)] for r in ryf]
    from_c = [[r[40 * p : 40 * p + 40] for p in range(3)] for r in rcf]
    placed = jnp.dot(
        jnp.concatenate(
            [
                jnp.concatenate([ry[side, 192:288, :] for side in range(2)], axis=1),
                jnp.concatenate([rc[corner[0, side], 80:128, :] for side in range(2)], axis=1),
                jnp.concatenate([rc[corner[1, side], 80:128, :] for side in range(2)], axis=1),
            ],
            axis=0,
        ),
        w_place[...],
        preferred_element_type=F32,
    )

    def keep_pieces(t, c, a):
        mt[c, t, 8:120, :] = a
        high, low = pieces(a)
        sp[t, 112 * c : 112 * c + 112, 0:128] = high
        sp[t, 112 * c : 112 * c + 112, 128:256] = low

    def assemble(t):
        for c in range(2):
            ls = slice(128 * t, 128 * t + 128)
            first, last = (r[40 * c : 40 * c + 40, ls] for r in rxf)
            ps = slice(512 * c + 128 * t, 512 * c + 128 * t + 128)
            parts = joined(
                mv[c, :, ls] + placed[0:96, ps],
                first + placed[96:136, ps],
                last + placed[144:184, ps],
            )
            keep_pieces(t, c, jnp.concatenate(parts, axis=0))

    def outside_pieces():
        for c in range(2):
            first, last = (r[40 * c : 40 * c + 40, 512:640] for r in rxf)
            whole = jnp.concatenate(joined(mv[c, :, 512:640], first, last), axis=0)
            high, low = pieces(whole)
            beyond[112 * c : 112 * c + 112, 0:128] = high
            beyond[112 * c : 112 * c + 112, 128:256] = low

    def assemble_strips():
        total = jnp.dot(beyond[...], w_strip[...], preferred_element_type=F32)
        for l in range(4):
            total = total + jnp.dot(
                sp[l], w_edge[256 * l : 256 * l + 256, :], preferred_element_type=F32
            )
        for side in range(2):
            for c in range(2):
                inside = joined(
                    from_y[side][c], from_c[corner[0, side]][c], from_c[corner[1, side]][c]
                )
                own = total[112 * c : 112 * c + 112, 128 * side : 128 * side + 128]
                keep_pieces(4 + side, c, own + jnp.concatenate(inside, axis=0))

    def advect(t):
        steps = jnp.dot(sp[t], w_adv[...], preferred_element_type=F32)
        for lo in range(0, 112, 16):
            here = slice(lo + 8, lo + 24)
            a = COURANT * mt[0, t, here, :]
            b = COURANT * mt[1, t, here, :]
            forth, right = a > 0.0, b > 0.0
            for c in range(2):
                q = mt[c, t, here, :]
                row = 112 * c + lo
                step_x = jnp.where(
                    forth, q - mt[c, t, lo + 7 : lo + 23, :], mt[c, t, lo + 9 : lo + 25, :] - q
                )
                step_y = jnp.where(
                    right, steps[row : row + 16, 0:128], steps[row : row + 16, 128:256]
                )
                value = q - (a * step_x + b * step_y)
                ca[c, t, here, :] = value
                high, low = pieces(value)
                ws[t, row : row + 16, 0:128] = high
                ws[t, row : row + 16, 128:256] = low

    scale = 1.0 / (1.0 + 6.0 * VISCOUS)

    def sweep(ref, beside, t, c, lo, row):
        here = slice(lo + 8, lo + 24)
        total = ref[c, t, lo + 7 : lo + 23, :] + ref[c, t, lo + 9 : lo + 25, :]
        total = total + beside[row : row + 16]
        if t < 4:
            total = total + (ref[c, min(t + 1, 3), here, :] + ref[c, max(t - 1, 0), here, :])
        return scale * ca[c, t, here, :] + (scale * VISCOUS) * total

    def first_sweep(t):
        beside = jnp.dot(ws[t], (w_t if t < 4 else w_s)[...], preferred_element_type=F32)
        for c in range(2):
            for lo in range(0, 112, 16):
                value = sweep(ca, beside, t, c, lo, 112 * c + lo)
                w1[c, t, lo + 8 : lo + 24, :] = value
                high, low = pieces(value)
                sp[t, 112 * c + lo : 112 * c + lo + 16, 0:128] = high
                sp[t, 112 * c + lo : 112 * c + lo + 16, 128:256] = low

    def second_sweep(t, c, beside):
        values = [sweep(w1, beside, t, c, lo, 112 * c + lo) for lo in range(0, 112, 16)]
        return jnp.concatenate(values, axis=0)[8:104]

    outside_pieces()
    for t in range(4):
        assemble(t)
    assemble_strips()
    for t in range(6):
        advect(t)
    first_sweep(4)
    first_sweep(5)
    for t in (4, 5):
        ls = slice(128 * (t - 4), 128 * (t - 4) + 128)
        beside = jnp.dot(sp[t], w_s[...], preferred_element_type=F32)
        for c in range(2):
            whole = second_sweep(t, c, beside)
            high, low = pieces(whole)
            ends_in[0, 96 * c : 96 * c + 96, ls] = high
            ends_in[1, 96 * c : 96 * c + 96, ls] = low
    cut = jnp.dot(ends_in[0], w_cut[...], preferred_element_type=F32)
    ta[:, 512:640] = cut.astype(BF)
    first_sweep(0)
    first_sweep(1)
    first_sweep(2)
    first_sweep(3)
    ends = jnp.dot(ends_in[0], w_fix[...], preferred_element_type=F32)
    ends = ends + jnp.dot(ends_in[1], w_fix[...], preferred_element_type=F32)
    lane = lax.broadcasted_iota(jnp.int32, (96, LANES), 1)
    inside = (lane >= 3) & (lane < 125)
    for t in range(4):
        ls = slice(128 * t, 128 * t + 128)
        beside = jnp.dot(sp[t], w_t[...], preferred_element_type=F32)
        for c in range(2):
            whole = second_sweep(t, c, beside)
            whole = jnp.where(inside, whole, ends[96 * c : 96 * c + 96, ls])
            out_v[t, c] = whole[16:80]
            ta[96 * c : 96 * c + 96, ls] = whole.astype(BF)


def sampling(v, ta, wy_hot, wx_hot, out_v, out_m, out_sem):
    copy = pltpu.make_async_copy(v, out_v, out_sem)
    copy.start()
    for r in range(4):
        lanes = slice(512 * r, 512 * r + 512)
        both = jnp.dot(ta[...], wy_hot[:, lanes], preferred_element_type=F32)
        for c in range(2):
            part = both[96 * c : 96 * c + 96]
            summed = jnp.sum(part * wx_hot[:, lanes], axis=0, keepdims=True)
            for i in range(4):
                out_m[c, 4 * r + i : 4 * r + i + 1, :] = summed[:, LANES * i : LANES * i + LANES]
    copy.wait()


def body(velocity, marker_cell, marker_frac, marker_force, fish_owner):
    nx = lax.axis_size("gx")
    ny = lax.axis_size("gy")
    vm = pl.BlockSpec(memory_space=pltpu.VMEM)
    v, ta, wy_hot, wx_hot = pl.pallas_call(
        functools.partial(kernel, nx, ny),
        out_shape=(
            jax.ShapeDtypeStruct((4, 2, 64, 128), F32),
            jax.ShapeDtypeStruct((192, 640), BF),
            jax.ShapeDtypeStruct((640, 2048), BF),
            jax.ShapeDtypeStruct((96, 2048), F32),
        ),
        in_specs=[pl.BlockSpec(memory_space=pltpu.HBM)] * 5,
        out_specs=(vm, vm, vm, vm),
        scratch_shapes=[
            pltpu.VMEM((4, 2, 64, 128), F32),
            pltpu.VMEM((3, 16, 128), jnp.int32),
            pltpu.VMEM((2, 16, 128), F32),
            pltpu.VMEM((2, 16, 128), F32),
            pltpu.VMEM((6, 128), jnp.int32),
            pltpu.VMEM((23, 16, 128), F32),
            pltpu.VMEM((192, 2048), BF),
            pltpu.VMEM((2, 96, 640), F32),
            pltpu.VMEM((192, 640), BF),
            pltpu.VMEM((2, 80, 640), BF),
            pltpu.VMEM((2, 288, 128), BF),
            pltpu.VMEM((4, 128, 128), BF),
            pltpu.VMEM((2, 80, 640), BF),
            pltpu.VMEM((2, 288, 128), BF),
            pltpu.VMEM((4, 128, 128), BF),
            pltpu.VMEM((2, 6, 128, 128), F32),
            pltpu.VMEM((2, 6, 128, 128), F32),
            pltpu.VMEM((2, 6, 128, 128), F32),
            pltpu.VMEM((6, 224, 256), BF),
            pltpu.VMEM((6, 224, 256), BF),
            pltpu.VMEM((2, 192, 256), BF),
            pltpu.VMEM((224, 256), BF),
            pltpu.VMEM((512, 256), BF),
            pltpu.VMEM((256, 256), BF),
            pltpu.VMEM((256, 1024), BF),
            pltpu.VMEM((256, 256), BF),
            pltpu.VMEM((256, 128), BF),
            pltpu.VMEM((256, 128), BF),
            pltpu.VMEM((256, 512), BF),
            pltpu.VMEM((256, 256), BF),
            pltpu.VMEM((1024, 256), BF),
            pltpu.VMEM((256, 128), BF),
            pltpu.SemaphoreType.DMA((5,)),
            pltpu.SemaphoreType.DMA,
            pltpu.SemaphoreType.DMA,
            pltpu.SemaphoreType.REGULAR((4,)),
        ],
        compiler_params=pltpu.CompilerParams(
            collective_id=0, has_side_effects=True, vmem_limit_bytes=24 * 1024 * 1024
        ),
        name="fish_step",
    )(
        pltpu.with_memory_space_constraint(velocity, pltpu.HBM),
        pltpu.with_memory_space_constraint(marker_cell.reshape(3, 16, 128), pltpu.HBM),
        pltpu.with_memory_space_constraint(marker_frac.reshape(2, 16, 128), pltpu.HBM),
        pltpu.with_memory_space_constraint(marker_force.reshape(2, 16, 128), pltpu.HBM),
        pltpu.with_memory_space_constraint(fish_owner.reshape(6, 128), pltpu.HBM),
    )
    out_v, out_m = pl.pallas_call(
        sampling,
        out_shape=(
            jax.ShapeDtypeStruct((4, 2, 64, 128), F32),
            jax.ShapeDtypeStruct((2, 16, 128), F32),
        ),
        in_specs=[vm] * 4,
        out_specs=(pl.BlockSpec(memory_space=pltpu.HBM), vm),
        scratch_shapes=[pltpu.SemaphoreType.DMA],
        compiler_params=pltpu.CompilerParams(vmem_limit_bytes=8 * 1024 * 1024),
        name="fish_sample",
    )(v, ta, wy_hot, wx_hot)
    return out_v, out_m.reshape(2, 1, 1, 2048)


def solution(mesh):
    placed = (
        P(None, None, "gx", "gy"),
        P(None, "gx", "gy", None),
        P(None, "gx", "gy", None),
        P(None, "gx", "gy", None),
        P(),
    )
    return jax.shard_map(
        body,
        mesh=mesh,
        in_specs=placed,
        out_specs=(P(None, None, "gx", "gy"), P(None, "gx", "gy", None)),
        check_vma=False,
    )
```

```python
import functools
import math

import jax
import jax.numpy as jnp
from jax import lax
from jax.experimental import pallas as pl
from jax.experimental.pallas import tpu as pltpu
from jax.sharding import PartitionSpec as P

MARGIN = 16
FISH_MARK = 1024
COURANT = 0.25
VISCOUS = 1.5
LANES = 128
BF = jnp.bfloat16
F32 = jnp.float32

SIDES = [(1, 0), (-1, 0), (0, 1), (0, -1), (1, 1), (-1, 1), (1, -1), (-1, -1)]
UPPER = [(0, 1), (1, 0), (1, 1), (1, -1)]


def half_angle(t):
    z = t * (0.5 * math.pi)
    q = z * z
    s = 1.0 / math.factorial(13)
    for n in (11, 9, 7, 5, 3, 1):
        s = s * q + (-1.0) ** ((n - 1) // 2) / math.factorial(n)
    c = 1.0 / math.factorial(12)
    for n in (10, 8, 6, 4, 2, 0):
        c = c * q + (-1.0) ** (n // 2) / math.factorial(n)
    return s * z, c


def weights(t):
    s, c = half_angle(t)
    return (0.25 * (1.0 - s), 0.25 * (1.0 + c), 0.25 * (1.0 + s), 0.25 * (1.0 - c))


def chain(d, values, zero):
    out = jnp.where(d == 2.0, values[3], zero)
    out = jnp.where(d == 1.0, values[2], out)
    out = jnp.where(d == 0.0, values[1], out)
    return jnp.where(d == -1.0, values[0], out)


def pick(ref, source):
    rows, columns = ref.shape
    n = lax.broadcasted_iota(jnp.int32, (16, columns), 1)
    below = source(n) - lax.broadcasted_iota(jnp.int32, (16, columns), 0)
    for lo in range(0, rows, 16):
        ref[lo : lo + 16, :] = jnp.where(below == lo, 1.0, 0.0).astype(BF)


def matrices(w_in, w_out, w_place, w_adv, w_t, w_s, w_fix, w_strip, w_edge, w_cut):
    def inner_of(n):
        p, l = n % 32, (n // 32) % 4
        up = jnp.where(p < 26, 128 * l + p + 102, -1)
        down = jnp.where(p < 6, -1, 128 * l + p - 6)
        return jnp.where(n < 128, up, down)

    def outer_of(n):
        i, c, l = n % 16, (n // 16) % 2, (n // 32) % 4
        return 128 * c + 16 * l + i + jnp.where(n < 128, 64, 0)

    def place_of(n):
        y, l, c = n % 128, (n // 128) % 4, n // 512
        at = 32 * l + 16 * c
        return jnp.where(y < 16, at + y, jnp.where(y >= 112, 128 + at + y - 112, -1))

    def fix_of(n):
        y, l = n % 128, n // 128
        return jnp.where(
            y < 3, 32 * l + 26 + y, jnp.where(y >= 125, 128 + 32 * l + y - 122, -1)
        )

    def strip_of(n):
        j, l, side = n % 32, (n // 32) % 4, n // 128
        i = j - jnp.where(side == 0, 10, 6)
        return jnp.where((i >= 0) & (i < 16), 64 * side + 16 * l + i, -1)

    def edge_of(n):
        j, l = n % 32, (n // 32) % 4
        low = jnp.where(j >= 26, 256 * l + j - 26, -1)
        return jnp.where(n < 128, low, jnp.where(j < 6, 256 * l + j + 122, -1))

    def cut_of(n):
        i, l, side = n % 16, (n // 16) % 4, n // 64
        return 128 * side + 32 * l + i + jnp.where(side == 0, 10, 6)

    for half in range(2):
        pick(w_strip.at[pl.ds(128 * half, 128)], strip_of)
    for l in range(4):
        for half in range(2):
            rows = pl.ds(256 * l + 128 * half, 128)
            pick(w_edge.at[rows], lambda n: jnp.where(edge_of(n) // 256 == l, edge_of(n) - 256 * l, -1))
    pick(w_cut, cut_of)
    pick(w_in, inner_of)
    pick(w_out, outer_of)
    pick(w_place, place_of)
    pick(w_fix, fix_of)
    y = lax.broadcasted_iota(jnp.int32, (16, LANES), 1)
    r = lax.broadcasted_iota(jnp.int32, (16, LANES), 0)

    def one(of):
        return jnp.where(of == r, 1.0, 0.0)

    for lo in range(0, 256, 16):
        base = lo % LANES
        here, prev, after = one(y - base), one((y + 127) % 128 - base), one((y + 1) % 128 - base)
        w_adv[lo : lo + 16, 0:128] = (here - prev).astype(BF)
        w_adv[lo : lo + 16, 128:256] = (after - here).astype(BF)
        w_t[lo : lo + 16, :] = (prev + after).astype(BF)
        upper = one(jnp.where(y < 96, y + 32, y) - base)
        lower = one(jnp.where(y >= 32, y - 32, y) - base)
        w_s[lo : lo + 16, :] = (prev + after + upper + lower).astype(BF)


def pieces(v):
    high = v.astype(BF)
    return high, (v - high.astype(F32)).astype(BF)


def kernel(
    nx, ny,
    vel_h, cell_h, frac_h, force_h, owner_h,
    out_v, ta, wy_hot, wx_hot,
    vel, cell, frac, force, owner,
    q32, left, mv, mvb, px, py, pc, rx, ry, rc,
    mt, ca, w1, sp, ws, ends_in, beyond, w_in, w_out, w_place, w_adv, w_t, w_s, w_fix,
    w_strip, w_edge, w_cut,
    in_sem, send1, recv1, here_sem,
):
    ix = lax.axis_index("gx")
    iy = lax.axis_index("gy")

    def at(dx, dy):
        return {"gx": lax.rem(ix + dx + nx, nx), "gy": lax.rem(iy + dy + ny, ny)}

    loads = []
    for n, (src, dst) in enumerate(
        ((cell_h, cell), (frac_h, frac), (force_h, force), (owner_h, owner), (vel_h, vel))
    ):
        loads.append(pltpu.make_async_copy(src, dst, in_sem.at[n]))
        loads[-1].start()
    barrier = pltpu.get_barrier_semaphore()
    for dx, dy in UPPER:
        pl.semaphore_signal(
            barrier, inc=1, device_id=at(-dx, -dy), device_id_type=pl.DeviceIdType.MESH
        )
    matrices(w_in, w_out, w_place, w_adv, w_t, w_s, w_fix, w_strip, w_edge, w_cut)
    for load in loads[:4]:
        load.wait()

    mine = jnp.where(owner[...] == ix * ny + iy, 1.0, 0.0)
    count = jnp.sum(jnp.sum(mine, axis=1, keepdims=True), axis=0, keepdims=True)
    slot = lax.broadcasted_iota(jnp.int32, (16, LANES), 0) * LANES + lax.broadcasted_iota(
        jnp.int32, (16, LANES), 1
    )
    alive = jnp.where(slot.astype(F32) < FISH_MARK * count, 1.0, 0.0)
    rel_x = lax.rem(cell[0] - ix * 64 + (MARGIN + nx * 64), nx * 64)
    rel_y = lax.rem(cell[1] - iy * 128 + (MARGIN + ny * 128), ny * 128) - MARGIN
    q32[0] = rel_x.astype(F32)
    q32[1] = rel_y.astype(F32)
    wx = weights(frac[0])
    wy = weights(frac[1])
    for k in range(4):
        q32[2 + k] = wx[k]
        q32[6 + k] = wy[k]
        for c in range(2):
            q32[10 + 4 * c + k] = force[c] * alive * wx[k]
        q32[18 + k] = jnp.where(cell[2] == k, 1.0, 0.0)
    q32[22] = alive

    loads[4].wait()

    rows16 = lax.broadcasted_iota(jnp.int32, (16, LANES), 0).astype(F32)
    zero16 = jnp.zeros((16, LANES), BF)
    strips = ((512, -16.0), (576, 128.0))

    def operands(r, _):
        lanes = slice(r * LANES, r * LANES + LANES)

        def row(n):
            return jnp.broadcast_to(q32[n, r : r + 1, :], (16, LANES))

        dx0 = (rows16 - row(0)).astype(BF)
        lw = [[row(10 + 4 * c + k).astype(BF) for k in range(4)] for c in range(2)]
        for b in range(6):
            d = dx0 + jnp.asarray(16.0 * b, BF)
            for c in range(2):
                left[pl.ds(96 * c + 16 * b, 16), lanes] = chain(d, lw[c], zero16)
        dy0 = (rows16 - row(1)).astype(BF)
        yw = [row(6 + k).astype(BF) for k in range(4)]
        lv = [row(18 + k).astype(BF) for k in range(4)]
        for b in range(10):
            base, step = (16.0 * b, 128) if b < 8 else (strips[b - 8][1], 16)
            first_row = 16 * b if b < 8 else strips[b - 8][0]
            d = dy0 + jnp.asarray(base, BF)
            w = chain(d, yw, zero16)
            for l in range(4):
                wy_hot[pl.ds(first_row + step * l, 16), lanes] = w * lv[l]
        return 0

    for r in range(16):
        operands(r, 0)

    both = lax.dot_general(
        left[...], wy_hot[...], (((1,), (1,)), ((), ())), preferred_element_type=F32
    )
    for c in range(2):
        spread = both[96 * c : 96 * c + 96]
        mv[c] = spread
        for l in range(4):
            ls = slice(128 * l, 128 * l + 128)
            v = vel[l, c]
            mv[c, 16:80, ls] = spread[16:80, ls] + v

    for c in range(2):
        mvb[96 * c : 96 * c + 96, :] = mv[c].astype(BF)
    inner = jnp.dot(mvb[:, 0:512], w_in[...], preferred_element_type=F32)
    outer = jnp.dot(
        jnp.concatenate([mvb[0:96, 512:640], mvb[96:192, 512:640]], axis=1),
        w_out[...],
        preferred_element_type=F32,
    )
    filler = jnp.zeros((8, LANES), F32)
    for side in range(2):
        ls = slice(128 * side, 128 * side + 128)
        parts = [inner[0:96, ls], inner[96:192, ls], outer[:, ls]]
        py[side] = jnp.concatenate(parts, axis=0).astype(BF)
        for n in range(4):
            dx, dy = SIDES[4 + n]
            if (0 if dy == 1 else 1) == side:
                lo = 56 if dx == 1 else 0
                pc[n] = jnp.concatenate([p[lo : lo + 40] for p in parts] + [filler], axis=0).astype(BF)
    for n, lo in enumerate((56, 0)):
        px[n] = jnp.concatenate([mv[0, lo : lo + 40, :], mv[1, lo : lo + 40, :]], axis=0).astype(BF)

    pl.semaphore_wait(barrier, 4)
    def send(src, dst, dx, dy):
        copy = pltpu.make_async_remote_copy(
            src_ref=src, dst_ref=dst, send_sem=send1, recv_sem=recv1,
            device_id=at(dx, dy), device_id_type=pl.DeviceIdType.MESH,
        )
        copy.start()

    def send_to(dx, dy):
        n = SIDES.index((dx, dy))
        if n < 2:
            send(px.at[n], rx.at[n], dx, dy)
        elif n < 4:
            send(py.at[n - 2], ry.at[n - 2], dx, dy)
        else:
            send(pc.at[n - 4], rc.at[n - 4], dx, dy)

    for dx, dy in UPPER[2:]:
        send_to(dx, dy)
    for n, (dx, dy) in enumerate(UPPER):
        pl.semaphore_signal(
            here_sem.at[n], inc=1, device_id=at(dx, dy), device_id_type=pl.DeviceIdType.MESH
        )

    for dx, dy in UPPER[:2]:
        send_to(dx, dy)


    for n, (dx, dy) in enumerate(UPPER):
        pl.semaphore_wait(here_sem.at[n], 1)
        send_to(-dx, -dy)

    rows8 = lax.broadcasted_iota(jnp.int32, (8, LANES), 0).astype(F32)

    def x_hot(r, _):
        lanes = pl.ds(pl.multiple_of(r * LANES, LANES), LANES)

        def row(n):
            return jnp.broadcast_to(q32[n, pl.ds(r, 1), :], (8, LANES))

        d = rows8 - row(0)
        ww = [row(2 + k) * row(22) for k in range(4)]
        for b in range(12):
            wx_hot[pl.ds(8 * b, 8), lanes] = chain(d + 8.0 * b, ww, 0.0)
        return 0

    lax.fori_loop(0, 16, x_hot, 0)
    for ref in (mt, ca, w1):
        for c in range(2):
            for t in range(6):
                ref[c, t, 0:8, :] = jnp.zeros((8, LANES), F32)
                ref[c, t, 120:128, :] = jnp.zeros((8, LANES), F32)

    everything = w_edge.at[pl.ds(0, 944)]
    pltpu.make_async_copy(everything, everything, recv1).wait()
    pltpu.make_async_copy(everything, everything, send1).wait()

    corner = {}
    for n in range(4):
        dx, dy = SIDES[4 + n]
        corner[0 if dx == 1 else 1, 0 if dy == 1 else 1] = n

    def joined(mid, first, last):
        return [
            first[0:8], mid[0:32] + first[8:40], mid[32:64], mid[64:96] + last[0:32], last[32:40]
        ]

    ryf = [ry[side].astype(F32) for side in range(2)]
    rcf = [rc[n].astype(F32) for n in range(4)]
    rxf = [rx[n].astype(F32) for n in range(2)]
    from_y = [[r[96 * p : 96 * p + 96] for p in range(3)] for r in ryf]
    from_c = [[r[40 * p : 40 * p + 40] for p in range(3)] for r in rcf]
    placed = jnp.dot(
        jnp.concatenate(
            [
                jnp.concatenate([ry[side, 192:288, :] for side in range(2)], axis=1),
                jnp.concatenate([rc[corner[0, side], 80:128, :] for side in range(2)], axis=1),
                jnp.concatenate([rc[corner[1, side], 80:128, :] for side in range(2)], axis=1),
            ],
            axis=0,
        ),
        w_place[...],
        preferred_element_type=F32,
    )

    def keep_pieces(t, c, a):
        mt[c, t, 8:120, :] = a
        high, low = pieces(a)
        sp[t, 112 * c : 112 * c + 112, 0:128] = high
        sp[t, 112 * c : 112 * c + 112, 128:256] = low

    def assemble(t):
        for c in range(2):
            ls = slice(128 * t, 128 * t + 128)
            first, last = (r[40 * c : 40 * c + 40, ls] for r in rxf)
            ps = slice(512 * c + 128 * t, 512 * c + 128 * t + 128)
            parts = joined(
                mv[c, :, ls] + placed[0:96, ps],
                first + placed[96:136, ps],
                last + placed[144:184, ps],
            )
            keep_pieces(t, c, jnp.concatenate(parts, axis=0))

    def outside_pieces():
        for c in range(2):
            first, last = (r[40 * c : 40 * c + 40, 512:640] for r in rxf)
            whole = jnp.concatenate(joined(mv[c, :, 512:640], first, last), axis=0)
            high, low = pieces(whole)
            beyond[112 * c : 112 * c + 112, 0:128] = high
            beyond[112 * c : 112 * c + 112, 128:256] = low

    def assemble_strips():
        total = jnp.dot(beyond[...], w_strip[...], preferred_element_type=F32)
        for l in range(4):
            total = total + jnp.dot(
                sp[l], w_edge[256 * l : 256 * l + 256, :], preferred_element_type=F32
            )
        for side in range(2):
            for c in range(2):
                inside = joined(
                    from_y[side][c], from_c[corner[0, side]][c], from_c[corner[1, side]][c]
                )
                own = total[112 * c : 112 * c + 112, 128 * side : 128 * side + 128]
                keep_pieces(4 + side, c, own + jnp.concatenate(inside, axis=0))

    def advect(t):
        steps = jnp.dot(sp[t], w_adv[...], preferred_element_type=F32)
        for lo in range(0, 112, 16):
            here = slice(lo + 8, lo + 24)
            a = COURANT * mt[0, t, here, :]
            b = COURANT * mt[1, t, here, :]
            forth, right = a > 0.0, b > 0.0
            for c in range(2):
                q = mt[c, t, here, :]
                row = 112 * c + lo
                step_x = jnp.where(
                    forth, q - mt[c, t, lo + 7 : lo + 23, :], mt[c, t, lo + 9 : lo + 25, :] - q
                )
                step_y = jnp.where(
                    right, steps[row : row + 16, 0:128], steps[row : row + 16, 128:256]
                )
                value = q - (a * step_x + b * step_y)
                ca[c, t, here, :] = value
                high, low = pieces(value)
                ws[t, row : row + 16, 0:128] = high
                ws[t, row : row + 16, 128:256] = low

    scale = 1.0 / (1.0 + 6.0 * VISCOUS)

    def sweep(ref, beside, t, c, lo, row):
        here = slice(lo + 8, lo + 24)
        total = ref[c, t, lo + 7 : lo + 23, :] + ref[c, t, lo + 9 : lo + 25, :]
        total = total + beside[row : row + 16]
        if t < 4:
            total = total + (ref[c, min(t + 1, 3), here, :] + ref[c, max(t - 1, 0), here, :])
        return scale * ca[c, t, here, :] + (scale * VISCOUS) * total

    def first_sweep(t):
        beside = jnp.dot(ws[t], (w_t if t < 4 else w_s)[...], preferred_element_type=F32)
        for c in range(2):
            for lo in range(0, 112, 16):
                value = sweep(ca, beside, t, c, lo, 112 * c + lo)
                w1[c, t, lo + 8 : lo + 24, :] = value
                high, low = pieces(value)
                sp[t, 112 * c + lo : 112 * c + lo + 16, 0:128] = high
                sp[t, 112 * c + lo : 112 * c + lo + 16, 128:256] = low

    def second_sweep(t, c, beside):
        values = [sweep(w1, beside, t, c, lo, 112 * c + lo) for lo in range(0, 112, 16)]
        return jnp.concatenate(values, axis=0)[8:104]

    outside_pieces()
    for t in range(4):
        assemble(t)
    assemble_strips()
    for t in range(6):
        advect(t)
    first_sweep(4)
    first_sweep(5)
    for t in (4, 5):
        ls = slice(128 * (t - 4), 128 * (t - 4) + 128)
        beside = jnp.dot(sp[t], w_s[...], preferred_element_type=F32)
        for c in range(2):
            whole = second_sweep(t, c, beside)
            high, low = pieces(whole)
            ends_in[0, 96 * c : 96 * c + 96, ls] = high
            ends_in[1, 96 * c : 96 * c + 96, ls] = low
    cut = jnp.dot(ends_in[0], w_cut[...], preferred_element_type=F32)
    ta[:, 512:640] = cut.astype(BF)
    first_sweep(0)
    first_sweep(1)
    first_sweep(2)
    first_sweep(3)
    ends = jnp.dot(ends_in[0], w_fix[...], preferred_element_type=F32)
    ends = ends + jnp.dot(ends_in[1], w_fix[...], preferred_element_type=F32)
    lane = lax.broadcasted_iota(jnp.int32, (96, LANES), 1)
    inside = (lane >= 3) & (lane < 125)
    for t in range(4):
        ls = slice(128 * t, 128 * t + 128)
        beside = jnp.dot(sp[t], w_t[...], preferred_element_type=F32)
        for c in range(2):
            whole = second_sweep(t, c, beside)
            whole = jnp.where(inside, whole, ends[96 * c : 96 * c + 96, ls])
            out_v[t, c] = whole[16:80]
            ta[96 * c : 96 * c + 96, ls] = whole.astype(BF)


def sampling(v, ta, wy_hot, wx_hot, out_v, out_m, out_sem):
    copy = pltpu.make_async_copy(v, out_v, out_sem)
    copy.start()
    for r in range(4):
        lanes = slice(512 * r, 512 * r + 512)
        both = jnp.dot(ta[...], wy_hot[:, lanes], preferred_element_type=F32)
        for c in range(2):
            part = both[96 * c : 96 * c + 96]
            summed = jnp.sum(part * wx_hot[:, lanes], axis=0, keepdims=True)
            for i in range(4):
                out_m[c, 4 * r + i : 4 * r + i + 1, :] = summed[:, LANES * i : LANES * i + LANES]
    copy.wait()


def body(velocity, marker_cell, marker_frac, marker_force, fish_owner):
    nx = lax.axis_size("gx")
    ny = lax.axis_size("gy")
    vm = pl.BlockSpec(memory_space=pltpu.VMEM)
    v, ta, wy_hot, wx_hot = pl.pallas_call(
        functools.partial(kernel, nx, ny),
        out_shape=(
            jax.ShapeDtypeStruct((4, 2, 64, 128), F32),
            jax.ShapeDtypeStruct((192, 640), BF),
            jax.ShapeDtypeStruct((640, 2048), BF),
            jax.ShapeDtypeStruct((96, 2048), F32),
        ),
        in_specs=[pl.BlockSpec(memory_space=pltpu.HBM)] * 5,
        out_specs=(vm, vm, vm, vm),
        scratch_shapes=[
            pltpu.VMEM((4, 2, 64, 128), F32),
            pltpu.VMEM((3, 16, 128), jnp.int32),
            pltpu.VMEM((2, 16, 128), F32),
            pltpu.VMEM((2, 16, 128), F32),
            pltpu.VMEM((6, 128), jnp.int32),
            pltpu.VMEM((23, 16, 128), F32),
            pltpu.VMEM((192, 2048), BF),
            pltpu.VMEM((2, 96, 640), F32),
            pltpu.VMEM((192, 640), BF),
            pltpu.VMEM((2, 80, 640), BF),
            pltpu.VMEM((2, 288, 128), BF),
            pltpu.VMEM((4, 128, 128), BF),
            pltpu.VMEM((2, 80, 640), BF),
            pltpu.VMEM((2, 288, 128), BF),
            pltpu.VMEM((4, 128, 128), BF),
            pltpu.VMEM((2, 6, 128, 128), F32),
            pltpu.VMEM((2, 6, 128, 128), F32),
            pltpu.VMEM((2, 6, 128, 128), F32),
            pltpu.VMEM((6, 224, 256), BF),
            pltpu.VMEM((6, 224, 256), BF),
            pltpu.VMEM((2, 192, 256), BF),
            pltpu.VMEM((224, 256), BF),
            pltpu.VMEM((512, 256), BF),
            pltpu.VMEM((256, 256), BF),
            pltpu.VMEM((256, 1024), BF),
            pltpu.VMEM((256, 256), BF),
            pltpu.VMEM((256, 128), BF),
            pltpu.VMEM((256, 128), BF),
            pltpu.VMEM((256, 512), BF),
            pltpu.VMEM((256, 256), BF),
            pltpu.VMEM((1024, 256), BF),
            pltpu.VMEM((256, 128), BF),
            pltpu.SemaphoreType.DMA((5,)),
            pltpu.SemaphoreType.DMA,
            pltpu.SemaphoreType.DMA,
            pltpu.SemaphoreType.REGULAR((4,)),
        ],
        compiler_params=pltpu.CompilerParams(
            collective_id=0, has_side_effects=True, vmem_limit_bytes=24 * 1024 * 1024
        ),
        name="fish_step",
    )(
        pltpu.with_memory_space_constraint(velocity, pltpu.HBM),
        pltpu.with_memory_space_constraint(marker_cell.reshape(3, 16, 128), pltpu.HBM),
        pltpu.with_memory_space_constraint(marker_frac.reshape(2, 16, 128), pltpu.HBM),
        pltpu.with_memory_space_constraint(marker_force.reshape(2, 16, 128), pltpu.HBM),
        pltpu.with_memory_space_constraint(fish_owner.reshape(6, 128), pltpu.HBM),
    )
    out_v, out_m = pl.pallas_call(
        sampling,
        out_shape=(
            jax.ShapeDtypeStruct((4, 2, 64, 128), F32),
            jax.ShapeDtypeStruct((2, 16, 128), F32),
        ),
        in_specs=[vm] * 4,
        out_specs=(pl.BlockSpec(memory_space=pltpu.HBM), vm),
        scratch_shapes=[pltpu.SemaphoreType.DMA],
        compiler_params=pltpu.CompilerParams(vmem_limit_bytes=8 * 1024 * 1024),
        name="fish_sample",
    )(v, ta, wy_hot, wx_hot)
    return out_v, out_m.reshape(2, 1, 1, 2048)


def solution(mesh):
    placed = (
        P(None, None, "gx", "gy"),
        P(None, "gx", "gy", None),
        P(None, "gx", "gy", None),
        P(None, "gx", "gy", None),
        P(),
    )
    return jax.shard_map(
        body,
        mesh=mesh,
        in_specs=placed,
        out_specs=(P(None, None, "gx", "gy"), P(None, "gx", "gy", None)),
        check_vma=False,
    )
```
